32 devices in a mesh: lon: 8 (over y, x, core), lat: 4 (over z).
Axes of the slice: x: 2, y: 2, z: 4, core: 2. Of those that a mesh axis runs over, the one named last changes fastest.
Arguments:
- thermal_anomaly: float32 [12, 128, 3072], P(None, 'lat', 'lon'), may hold values from -6 to 6
- saltiness_anomaly: float32 [12, 128, 3072], P(None, 'lat', 'lon'), may hold values from -6 to 6
- zonal_current: float32 [12, 128, 3072], P(None, 'lat', 'lon'), may hold values from -1.8 to 1.8
- meridional_current: float32 [12, 128, 3072], P(None, 'lat', 'lon'), may hold values from -1.8 to 1.8
- free_elevation: float32 [128, 3072], P('lat', 'lon'), may hold values from -1.8 to 1.8
- zonal_traction: float32 [128, 3072], P('lat', 'lon'), may hold values from -6 to 6
- meridional_traction: float32 [128, 3072], P('lat', 'lon'), may hold values from -6 to 6
- water_indicator: int32 [128, 3072], P('lat', 'lon'), may hold values 0 or 1
- bottom_layer_index: int32 [128, 3072], P('lat', 'lon'), may hold values from 1 to 12
Outputs:
- temperature_next: float32 [12, 128, 3072], P(None, 'lat', 'lon')
- salinity_next: float32 [12, 128, 3072], P(None, 'lat', 'lon')
- u_next: float32 [12, 128, 3072], P(None, 'lat', 'lon')
- v_next: float32 [12, 128, 3072], P(None, 'lat', 'lon')
- height_next: float32 [128, 3072], P('lat', 'lon')
- transport_x: float32 [128, 3072], P('lat', 'lon')
- transport_y: float32 [128, 3072], P('lat', 'lon')
The draws below stay inside these ranges and needn't reach their ends.
All inputs are finite; a program needn't handle non-finite values. No bound on the sum of `water_indicator` on one device may be relied on, other than what follows from the above.
Results may differ from the reference program's by a relative error of at most 0.00002.
Values sent between devices are 32-bit elements; how exact they have to be, the bound alone decides.
A program may use at most 64 MiB of HBM per device.

```python
import jax
import jax.numpy as jnp

VERTICAL_LAYERS = 12
NSUB = 4
MERIDIAN_CELLS = 128
PARALLEL_CELLS = 3072


def set_ends(drawn, own_key, smallest, top_value):
    place = [jax.random.randint(jax.random.fold_in(own_key, axis), (), 0, length) for axis, length in enumerate(drawn.shape)]
    longest = drawn.shape.index(max(drawn.shape))
    beside = place[:longest] + [(place[longest] + 1) % drawn.shape[longest]] + place[longest + 1:]
    return drawn.at[tuple(place)].set(smallest).at[tuple(beside)].set(top_value)


def steps_of(rng, dims, shards, least, largest):
    gain = 1.0
    for axis_at, parts in shards:
        steps = jax.random.uniform(jax.random.fold_in(jax.random.fold_in(rng, 6), axis_at), (parts,), jnp.float32, least / len(shards), largest / len(shards))
        gain = gain * jnp.repeat(jnp.exp(steps), dims[axis_at] // parts).reshape((-1,) + (1,) * (len(dims) - 1 - axis_at))
    return gain


def bell_draw(stream_key, shape, scale, most, shards=(), kind=jnp.bfloat16):
    drawn = jax.random.normal(stream_key, shape, jnp.float32) * scale
    if len(shards) > 0:
        drawn = steps_of(stream_key, shape, shards, -0.22, 0.18) * drawn
    return jnp.clip(drawn, min=-most, max=most).astype(kind)


def setup_inputs(seed: int = 0) -> dict:
    splits = jax.random.split(jax.random.key(seed), 10)
    return {
        "thermal_anomaly": bell_draw(splits[0], (VERTICAL_LAYERS, MERIDIAN_CELLS, PARALLEL_CELLS), 1.0, 6.0, ((1, 4), (2, 8)), jnp.float32),
        "saltiness_anomaly": bell_draw(splits[1], (VERTICAL_LAYERS, MERIDIAN_CELLS, PARALLEL_CELLS), 1.0, 6.0, ((1, 4), (2, 8)), jnp.float32),
        "zonal_current": bell_draw(splits[2], (VERTICAL_LAYERS, MERIDIAN_CELLS, PARALLEL_CELLS), 0.3, 1.8, ((1, 4), (2, 8)), jnp.float32),
        "meridional_current": bell_draw(splits[3], (VERTICAL_LAYERS, MERIDIAN_CELLS, PARALLEL_CELLS), 0.3, 1.8, ((1, 4), (2, 8)), jnp.float32),
        "free_elevation": bell_draw(splits[4], (MERIDIAN_CELLS, PARALLEL_CELLS), 0.3, 1.8, ((0, 4), (1, 8)), jnp.float32),
        "zonal_traction": bell_draw(splits[5], (MERIDIAN_CELLS, PARALLEL_CELLS), 1.0, 6.0, ((0, 4), (1, 8)), jnp.float32),
        "meridional_traction": bell_draw(splits[6], (MERIDIAN_CELLS, PARALLEL_CELLS), 1.0, 6.0, ((0, 4), (1, 8)), jnp.float32),
        "water_indicator": set_ends((jax.random.randint(splits[7], (MERIDIAN_CELLS, PARALLEL_CELLS), 0, 5) < 4).astype(jnp.int32), jax.random.fold_in(splits[7], 1), 0, 1),
        "bottom_layer_index": set_ends(jax.random.randint(splits[8], (MERIDIAN_CELLS, PARALLEL_CELLS), 1, VERTICAL_LAYERS + 1), jax.random.fold_in(splits[8], 1), 1, VERTICAL_LAYERS).astype(jnp.int32),
    }


TIME_STEP = 0.4
TRACER_DIFF = 0.05
MOMENTUM_DIFF = 0.05
BOTTOM_DRAG = 0.05
WIND_FACTOR = 0.5
CORIOLIS_SCALE = 0.5
LATITUDE_SPAN = 2.6
GRAVITY_FACTOR = 0.3
THERMAL_COEF = 0.2
HALINE_COEF = 0.8
BACKGROUND_MIX = 0.05
CONVECTIVE_MIX = 1.5
STABILITY_FACTOR = 5.0
HEIGHT_FACTOR = 0.2
SLOPE_FACTOR = 0.15


def offset_view(field, margin, shift_lat, shift_lon, meridional_cell_count, zonal_cell_count):
    return field[..., margin + shift_lat:margin + shift_lat + meridional_cell_count, margin + shift_lon:margin + shift_lon + zonal_cell_count]


def column_solve(couplings, first, second, layered_profile):
    zero_plane = jnp.zeros_like(first[0])
    ratios = []
    parts_first = []
    parts_second = []
    for layer in range(layered_profile):
        lower = couplings[layer - 1] if layer > 0 else zero_plane
        upper = couplings[layer] if layer < layered_profile - 1 else zero_plane
        denom = 1.0 + lower + upper
        rhs_first = first[layer]
        rhs_second = second[layer]
        if layer > 0:
            denom = denom - lower * ratios[-1]
            rhs_first = rhs_first + lower * parts_first[-1]
            rhs_second = rhs_second + lower * parts_second[-1]
        ratios.append(upper / denom)
        parts_first.append(rhs_first / denom)
        parts_second.append(rhs_second / denom)
    out_first = list(parts_first)
    out_second = list(parts_second)
    for layer in reversed(range(layered_profile - 1)):
        out_first[layer] = parts_first[layer] + ratios[layer] * out_first[layer + 1]
        out_second[layer] = parts_second[layer] + ratios[layer] * out_second[layer + 1]
    return jnp.stack(out_first), jnp.stack(out_second)


def advance_stratified_flow(tem, sal, uvel, vvel, vertical_layer_count, tracer_pad, flow_pad, lat_first, meridional_cell_count, zonal_cell_count, zonal_traction, meridional_traction, lat_total):
    layered_profile = tem.shape[0]
    level_index = jnp.arange(layered_profile, dtype=jnp.float32)[:, None, None]

    def wet_at(shift_lat, shift_lon):
        return jnp.clip(offset_view(vertical_layer_count, tracer_pad, shift_lat, shift_lon, meridional_cell_count, zonal_cell_count)[None] - level_index, 0.0, 1.0)

    def tracer_at(field, shift_lat, shift_lon):
        return offset_view(field, tracer_pad, shift_lat, shift_lon, meridional_cell_count, zonal_cell_count) * wet_at(shift_lat, shift_lon)

    def east_flow(shift_lat, shift_lon):
        return offset_view(uvel, flow_pad, shift_lat, shift_lon, meridional_cell_count, zonal_cell_count) * wet_at(shift_lat, shift_lon) * wet_at(shift_lat, shift_lon + 1)

    def north_flow(shift_lat, shift_lon):
        return offset_view(vvel, flow_pad, shift_lat, shift_lon, meridional_cell_count, zonal_cell_count) * wet_at(shift_lat, shift_lon) * wet_at(shift_lat + 1, shift_lon)

    def east_flux(field, shift_lon):
        far_west = tracer_at(field, 0, shift_lon - 1)
        near_west = tracer_at(field, 0, shift_lon)
        near_east = tracer_at(field, 0, shift_lon + 1)
        far_east = tracer_at(field, 0, shift_lon + 2)
        speed = east_flow(0, shift_lon)
        centred = speed * (7.0 * (near_west + near_east) - (far_west + far_east)) / 12.0
        upwind = jnp.abs(speed) * (3.0 * (near_west - near_east) - (far_west - far_east)) / 12.0
        mixing = TRACER_DIFF * (near_east - near_west) * wet_at(0, shift_lon) * wet_at(0, shift_lon + 1)
        return centred - upwind - mixing

    def north_flux(field, shift_lat):
        far_south = tracer_at(field, shift_lat - 1, 0)
        near_south = tracer_at(field, shift_lat, 0)
        near_north = tracer_at(field, shift_lat + 1, 0)
        far_north = tracer_at(field, shift_lat + 2, 0)
        speed = north_flow(shift_lat, 0)
        centred = speed * (7.0 * (near_south + near_north) - (far_south + far_north)) / 12.0
        upwind = jnp.abs(speed) * (3.0 * (near_south - near_north) - (far_south - far_north)) / 12.0
        mixing = TRACER_DIFF * (near_north - near_south) * wet_at(shift_lat, 0) * wet_at(shift_lat + 1, 0)
        return centred - upwind - mixing

    def advect(field):
        return tracer_at(field, 0, 0) - TIME_STEP * (east_flux(field, 0) - east_flux(field, -1) + north_flux(field, 0) - north_flux(field, -1))

    tem_star = advect(tem)
    sal_star = advect(sal)
    wet_here = wet_at(0, 0)
    dens_star = HALINE_COEF * sal_star - THERMAL_COEF * tem_star
    couplings = []
    for layer in range(layered_profile - 1):
        rise = jnp.maximum(dens_star[layer + 1] - dens_star[layer], 0.0)
        couplings.append(TIME_STEP * (BACKGROUND_MIX + CONVECTIVE_MIX / (1.0 + STABILITY_FACTOR * rise)) * wet_here[layer + 1])
    tem_new, sal_new = column_solve(couplings, tem_star, sal_star, layered_profile)

    def pressure_at(shift_lat, shift_lon):
        dens = HALINE_COEF * tracer_at(sal, shift_lat, shift_lon) - THERMAL_COEF * tracer_at(tem, shift_lat, shift_lon)
        return GRAVITY_FACTOR * (jnp.cumsum(dens, axis=0) - 0.5 * dens)

    press = pressure_at(0, 0)
    grad_x = pressure_at(0, 1) - press
    grad_y = pressure_at(1, 0) - press
    rows_global = lat_first + jnp.arange(meridional_cell_count, dtype=jnp.float32)
    coriolis_u = (CORIOLIS_SCALE * jnp.sin(LATITUDE_SPAN * ((rows_global + 0.5) / lat_total - 0.5)))[:, None]
    coriolis_v = (CORIOLIS_SCALE * jnp.sin(LATITUDE_SPAN * ((rows_global + 1.0) / lat_total - 0.5)))[:, None]
    u_here = east_flow(0, 0)
    v_here = north_flow(0, 0)
    v_at_u = 0.25 * (north_flow(0, 0) + north_flow(0, 1) + north_flow(-1, 0) + north_flow(-1, 1))
    u_at_v = 0.25 * (east_flow(0, 0) + east_flow(0, -1) + east_flow(1, 0) + east_flow(1, -1))
    lap_u = east_flow(0, 1) + east_flow(0, -1) + east_flow(1, 0) + east_flow(-1, 0) - 4.0 * u_here
    lap_v = north_flow(0, 1) + north_flow(0, -1) + north_flow(1, 0) + north_flow(-1, 0) - 4.0 * v_here
    open_u = wet_here * wet_at(0, 1)
    open_v = wet_here * wet_at(1, 0)
    surface = (jnp.arange(layered_profile) == 0).astype(jnp.float32)[:, None, None]
    u_trial = open_u * (u_here + TIME_STEP * (coriolis_u * v_at_u - grad_x + MOMENTUM_DIFF * lap_u - BOTTOM_DRAG * u_here) + TIME_STEP * WIND_FACTOR * surface * zonal_traction)
    v_trial = open_v * (v_here + TIME_STEP * (-coriolis_v * u_at_v - grad_y + MOMENTUM_DIFF * lap_v - BOTTOM_DRAG * v_here) + TIME_STEP * WIND_FACTOR * surface * meridional_traction)
    return (tem_new, sal_new, u_trial, v_trial, open_u, open_v,
            jnp.sum(u_trial - u_here, axis=0), jnp.sum(v_trial - v_here, axis=0),
            jnp.sum(u_here, axis=0), jnp.sum(v_here, axis=0),
            jnp.sum(open_u, axis=0), jnp.sum(open_v, axis=0))


def finish(trial, opening, face_depth, transport):
    return opening * (trial + (transport - jnp.sum(trial, axis=0)) / jnp.maximum(face_depth, 1.0))


def extend_border_cells(field, width):
    beside_all = jnp.concatenate([field[..., -width:], field, field[..., :width]], axis=-1)
    pads = [(0, 0)] * (field.ndim - 2) + [(width, width), (0, 0)]
    return jnp.pad(beside_all, pads)


def neighbour(field, shift_lat, shift_lon):
    rolled = jnp.roll(field, -shift_lon, axis=-1)
    padded = jnp.pad(rolled, ((1, 1), (0, 0)))
    return padded[1 + shift_lat:1 + shift_lat + field.shape[0]]


def reference(thermal_anomaly, saltiness_anomaly, zonal_current, meridional_current, free_elevation, zonal_traction, meridional_traction, water_indicator, bottom_layer_index):
    vertical_layer_count = (water_indicator * bottom_layer_index).astype(jnp.float32)
    advanced_state = advance_stratified_flow(extend_border_cells(thermal_anomaly, 2), extend_border_cells(saltiness_anomaly, 2), extend_border_cells(zonal_current, 2), extend_border_cells(meridional_current, 2),
                         extend_border_cells(vertical_layer_count, 2), 2, 2, jnp.float32(0.0), MERIDIAN_CELLS, PARALLEL_CELLS, zonal_traction, meridional_traction, MERIDIAN_CELLS)
    tem_new, sal_new, u_trial, v_trial, open_u, open_v, force_u, force_v, big_u, big_v, depth_u, depth_v = advanced_state
    mouth_u = jnp.minimum(depth_u, 1.0)
    mouth_v = jnp.minimum(depth_v, 1.0)
    height = free_elevation
    for substep in range(NSUB):
        height = height - HEIGHT_FACTOR * (big_u - neighbour(big_u, 0, -1) + big_v - neighbour(big_v, -1, 0))
        big_u = mouth_u * (big_u + force_u / NSUB - SLOPE_FACTOR * depth_u * (neighbour(height, 0, 1) - height))
        big_v = mouth_v * (big_v + force_v / NSUB - SLOPE_FACTOR * depth_v * (neighbour(height, 1, 0) - height))
    u_next = finish(u_trial, open_u, depth_u, big_u)
    v_next = finish(v_trial, open_v, depth_v, big_v)
    return tem_new, sal_new, u_next, v_next, height, big_u, big_v
```

```python
import functools

import jax
import jax.numpy as jnp
from jax import lax
from jax.experimental import pallas as pl
from jax.experimental.pallas import tpu as pltpu
from jax.sharding import PartitionSpec as P

NSUB = 4
TIME_STEP = 0.4
TRACER_DIFF = 0.05
MOMENTUM_DIFF = 0.05
BOTTOM_DRAG = 0.05
WIND_FACTOR = 0.5
CORIOLIS_SCALE = 0.5
LATITUDE_SPAN = 2.6
GRAVITY_FACTOR = 0.3
THERMAL_COEF = 0.2
HALINE_COEF = 0.8
BACKGROUND_MIX = 0.05
CONVECTIVE_MIX = 1.5
STABILITY_FACTOR = 5.0
HEIGHT_FACTOR = 0.2
SLOPE_FACTOR = 0.15

LANES = 128
SUB = 8
FLAT = 6
MESH = pl.DeviceIdType.MESH
F32 = jnp.float32


def lane_of(shape):
    return lax.broadcasted_iota(jnp.int32, shape, len(shape) - 1)


def east(x, lane, s=1):
    r = pltpu.roll(x, LANES - s, 2)
    return jnp.where(lane < LANES - s, r[:-1], r[1:])


def west(x, lane):
    r = pltpu.roll(x, 1, 2)
    return jnp.where(lane >= 1, r[:-1], jnp.concatenate([r[-1:], r[:-2]], axis=0))


def east_all(x, lane, s=1):
    r = pltpu.roll(x, LANES - s, 2)
    return jnp.where(lane < LANES - s, r, jnp.concatenate([r[1:], r[:1]], axis=0))


def west_all(x, lane):
    r = pltpu.roll(x, 1, 2)
    return jnp.where(lane >= 1, r, jnp.concatenate([r[-1:], r[:-1]], axis=0))


def step_loop(first, last, unroll, body, carry):
    n = (last - first) // unroll

    def group(g, c):
        for i in range(unroll):
            c = body(first + g * unroll + i, c)
        return c

    carry = lax.fori_loop(0, n, group, carry)
    for k in range(first + n * unroll, last):
        carry = body(jnp.int32(k), carry)
    return carry


def face_weights(speed, opening):
    p = speed * (TIME_STEP / 12.0)
    q = jnp.abs(p)
    m = 3.0 * q - jnp.where(opening, TIME_STEP * TRACER_DIFF, 0.0)
    p7 = 7.0 * p
    return p7 - m, p7 + m, p + q, q - p


def kernel(
    lat_total,
    t_in, s_in, u_in, v_in, eta_in, zt_in, mt_in, wi_in, bi_in,
    t_out, s_out, u_out, v_out, flat_out,
    tr, sr, ur, vr, tm, sm, um, vm, pm, xt, xs, yt, ys, ratio,
    zt, mt, wi, bi, de, hue, hve, flat, fu_ref, fv_ref,
    strip1, fe1, fw1, strip2, fe2, fw2,
    load_sem, send1, recv1, send2, recv2,
):
    levels, nt, rows, _ = t_out.shape
    end = SUB + rows
    nr = rows // SUB
    lon, lat = lax.axis_index("lon"), lax.axis_index("lat")
    nlon, nlat = lax.axis_size("lon"), lax.axis_size("lat")
    wst, est = lax.rem(lon + nlon - 1, nlon), lax.rem(lon + 1, nlon)
    nth, sth = lax.rem(lat + 1, nlat), lax.rem(lat + nlat - 1, nlat)
    has_n, has_s = lat < nlat - 1, lat > 0
    own = pl.ds(SUB, rows)

    loads = []

    def load(src, dst):
        group = []
        for c in range(nt):
            cols = pl.ds(c * LANES, LANES)
            group.append(pltpu.make_async_copy(
                src(cols), dst(c), load_sem.at[len(loads) * nt + c]))
            group[-1].start()
        loads.append(group)
        return group

    ld_wi = load(lambda s: wi_in.at[:, s], lambda c: wi.at[c])
    ld_bi = load(lambda s: bi_in.at[:, s], lambda c: bi.at[c])
    ld_t = load(lambda s: t_in.at[:, :, s], lambda c: tr.at[:, c])
    ld_s = load(lambda s: s_in.at[:, :, s], lambda c: sr.at[:, c])
    ld_u = load(lambda s: u_in.at[:, :, s], lambda c: ur.at[:, c, own, :])
    ld_v = load(lambda s: v_in.at[:, :, s], lambda c: vr.at[:, c, own, :])
    ld_e = load(lambda s: eta_in.at[:, s], lambda c: flat.at[0, c, own, :])
    ld_z = load(lambda s: zt_in.at[:, s], lambda c: zt.at[c])
    ld_m = load(lambda s: mt_in.at[:, s], lambda c: mt.at[c])

    def arrived(*groups):
        for g in groups:
            for c in g:
                c.wait()

    de[:, 0:SUB, :] = jnp.zeros((nt + 1, SUB, LANES), F32)
    de[:, end:, :] = jnp.zeros((nt + 1, 2 * SUB, LANES), F32)
    for ref in (fe1, fw1):
        ref[:, 0:SUB, :] = jnp.zeros((2, SUB, LANES), F32)
        ref[:, end:, :] = jnp.zeros((2, SUB, LANES), F32)
    for ref in (fe2, fw2):
        ref[0:SUB, :] = jnp.zeros((SUB, LANES), F32)
        ref[end:, :] = jnp.zeros((SUB, LANES), F32)
    for f in range(FLAT):
        flat[f, :, 0:SUB, :] = jnp.zeros((nt, SUB, LANES), F32)
        flat[f, :, end:, :] = jnp.zeros((nt, SUB, LANES), F32)
    for ref in (tm, sm):
        for k in range(levels):
            ref[k, 0:nt, 0:SUB, :] = jnp.zeros((nt, SUB, LANES), F32)
            ref[k, 0:nt, end:, :] = jnp.zeros((nt, SUB, LANES), F32)

    barrier = pltpu.get_barrier_semaphore()

    def greet(lo, la):
        pl.semaphore_signal(barrier, inc=1, device_id=(lo, la), device_id_type=MESH)

    greet(wst, lat)
    greet(est, lat)

    @pl.when(has_n)
    def _():
        greet(wst, nth)
        greet(lon, nth)
        greet(est, nth)

    @pl.when(has_s)
    def _():
        greet(wst, sth)
        greet(lon, sth)
        greet(est, sth)

    def copier(send, recv):
        made = []

        def cp(src, dst, lo, la):
            n = len(made)
            made.append(pltpu.make_async_remote_copy(
                src_ref=src, dst_ref=dst, send_sem=send.at[n], recv_sem=recv.at[n],
                device_id=(lo, la), device_id_type=MESH))
            return made[-1]

        return cp

    def start_ns(up, down):
        @pl.when(has_n)
        def _():
            for c in up:
                c.start()

        @pl.when(has_s)
        def _():
            for c in down:
                c.start()

    def recv_ns(up, down):
        @pl.when(has_s)
        def _():
            for c in up:
                c.wait_recv()

        @pl.when(has_n)
        def _():
            for c in down:
                c.wait_recv()

    def sent_ns(up, down):
        @pl.when(has_n)
        def _():
            for c in up:
                c.wait_send()

        @pl.when(has_s)
        def _():
            for c in down:
                c.wait_send()

    cp = copier(send1, recv1)

    def rows_up(ref, n, at):
        return cp(at(ref, end - n, n), at(ref, SUB - n, n), lon, nth)

    def rows_down(ref, n, at):
        return cp(at(ref, SUB, n), at(ref, end, n), lon, sth)

    def cube_rows(ref, first, n):
        return ref.at[:, 0:nt, pl.ds(first, n), :]

    def plane_rows(ref, first, n):
        return ref.at[0:nt, pl.ds(first, n), :]

    depth_up, depth_down = [rows_up(de, 2, plane_rows)], [rows_down(de, 2, plane_rows)]
    flow_up = [rows_up(r, 1, cube_rows) for r in (ur, vr)]
    flow_down = [rows_down(r, 1, cube_rows) for r in (ur, vr)]
    tracer_up = [rows_up(r, 2, cube_rows) for r in (tm, sm)]
    tracer_down = [rows_down(r, 2, cube_rows) for r in (tm, sm)]

    def strips(cp, strip, fe, fw, at, n):
        along = [cp(at(strip, 0, rows), at(fe, SUB, rows), wst, lat),
                 cp(at(strip, 0, rows), at(fw, SUB, rows), est, lat)]
        up = [cp(at(strip, rows - n, n), at(fe, SUB - n, n), wst, nth),
              cp(at(strip, rows - n, n), at(fw, SUB - n, n), est, nth)]
        down = [cp(at(strip, 0, n), at(fe, end, n), wst, sth),
                cp(at(strip, 0, n), at(fw, end, n), est, sth)]
        return along, up, down

    along1, corner_up1, corner_down1 = strips(
        cp, strip1, fe1, fw1, lambda r, a, n: r.at[:, pl.ds(a, n), :], 2)

    lane = lane_of((SUB, LANES))
    tall = lane_of((rows, LANES))

    sub = lax.broadcasted_iota(jnp.int32, (SUB, LANES), 0)
    j = (lat * rows + sub + SUB * lax.rem(lane, nr)).astype(F32)
    j = j + jnp.where(lane < LANES // 2, 0.5, 1.0)
    f = CORIOLIS_SCALE * jnp.sin(LATITUDE_SPAN * (j / lat_total - 0.5)) * (0.25 * TIME_STEP)
    for r in range(nr):
        fu_ref[r] = jnp.broadcast_to(f[:, r:r + 1], (SUB, LANES))
        at = LANES // 2 - (LANES // 2) % nr + nr + r
        fv_ref[r] = jnp.broadcast_to(f[:, at:at + 1], (SUB, LANES))

    arrived(ld_wi, ld_bi)
    depth = (wi[...] * bi[...]).astype(F32)
    de[0:nt, own, :] = depth
    arrived(ld_t, ld_s, ld_u, ld_v)
    pl.semaphore_wait(barrier, 2 + 3 * has_n.astype(jnp.int32) + 3 * has_s.astype(jnp.int32))
    start_ns(depth_up, depth_down)
    start_ns(flow_up, flow_down)

    place = lax.shift_right_logical(tall, 2)

    def edge(first, last, p):
        return pltpu.roll(jnp.where(tall < LANES // 2, first, last), 4 * p + 2, 1)

    group_a = edge(depth[0], depth[nt - 1], 2 * levels)
    group_b = jnp.zeros((rows, LANES), F32)
    for k in range(levels):
        wet = de[0:nt, own, :] > k
        t = jnp.where(wet, tr[k], 0.0)
        s = jnp.where(wet, sr[k], 0.0)
        tm[k, 0:nt, own, :] = t
        sm[k, 0:nt, own, :] = s
        group_a = jnp.where(place == 2 * k, edge(t[0], t[nt - 1], 2 * k), group_a)
        group_a = jnp.where(place == 2 * k + 1, edge(s[0], s[nt - 1], 2 * k + 1), group_a)
        group_b = jnp.where(place == 2 * k, edge(ur[k, 0, own, :], ur[k, nt - 1, own, :], 2 * k), group_b)
        group_b = jnp.where(place == 2 * k + 1, edge(vr[k, 0, own, :], vr[k, nt - 1, own, :], 2 * k + 1), group_b)
    strip1[0] = group_a
    strip1[1] = group_b
    for c in along1:
        c.start()
    start_ns(corner_up1, corner_down1)
    start_ns(tracer_up, tracer_down)

    HALF = 0.5 * GRAVITY_FACTOR * TIME_STEP

    def pressure(t, s, total):
        h = (HALF * HALINE_COEF) * s - (HALF * THERMAL_COEF) * t
        p = total + h
        return p, p + h

    def own_pressure(k, total):
        p, total = pressure(tm[k, 0:nt, own, :], sm[k, 0:nt, own, :], total)
        pm[k, 0:nt, own, :] = p
        return total

    lax.fori_loop(0, levels, own_pressure, jnp.zeros((nt, rows, LANES), F32))
    arrived(ld_e, ld_z, ld_m)
    flat[5, :, own, :] = depth

    for c in along1:
        c.wait_recv()
    recv_ns(corner_up1, corner_down1)
    recv_ns(depth_up, depth_down)

    pair = (lane_of((end + SUB, LANES)) & 3) >= 2
    halo_a = jnp.where(pair, fe1[0], fw1[0])
    halo_b = jnp.where(pair, fe1[1], fw1[1])
    fe1[0] = halo_a
    fe1[1] = halo_b
    de[nt, 0:end + SUB, :] = pltpu.roll(halo_a, LANES - (8 * levels + 2), 1)
    for r in range(0, end + SUB, SUB):
        d = de[:, r:r + SUB, :]
        hue[:, r:r + SUB, :] = jnp.minimum(d, east_all(d, lane))
        hve[:, r:r + SUB, :] = jnp.minimum(d, de[:, r + 1:r + SUB + 1, :])

    def edges(k, total):
        kf = k.astype(F32)
        back = LANES - 2 - 8 * k
        a = fe1[0, own, :]
        t = pltpu.roll(a, back, 1)
        s = pltpu.roll(a, back - 4, 1)
        tm[k, nt, own, :] = t
        sm[k, nt, own, :] = s
        p, total = pressure(t, s, total)
        pm[k, nt, own, :] = p
        b = fe1[1]
        um[k, nt] = jnp.where(hue[nt] > kf, pltpu.roll(b, back, 1), 0.0)
        vm[k, nt] = jnp.where(hve[nt] > kf, pltpu.roll(b, back - 4, 1), 0.0)
        um[k, 0:nt, own, :] = jnp.where(hue[0:nt, own, :] > kf, ur[k, :, own, :], 0.0)
        vm[k, 0:nt, own, :] = jnp.where(hve[0:nt, own, :] > kf, vr[k, :, own, :], 0.0)
        return total

    total = jnp.zeros((rows, LANES), F32)
    for k in range(levels):
        total = edges(jnp.int32(k), total)

    @pl.loop(0, levels)
    def _(k):
        kf = k.astype(F32)
        for r in range(SUB, end, SUB):
            here = slice(r, r + SUB)
            w0, w1, w2, w3 = face_weights(um[k, :, here, :], hue[:, here, :] > kf)
            for ref, to in ((tm, xt), (sm, xs)):
                c = ref[k, :, here, :]
                fx = (w0 * c + w1 * east_all(c, lane)
                      - w2 * east_all(c, lane, 2) + w3 * west_all(c, lane))
                to[k, :, r - SUB:r, :] = c[:nt] - (fx[:nt] - west(fx, lane))

    recv_ns(flow_up, flow_down)
    recv_ns(tracer_up, tracer_down)

    def far_rows(k, total):
        kf = k.astype(F32)
        for a in (0, end):
            out = slice(a, a + SUB)
            um[k, 0:nt, out, :] = jnp.where(hue[0:nt, out, :] > kf, ur[k, :, out, :], 0.0)
            vm[k, 0:nt, out, :] = jnp.where(hve[0:nt, out, :] > kf, vr[k, :, out, :], 0.0)
        out = slice(end, end + SUB)
        p, total = pressure(tm[k, 0:nt, out, :], sm[k, 0:nt, out, :], total)
        pm[k, 0:nt, out, :] = p
        return total

    step_loop(0, levels, 2, far_rows, jnp.zeros((nt, SUB, LANES), F32))

    MIX = TIME_STEP * MOMENTUM_DIFF
    KEEP = 1.0 - TIME_STEP * BOTTOM_DRAG - 4.0 * MIX
    for r in range(nr):
        at = SUB + SUB * r
        here, above, below = slice(at, at + SUB), slice(at + 1, at + SUB + 1), slice(at - 1, at + SUB - 1)
        out = slice(SUB * r, SUB * r + SUB)

        def momentum(k, carry, wind=None):
            su, sv, tu, tv = carry
            kf = k.astype(F32)
            u4, un = um[k, :, here, :], um[k, :, above, :]
            v4, vs = vm[k, :, here, :], vm[k, :, below, :]
            u, v = u4[:nt], v4[:nt]
            around_u = east(u4, lane) + west(u4, lane) + un[:nt] + um[k, 0:nt, below, :]
            around_v = east(v4, lane) + west(v4, lane) + vs[:nt] + vm[k, 0:nt, above, :]
            a, b = v4 + vs, u4 + un
            vbar = a[:nt] + east(a, lane)
            ubar = b[:nt] + west(b, lane)
            p = pm[k, :, here, :]
            px = east(p, lane) - p[:nt]
            py = pm[k, 0:nt, above, :] - p[:nt]
            ut = KEEP * u + MIX * around_u + fu_ref[r] * vbar - px
            vt = KEEP * v + MIX * around_v - fv_ref[r] * ubar - py
            if wind is not None:
                ut = ut + wind * zt[:, out, :]
                vt = vt + wind * mt[:, out, :]
            ut = jnp.where(hue[0:nt, here, :] > kf, ut, 0.0)
            vt = jnp.where(hve[0:nt, here, :] > kf, vt, 0.0)
            u_out[k, :, out, :] = ut
            v_out[k, :, out, :] = vt
            return su + u, sv + v, tu + ut, tv + vt

        zero = jnp.zeros((nt, SUB, LANES), F32)
        carry = momentum(jnp.int32(0), (zero,) * 4, TIME_STEP * WIND_FACTOR)
        su, sv, tu, tv = step_loop(1, levels, 2, momentum, carry)
        flat[1, :, here, :] = su
        flat[2, :, here, :] = sv
        flat[3, :, here, :] = tu - su
        flat[4, :, here, :] = tv - sv

    spot = lax.shift_right_logical(tall, 3)
    group = jnp.zeros((rows, LANES), F32)
    for f in range(FLAT):
        x = jnp.where(tall < LANES // 2, flat[f, 0, own, :], flat[f, nt - 1, own, :])
        group = jnp.where(spot == f, pltpu.roll(x, 8 * f + 4, 1), group)
    strip2[...] = group
    cp = copier(send2, recv2)
    flat_up = [cp(cube_rows(flat, end - NSUB, NSUB), cube_rows(flat, SUB - NSUB, NSUB), lon, nth)]
    flat_down = [cp(cube_rows(flat, SUB, NSUB), cube_rows(flat, end, NSUB), lon, sth)]
    along2, corner_up2, corner_down2 = strips(
        cp, strip2, fe2, fw2, lambda r, a, n: r.at[pl.ds(a, n), :], NSUB)
    start_ns(flat_up, flat_down)
    for c in along2:
        c.start()
    start_ns(corner_up2, corner_down2)

    starts = list(range(SUB - 1, end - SUB, SUB)) + [end - SUB]

    @pl.loop(0, levels)
    def _(k):
        kf = k.astype(F32)
        for a in starts:
            here = slice(a, a + SUB)
            w0, w1, w2, w3 = face_weights(vm[k, 0:nt, here, :], hve[0:nt, here, :] > kf)
            for ref, to in ((tm, yt), (sm, ys)):
                to[k, :, here, :] = (
                    w0 * ref[k, 0:nt, here, :] + w1 * ref[k, 0:nt, a + 1:a + SUB + 1, :]
                    - w2 * ref[k, 0:nt, a + 2:a + SUB + 2, :] + w3 * ref[k, 0:nt, a - 1:a + SUB - 1, :])

    span = 2 * SUB if rows % (2 * SUB) == 0 else SUB
    DIFF = TIME_STEP * STABILITY_FACTOR * BACKGROUND_MIX
    BASE = TIME_STEP * (BACKGROUND_MIX + CONVECTIVE_MIX)
    for r in range(0, rows, span):
        out = slice(r, r + span)
        here, below = slice(SUB + r, SUB + r + span), slice(SUB + r - 1, SUB + r + span - 1)

        def star(k):
            t = xt[k, :, out, :] - (yt[k, :, here, :] - yt[k, :, below, :])
            s = xs[k, :, out, :] - (ys[k, :, here, :] - ys[k, :, below, :])
            return t, s, HALINE_COEF * s - THERMAL_COEF * t

        def forward(k, carry):
            t, s, dens, lower, qt, qs = carry
            tn, sn, densn = star(k)
            rise = jnp.maximum(densn - dens, 0.0)
            e = 1.0 + STABILITY_FACTOR * rise
            n = jnp.where(de[0:nt, here, :] > k.astype(F32), BASE + DIFF * rise, 0.0)
            w = 1.0 / (e * lower + n)
            rat = n * w
            ew = e * w
            gt, gs = t + qt, s + qs
            t_out[k - 1, :, out, :] = gt * ew
            s_out[k - 1, :, out, :] = gs * ew
            ratio[k - 1, :, out, :] = rat
            return tn, sn, densn, 1.0 + rat * lower, rat * gt, rat * gs

        zero = jnp.zeros((nt, span, LANES), F32)
        carry = star(0) + (zero + 1.0, zero, zero)
        t, s, _, lower, qt, qs = lax.fori_loop(1, levels, forward, carry)
        w = 1.0 / lower
        t, s = (t + qt) * w, (s + qs) * w
        t_out[levels - 1, :, out, :] = t
        s_out[levels - 1, :, out, :] = s

        def backward(i, carry):
            t, s = carry
            k = levels - 2 - i
            rat = ratio[k, :, out, :]
            t = t_out[k, :, out, :] + rat * t
            s = s_out[k, :, out, :] + rat * s
            t_out[k, :, out, :] = t
            s_out[k, :, out, :] = s
            return t, s

        lax.fori_loop(0, levels - 1, backward, (t, s))

    recv_ns(flat_up, flat_down)
    for c in along2:
        c.wait_recv()
    recv_ns(corner_up2, corner_down2)
    wide = slice(SUB - NSUB, end + NSUB)
    count = rows + 2 * NSUB
    halo = jnp.where((lane_of((count, LANES)) & 7) >= 4, fe2[wide, :], fw2[wide, :])
    for f in range(FLAT):
        flat_out[f, 0:nt, 0:count] = flat[f, :, wide, :]
        flat_out[f, nt, 0:count] = pltpu.roll(halo, LANES - 8 * f - 4, 1)
    flat_out[5, :, count:, :] = jnp.zeros((nt + 1, SUB, LANES), F32)

    for c in along1 + along2:
        c.wait_send()
    sent_ns(depth_up + flow_up + tracer_up + corner_up1 + flat_up + corner_up2,
            depth_down + flow_down + tracer_down + corner_down1 + flat_down + corner_down2)


def tail(
    t, s, ut, vt, flat,
    t_out, s_out, u_out, v_out, eta_out, tx_out, ty_out,
    eta, bu, bv, hx, hy, un, vn, cor, sem,
):
    levels, nt, rows, _ = t.shape
    count = rows + 2 * NSUB
    lane = lane_of((SUB, LANES))
    copies = []

    def put(src, dst):
        for c in range(nt):
            copies.append(pltpu.make_async_copy(
                src(c), dst(pl.ds(c * LANES, LANES)), sem.at[len(copies)]))
            copies[-1].start()

    put(lambda c: t.at[:, c], lambda d: t_out.at[:, :, d])
    put(lambda c: s.at[:, c], lambda d: s_out.at[:, :, d])

    for ref in (eta, bu, bv):
        ref[:, 0:SUB, :] = jnp.zeros((nt + 1, SUB, LANES), F32)
        ref[:, count + SUB:, :] = jnp.zeros((nt + 1, SUB, LANES), F32)
    tiles = range(0, count, SUB)
    eta[:, SUB:count + SUB, :] = flat[0, :, 0:count, :]
    bu[:, SUB:count + SUB, :] = flat[1, :, 0:count, :]
    bv[:, SUB:count + SUB, :] = flat[2, :, 0:count, :]
    for r in tiles:
        d = flat[5, :, r:r + SUB, :]
        hx[:, r:r + SUB, :] = jnp.minimum(d, east_all(d, lane))
        hy[:, r:r + SUB, :] = jnp.minimum(d, flat[5, :, r + 1:r + SUB + 1, :])
    for sub in range(NSUB):
        for r in tiles:
            here, below = slice(SUB + r, 2 * SUB + r), slice(SUB + r - 1, 2 * SUB + r - 1)
            x = bu[:, here, :]
            eta[:, here, :] = eta[:, here, :] - HEIGHT_FACTOR * (
                x - west_all(x, lane) + (bv[:, here, :] - bv[:, below, :]))
        for r in tiles:
            here, above = slice(SUB + r, 2 * SUB + r), slice(SUB + r + 1, 2 * SUB + r + 1)
            raw = slice(r, r + SUB)
            x = eta[:, here, :]
            bu[:, here, :] = (bu[:, here, :] + (1.0 / NSUB) * flat[3, :, raw, :]
                              - SLOPE_FACTOR * hx[:, raw, :] * (east_all(x, lane) - x))
            bv[:, here, :] = (bv[:, here, :] + (1.0 / NSUB) * flat[4, :, raw, :]
                              - SLOPE_FACTOR * hy[:, raw, :] * (eta[:, above, :] - x))
    mid = pl.ds(SUB + NSUB, rows)
    put(lambda c: eta.at[c, mid, :], lambda d: eta_out.at[:, d])
    put(lambda c: bu.at[c, mid, :], lambda d: tx_out.at[:, d])
    put(lambda c: bv.at[c, mid, :], lambda d: ty_out.at[:, d])

    for r in range(0, rows, SUB):
        raw = slice(NSUB + r, NSUB + r + SUB)
        hu, hv = hx[0:nt, raw, :], hy[0:nt, raw, :]
        done = slice(SUB + NSUB + r, 2 * SUB + NSUB + r)
        out = slice(r, r + SUB)
        cor[0, :, out, :] = (bu[0:nt, done, :] - (flat[3, 0:nt, raw, :] + flat[1, 0:nt, raw, :])) / jnp.maximum(hu, 1.0)
        cor[1, :, out, :] = (bv[0:nt, done, :] - (flat[4, 0:nt, raw, :] + flat[2, 0:nt, raw, :])) / jnp.maximum(hv, 1.0)
        cor[2, :, out, :] = hu
        cor[3, :, out, :] = hv

    @pl.loop(0, levels)
    def _(k):
        kf = k.astype(F32)
        un[k] = jnp.where(cor[2] > kf, ut[k] + cor[0], 0.0)
        vn[k] = jnp.where(cor[3] > kf, vt[k] + cor[1], 0.0)

    put(lambda c: un.at[:, c], lambda d: u_out.at[:, :, d])
    put(lambda c: vn.at[:, c], lambda d: v_out.at[:, :, d])
    for c in copies:
        c.wait()


def body(*args):
    levels, rows, cols = args[0].shape
    nt = cols // LANES
    erows = rows + 2 * SUB
    count = rows + 2 * NSUB

    def vmem(*shape):
        return pltpu.VMEM(shape, F32)

    def out(*shape):
        return jax.ShapeDtypeStruct(shape, F32)

    block = pl.BlockSpec(memory_space=pltpu.VMEM)
    far = pl.BlockSpec(memory_space=pltpu.HBM)
    raw = vmem(levels, nt, erows, LANES)
    own = vmem(levels, nt, rows, LANES)
    wide = vmem(levels, nt + 1, erows, LANES)
    ints = pltpu.VMEM((nt, rows, LANES), jnp.int32)
    n1, n2 = 2 + 4 + 4 + 6, 2 + 6
    cube = (levels, nt, rows, LANES)
    parts = pl.pallas_call(
        functools.partial(kernel, rows * lax.axis_size("lat")),
        out_shape=(out(*cube),) * 4 + (out(FLAT, nt + 1, count + SUB, LANES),),
        in_specs=[far] * 9,
        out_specs=(block,) * 5,
        scratch_shapes=(
            [own, own, raw, raw] + [wide] * 5 + [own, own, raw, raw, own]
            + [vmem(nt, rows, LANES)] * 2 + [ints] * 2
            + [vmem(nt + 1, erows + SUB, LANES)] + [vmem(nt + 1, erows, LANES)] * 2
            + [vmem(FLAT, nt, erows, LANES)]
            + [vmem(rows // SUB, SUB, LANES)] * 2
            + [vmem(2, rows, LANES), vmem(2, erows, LANES), vmem(2, erows, LANES)]
            + [vmem(rows, LANES), vmem(erows, LANES), vmem(erows, LANES)]
            + [pltpu.SemaphoreType.DMA((9 * nt,))]
            + [pltpu.SemaphoreType.DMA((n1,))] * 2
            + [pltpu.SemaphoreType.DMA((n2,))] * 2
        ),
        compiler_params=pltpu.CompilerParams(
            collective_id=0, has_side_effects=True, vmem_limit_bytes=32 * 1024 * 1024),
    )(*[pltpu.with_memory_space_constraint(a, pltpu.HBM) for a in args])
    cube, plane = (levels, rows, cols), (rows, cols)
    return pl.pallas_call(
        tail,
        out_shape=(pltpu.HBM(cube, F32),) * 4 + (pltpu.HBM(plane, F32),) * 3,
        in_specs=[block] * 5,
        out_specs=(far,) * 7,
        scratch_shapes=(
            [vmem(nt + 1, count + 2 * SUB, LANES)] * 3 + [vmem(nt + 1, count, LANES)] * 2
            + [own, own, vmem(4, nt, rows, LANES)]
            + [pltpu.SemaphoreType.DMA((7 * nt,))]
        ),
        compiler_params=pltpu.CompilerParams(vmem_limit_bytes=32 * 1024 * 1024),
    )(*parts)


def solution(mesh):
    cube, plane = P(None, "lat", "lon"), P("lat", "lon")
    return jax.shard_map(
        body,
        mesh=mesh,
        in_specs=(cube,) * 4 + (plane,) * 5,
        out_specs=(cube,) * 4 + (plane,) * 3,
        check_vma=False,
    )
```

```python
import functools

import jax
import jax.numpy as jnp
from jax import lax
from jax.experimental import pallas as pl
from jax.experimental.pallas import tpu as pltpu
from jax.sharding import PartitionSpec as P

NSUB = 4
TIME_STEP = 0.4
TRACER_DIFF = 0.05
MOMENTUM_DIFF = 0.05
BOTTOM_DRAG = 0.05
WIND_FACTOR = 0.5
CORIOLIS_SCALE = 0.5
LATITUDE_SPAN = 2.6
GRAVITY_FACTOR = 0.3
THERMAL_COEF = 0.2
HALINE_COEF = 0.8
BACKGROUND_MIX = 0.05
CONVECTIVE_MIX = 1.5
STABILITY_FACTOR = 5.0
HEIGHT_FACTOR = 0.2
SLOPE_FACTOR = 0.15

LANES = 128
SUB = 8
FLAT = 6
MESH = pl.DeviceIdType.MESH
F32 = jnp.float32


def lane_of(shape):
    return lax.broadcasted_iota(jnp.int32, shape, len(shape) - 1)


def east(x, lane, s=1):
    r = pltpu.roll(x, LANES - s, 2)
    return jnp.where(lane < LANES - s, r[:-1], r[1:])


def west(x, lane):
    r = pltpu.roll(x, 1, 2)
    return jnp.where(lane >= 1, r[:-1], jnp.concatenate([r[-1:], r[:-2]], axis=0))


def east_all(x, lane, s=1):
    r = pltpu.roll(x, LANES - s, 2)
    return jnp.where(lane < LANES - s, r, jnp.concatenate([r[1:], r[:1]], axis=0))


def west_all(x, lane):
    r = pltpu.roll(x, 1, 2)
    return jnp.where(lane >= 1, r, jnp.concatenate([r[-1:], r[:-1]], axis=0))


def step_loop(first, last, unroll, body, carry):
    n = (last - first) // unroll

    def group(g, c):
        for i in range(unroll):
            c = body(first + g * unroll + i, c)
        return c

    carry = lax.fori_loop(0, n, group, carry)
    for k in range(first + n * unroll, last):
        carry = body(jnp.int32(k), carry)
    return carry


def east_in(x, lane, s):
    r = pltpu.roll(x, LANES - s, 2)
    return jnp.where(lane < LANES - s, r, jnp.concatenate([r[1:], jnp.zeros_like(r[:1])], axis=0))


def west_in(x, lane):
    r = pltpu.roll(x, 1, 2)
    return jnp.where(lane >= 1, r, jnp.concatenate([jnp.zeros_like(r[:1]), r[:-1]], axis=0))


def face_weights(speed, opening):
    p = speed * (TIME_STEP / 12.0)
    q = jnp.abs(p)
    m = 3.0 * q - jnp.where(opening, TIME_STEP * TRACER_DIFF, 0.0)
    p7 = 7.0 * p
    return p7 - m, p7 + m, p + q, q - p


def kernel(
    lat_total,
    t_in, s_in, u_in, v_in, eta_in, zt_in, mt_in, wi_in, bi_in,
    t_out, s_out, u_out, v_out, flat_out,
    tr, sr, ur, vr, tm, sm, um, vm, pm, xt, xs, yt, ys, ratio,
    zt, mt, wi, bi, de, hue, hve, flat, fu_ref, fv_ref,
    strip0, fe0, fw0, strip1, fe1, fw1, strip2, fe2, fw2, mend,
    load_sem, send1, recv1, send2, recv2,
):
    levels, nt, rows, _ = t_out.shape
    end = SUB + rows
    nr = rows // SUB
    lon, lat = lax.axis_index("lon"), lax.axis_index("lat")
    nlon, nlat = lax.axis_size("lon"), lax.axis_size("lat")
    wst, est = lax.rem(lon + nlon - 1, nlon), lax.rem(lon + 1, nlon)
    nth, sth = lax.rem(lat + 1, nlat), lax.rem(lat + nlat - 1, nlat)
    has_n, has_s = lat < nlat - 1, lat > 0
    own = pl.ds(SUB, rows)

    barrier = pltpu.get_barrier_semaphore()

    def greet(lo, la):
        pl.semaphore_signal(barrier, inc=1, device_id=(lo, la), device_id_type=MESH)

    greet(wst, lat)
    greet(est, lat)

    @pl.when(has_n)
    def _():
        greet(wst, nth)
        greet(lon, nth)
        greet(est, nth)

    @pl.when(has_s)
    def _():
        greet(wst, sth)
        greet(lon, sth)
        greet(est, sth)

    loads = []

    def load(src, dst):
        group = []
        for c in range(nt):
            cols = pl.ds(c * LANES, LANES)
            group.append(pltpu.make_async_copy(
                src(cols), dst(c), load_sem.at[len(loads) * nt + c]))
            group[-1].start()
        loads.append(group)
        return group

    ld_wi = load(lambda s: wi_in.at[:, s], lambda c: wi.at[c])
    ld_bi = load(lambda s: bi_in.at[:, s], lambda c: bi.at[c])
    ld_t = load(lambda s: t_in.at[:, :, s], lambda c: tr.at[:, c, own, :])
    ld_s = load(lambda s: s_in.at[:, :, s], lambda c: sr.at[:, c, own, :])
    ld_u = load(lambda s: u_in.at[:, :, s], lambda c: ur.at[:, c, own, :])
    ld_v = load(lambda s: v_in.at[:, :, s], lambda c: vr.at[:, c, own, :])
    ld_e = load(lambda s: eta_in.at[:, s], lambda c: flat.at[0, c, own, :])
    ld_z = load(lambda s: zt_in.at[:, s], lambda c: zt.at[c])
    ld_m = load(lambda s: mt_in.at[:, s], lambda c: mt.at[c])

    def arrived(*groups):
        for g in groups:
            for c in g:
                c.wait()

    def clear(first):
        beyond = slice(first, first + SUB)
        de[:, beyond, :] = jnp.zeros((nt + 1, SUB, LANES), F32)
        for ref in (fe0, fw0, fe2, fw2):
            ref[beyond, :] = jnp.zeros((SUB, LANES), F32)
        for ref in (fe1, fw1):
            ref[:, beyond, :] = jnp.zeros((2, SUB, LANES), F32)
        for f in range(FLAT):
            flat[f, :, beyond, :] = jnp.zeros((nt, SUB, LANES), F32)

    @pl.when(jnp.logical_not(has_s))
    def _():
        clear(0)

    @pl.when(jnp.logical_not(has_n))
    def _():
        clear(end)

    def copier(send, recv):
        made = []

        def cp(src, dst, lo, la):
            n = len(made)
            made.append(pltpu.make_async_remote_copy(
                src_ref=src, dst_ref=dst, send_sem=send.at[n], recv_sem=recv.at[n],
                device_id=(lo, la), device_id_type=MESH))
            return made[-1]

        return cp

    def start_ns(up, down):
        @pl.when(has_n)
        def _():
            for c in up:
                c.start()

        @pl.when(has_s)
        def _():
            for c in down:
                c.start()

    def recv_ns(up, down):
        @pl.when(has_s)
        def _():
            for c in up:
                c.wait_recv()

        @pl.when(has_n)
        def _():
            for c in down:
                c.wait_recv()

    def sent_ns(up, down):
        @pl.when(has_n)
        def _():
            for c in up:
                c.wait_send()

        @pl.when(has_s)
        def _():
            for c in down:
                c.wait_send()

    cp = copier(send1, recv1)

    def rows_up(ref, n, at):
        return cp(at(ref, end - n, n), at(ref, SUB - n, n), lon, nth)

    def rows_down(ref, n, at):
        return cp(at(ref, SUB, n), at(ref, end, n), lon, sth)

    def cube_rows(ref, first, n):
        return ref.at[:, 0:nt, pl.ds(first, n), :]

    def plane_rows(ref, first, n):
        return ref.at[0:nt, pl.ds(first, n), :]

    depth_up, depth_down = [rows_up(de, 2, plane_rows)], [rows_down(de, 2, plane_rows)]
    field_up = [rows_up(r, n, cube_rows) for r, n in ((tr, 2), (sr, 2), (ur, 1), (vr, 1))]
    field_down = [rows_down(r, n, cube_rows) for r, n in ((tr, 2), (sr, 2), (ur, 1), (vr, 1))]

    def strips(cp, strip, fe, fw, at, n):
        along = [cp(at(strip, 0, rows), at(fe, SUB, rows), wst, lat),
                 cp(at(strip, 0, rows), at(fw, SUB, rows), est, lat)]
        up = [cp(at(strip, rows - n, n), at(fe, SUB - n, n), wst, nth),
              cp(at(strip, rows - n, n), at(fw, SUB - n, n), est, nth)]
        down = [cp(at(strip, 0, n), at(fe, end, n), wst, sth),
                cp(at(strip, 0, n), at(fw, end, n), est, sth)]
        return along, up, down

    along0, corner_up0, corner_down0 = strips(
        cp, strip0, fe0, fw0, lambda r, a, n: r.at[pl.ds(a, n), :], 2)
    along1, corner_up1, corner_down1 = strips(
        cp, strip1, fe1, fw1, lambda r, a, n: r.at[:, pl.ds(a, n), :], 2)

    lane = lane_of((SUB, LANES))
    tall = lane_of((rows, LANES))

    sub = lax.broadcasted_iota(jnp.int32, (SUB, LANES), 0)
    j = (lat * rows + sub + SUB * lax.rem(lane, nr)).astype(F32)
    j = j + jnp.where(lane < LANES // 2, 0.5, 1.0)
    f = CORIOLIS_SCALE * jnp.sin(LATITUDE_SPAN * (j / lat_total - 0.5)) * (0.25 * TIME_STEP)
    for r in range(nr):
        fu_ref[r] = jnp.broadcast_to(f[:, r:r + 1], (SUB, LANES))
        at = LANES // 2 - (LANES // 2) % nr + nr + r
        fv_ref[r] = jnp.broadcast_to(f[:, at:at + 1], (SUB, LANES))

    def edge(first, last, p):
        return pltpu.roll(jnp.where(tall < LANES // 2, first, last), 4 * p + 2, 1)

    arrived(ld_wi, ld_bi)
    depth = (wi[...] * bi[...]).astype(F32)
    de[0:nt, own, :] = depth
    strip0[...] = edge(depth[0], depth[nt - 1], 0)
    pl.semaphore_wait(barrier, 2 + 3 * has_n.astype(jnp.int32) + 3 * has_s.astype(jnp.int32))
    for c in along0:
        c.start()
    start_ns(depth_up + corner_up0, depth_down + corner_down0)
    for n, group in enumerate((ld_t, ld_s, ld_u, ld_v)):
        arrived(group)
        start_ns(field_up[n:n + 1], field_down[n:n + 1])

    HALF = 0.5 * GRAVITY_FACTOR * TIME_STEP

    def pressure(t, s, total):
        h = (HALF * HALINE_COEF) * s - (HALF * THERMAL_COEF) * t
        p = total + h
        return p, p + h

    place = lax.shift_right_logical(tall, 2)
    group_a = jnp.zeros((rows, LANES), F32)
    group_b = jnp.zeros((rows, LANES), F32)
    total = jnp.zeros((nt, rows, LANES), F32)
    for k in range(levels):
        wet = de[0:nt, own, :] > k
        t = jnp.where(wet, tr[k, :, own, :], 0.0)
        s = jnp.where(wet, sr[k, :, own, :], 0.0)
        tm[k, :, own, :] = t
        sm[k, :, own, :] = s
        p, total = pressure(t, s, total)
        pm[k, 0:nt, own, :] = p
        group_a = jnp.where(place == 2 * k, edge(t[0], t[nt - 1], 2 * k), group_a)
        group_a = jnp.where(place == 2 * k + 1, edge(s[0], s[nt - 1], 2 * k + 1), group_a)
        group_b = jnp.where(place == 2 * k, edge(ur[k, 0, own, :], ur[k, nt - 1, own, :], 2 * k), group_b)
        group_b = jnp.where(place == 2 * k + 1, edge(vr[k, 0, own, :], vr[k, nt - 1, own, :], 2 * k + 1), group_b)
        group_b = jnp.where(tall == 8 * k + 7, pltpu.roll(p[0], 8 * k + 7, 1), group_b)
    strip1[0] = group_a
    strip1[1] = group_b
    for c in along1:
        c.start()
    start_ns(corner_up1, corner_down1)
    arrived(ld_e, ld_z, ld_m)
    flat[5, :, own, :] = depth

    for c in along0:
        c.wait_recv()
    recv_ns(depth_up + corner_up0, depth_down + corner_down0)
    high = lane_of((end + SUB, LANES))
    pair = (high & 3) >= 2
    de[nt, 0:end + SUB, :] = pltpu.roll(jnp.where(pair, fe0[...], fw0[...]), LANES - 2, 1)
    for r in range(0, end + SUB, SUB):
        d = de[:, r:r + SUB, :]
        hue[:, r:r + SUB, :] = jnp.minimum(d, east_all(d, lane))
        hve[:, r:r + SUB, :] = jnp.minimum(d, de[:, r + 1:r + SUB + 1, :])

    @pl.loop(0, levels)
    def _(k):
        kf = k.astype(F32)
        for r in range(SUB, end, SUB):
            here = slice(r, r + SUB)
            opening = hue[0:nt, here, :] > kf
            u = jnp.where(opening, ur[k, :, here, :], 0.0)
            um[k, 0:nt, here, :] = u
            vm[k, 0:nt, here, :] = jnp.where(hve[0:nt, here, :] > kf, vr[k, :, here, :], 0.0)
            w0, w1, w2, w3 = face_weights(u, opening)
            for ref, to in ((tm, xt), (sm, xs)):
                c = ref[k, :, here, :]
                fx = (w0 * c + w1 * east_in(c, lane, 1)
                      - w2 * east_in(c, lane, 2) + w3 * west_in(c, lane))
                to[k, :, r - SUB:r, :] = c - (fx - west_in(fx, lane))

    for c in along1:
        c.wait_recv()
    recv_ns(corner_up1, corner_down1)
    halo_b = jnp.where(pair, fe1[1], fw1[1])
    for k in range(levels):
        back = LANES - 2 - 8 * k
        um[k, nt] = jnp.where(hue[nt] > k, pltpu.roll(halo_b, back, 1), 0.0)
        vm[k, nt] = jnp.where(hve[nt] > k, pltpu.roll(halo_b, back - 4, 1), 0.0)
        pm[k, nt, own, :] = pltpu.roll(halo_b[SUB:end], back - 5, 1)

    q = tall & 3
    level = lax.shift_right_logical(tall, 3).astype(F32)

    def column(c, at):
        return jnp.broadcast_to(hue[c, own, at:at + 1], (rows, LANES))

    def speeds(x, limit):
        x = jnp.where((tall & 7) < 4, x, pltpu.roll(x, 4, 1))
        opening = limit > level
        return face_weights(jnp.where(opening, x, 0.0), opening)

    mine = strip1[0]
    a = jnp.where(q < 2, mine, fe1[0, own, :])
    b = jnp.where(q < 2, fw1[0, own, :], mine)
    _, w1, w2, w3 = speeds(strip1[1], jnp.where(
        q == 0, column(nt - 1, LANES - 2), jnp.where(q == 1, column(nt - 1, LANES - 1), column(0, 0))))
    b_west = pltpu.roll(b, 1, 1)
    flux = jnp.where(q == 1, w1 * pltpu.roll(a, LANES - 1, 1), 0.0) - w2 * pltpu.roll(a, LANES - 2, 1)
    flux = jnp.where(q < 2, flux, jnp.where(q == 2, w3 * b_west, 0.0))
    w0, w1, w2, w3 = speeds(fw1[1, own, :], column(nt, LANES - 1))
    first = w0 * b + w1 * pltpu.roll(b, LANES - 1, 1) - w2 * pltpu.roll(b, LANES - 2, 1) + w3 * b_west
    mend[...] = flux - pltpu.roll(jnp.where(q == 1, first, flux), 1, 1)

    recv_ns(field_up, field_down)

    def far_rows(k, total):
        kf = k.astype(F32)
        for a in (0, end):
            out = slice(a, a + SUB)
            um[k, 0:nt, out, :] = jnp.where(hue[0:nt, out, :] > kf, ur[k, :, out, :], 0.0)
            vm[k, 0:nt, out, :] = jnp.where(hve[0:nt, out, :] > kf, vr[k, :, out, :], 0.0)
            wet = de[0:nt, out, :] > kf
            tm[k, :, out, :] = jnp.where(wet, tr[k, :, out, :], 0.0)
            sm[k, :, out, :] = jnp.where(wet, sr[k, :, out, :], 0.0)
        out = slice(end, end + SUB)
        p, total = pressure(tm[k, :, out, :], sm[k, :, out, :], total)
        pm[k, 0:nt, out, :] = p
        return total

    step_loop(0, levels, 2, far_rows, jnp.zeros((nt, SUB, LANES), F32))

    MIX = TIME_STEP * MOMENTUM_DIFF
    KEEP = 1.0 - TIME_STEP * BOTTOM_DRAG - 4.0 * MIX
    for r in range(nr):
        at = SUB + SUB * r
        here, above, below = slice(at, at + SUB), slice(at + 1, at + SUB + 1), slice(at - 1, at + SUB - 1)
        out = slice(SUB * r, SUB * r + SUB)

        def momentum(k, carry, wind=None):
            su, sv, tu, tv = carry
            kf = k.astype(F32)
            u4, un = um[k, :, here, :], um[k, :, above, :]
            v4, vs = vm[k, :, here, :], vm[k, :, below, :]
            u, v = u4[:nt], v4[:nt]
            around_u = east(u4, lane) + west(u4, lane) + un[:nt] + um[k, 0:nt, below, :]
            around_v = east(v4, lane) + west(v4, lane) + vs[:nt] + vm[k, 0:nt, above, :]
            a, b = v4 + vs, u4 + un
            vbar = a[:nt] + east(a, lane)
            ubar = b[:nt] + west(b, lane)
            p = pm[k, :, here, :]
            px = east(p, lane) - p[:nt]
            py = pm[k, 0:nt, above, :] - p[:nt]
            ut = KEEP * u + MIX * around_u + fu_ref[r] * vbar - px
            vt = KEEP * v + MIX * around_v - fv_ref[r] * ubar - py
            if wind is not None:
                ut = ut + wind * zt[:, out, :]
                vt = vt + wind * mt[:, out, :]
            ut = jnp.where(hue[0:nt, here, :] > kf, ut, 0.0)
            vt = jnp.where(hve[0:nt, here, :] > kf, vt, 0.0)
            u_out[k, :, out, :] = ut
            v_out[k, :, out, :] = vt
            return su + u, sv + v, tu + ut, tv + vt

        zero = jnp.zeros((nt, SUB, LANES), F32)
        carry = momentum(jnp.int32(0), (zero,) * 4, TIME_STEP * WIND_FACTOR)
        su, sv, tu, tv = step_loop(1, levels, 2, momentum, carry)
        flat[1, :, here, :] = su
        flat[2, :, here, :] = sv
        flat[3, :, here, :] = tu - su
        flat[4, :, here, :] = tv - sv

    spot = lax.shift_right_logical(tall, 3)
    group = jnp.zeros((rows, LANES), F32)
    for f in range(FLAT):
        x = jnp.where(tall < LANES // 2, flat[f, 0, own, :], flat[f, nt - 1, own, :])
        group = jnp.where(spot == f, pltpu.roll(x, 8 * f + 4, 1), group)
    strip2[...] = group
    cp = copier(send2, recv2)
    flat_up = [cp(cube_rows(flat, end - NSUB, NSUB), cube_rows(flat, SUB - NSUB, NSUB), lon, nth)]
    flat_down = [cp(cube_rows(flat, SUB, NSUB), cube_rows(flat, end, NSUB), lon, sth)]
    along2, corner_up2, corner_down2 = strips(
        cp, strip2, fe2, fw2, lambda r, a, n: r.at[pl.ds(a, n), :], NSUB)
    start_ns(flat_up, flat_down)
    for c in along2:
        c.start()
    start_ns(corner_up2, corner_down2)

    starts = list(range(SUB - 1, end - SUB, SUB)) + [end - SUB]

    @pl.loop(0, levels)
    def _(k):
        kf = k.astype(F32)
        for a in starts:
            here = slice(a, a + SUB)
            w0, w1, w2, w3 = face_weights(vm[k, 0:nt, here, :], hve[0:nt, here, :] > kf)
            for ref, to in ((tm, yt), (sm, ys)):
                to[k, :, here, :] = (
                    w0 * ref[k, :, here, :] + w1 * ref[k, :, a + 1:a + SUB + 1, :]
                    - w2 * ref[k, :, a + 2:a + SUB + 2, :] + w3 * ref[k, :, a - 1:a + SUB - 1, :])

    def mended(x, m):
        edge_lane = lane_of(m.shape)
        first = x[:1] - jnp.where(edge_lane < 2, m, 0.0)[None]
        last = x[-1:] - jnp.where(edge_lane >= LANES - 2, m, 0.0)[None]
        return jnp.concatenate([first, x[1:-1], last], axis=0)

    span = 2 * SUB if rows % (2 * SUB) == 0 else SUB
    DIFF = TIME_STEP * STABILITY_FACTOR * BACKGROUND_MIX
    BASE = TIME_STEP * (BACKGROUND_MIX + CONVECTIVE_MIX)
    for r in range(0, rows, span):
        out = slice(r, r + span)
        here, below = slice(SUB + r, SUB + r + span), slice(SUB + r - 1, SUB + r + span - 1)

        def star(k):
            t = xt[k, :, out, :] - (yt[k, :, here, :] - yt[k, :, below, :])
            s = xs[k, :, out, :] - (ys[k, :, here, :] - ys[k, :, below, :])
            t = mended(t, pltpu.roll(mend[out, :], LANES - 2 - 8 * k, 1))
            s = mended(s, pltpu.roll(mend[out, :], LANES - 6 - 8 * k, 1))
            return t, s, HALINE_COEF * s - THERMAL_COEF * t

        def forward(k, carry):
            t, s, dens, lower, qt, qs = carry
            tn, sn, densn = star(k)
            rise = jnp.maximum(densn - dens, 0.0)
            e = 1.0 + STABILITY_FACTOR * rise
            n = jnp.where(de[0:nt, here, :] > k.astype(F32), BASE + DIFF * rise, 0.0)
            w = 1.0 / (e * lower + n)
            rat = n * w
            ew = e * w
            gt, gs = t + qt, s + qs
            t_out[k - 1, :, out, :] = gt * ew
            s_out[k - 1, :, out, :] = gs * ew
            ratio[k - 1, :, out, :] = rat
            return tn, sn, densn, 1.0 + rat * lower, rat * gt, rat * gs

        zero = jnp.zeros((nt, span, LANES), F32)
        carry = star(0) + (zero + 1.0, zero, zero)
        t, s, _, lower, qt, qs = lax.fori_loop(1, levels, forward, carry)
        w = 1.0 / lower
        t, s = (t + qt) * w, (s + qs) * w
        t_out[levels - 1, :, out, :] = t
        s_out[levels - 1, :, out, :] = s

        def backward(i, carry):
            t, s = carry
            k = levels - 2 - i
            rat = ratio[k, :, out, :]
            t = t_out[k, :, out, :] + rat * t
            s = s_out[k, :, out, :] + rat * s
            t_out[k, :, out, :] = t
            s_out[k, :, out, :] = s
            return t, s

        lax.fori_loop(0, levels - 1, backward, (t, s))

    recv_ns(flat_up, flat_down)
    for c in along2:
        c.wait_recv()
    recv_ns(corner_up2, corner_down2)
    wide = slice(SUB - NSUB, end + NSUB)
    count = rows + 2 * NSUB
    halo = jnp.where((lane_of((count, LANES)) & 7) >= 4, fe2[wide, :], fw2[wide, :])
    for f in range(FLAT):
        flat_out[f, 0:nt, 0:count] = flat[f, :, wide, :]
        flat_out[f, nt, 0:count] = pltpu.roll(halo, LANES - 8 * f - 4, 1)
    flat_out[5, :, count:, :] = jnp.zeros((nt + 1, SUB, LANES), F32)

    for c in along0 + along1 + along2:
        c.wait_send()
    sent_ns(depth_up + corner_up0 + field_up + corner_up1 + flat_up + corner_up2,
            depth_down + corner_down0 + field_down + corner_down1 + flat_down + corner_down2)


def tail(
    t, s, ut, vt, flat,
    t_out, s_out, u_out, v_out, eta_out, tx_out, ty_out,
    eta, bu, bv, hx, hy, un, vn, cor, sem,
):
    levels, nt, rows, _ = t.shape
    count = rows + 2 * NSUB
    lane = lane_of((SUB, LANES))
    copies = []

    def put(src, dst):
        for c in range(nt):
            copies.append(pltpu.make_async_copy(
                src(c), dst(pl.ds(c * LANES, LANES)), sem.at[len(copies)]))
            copies[-1].start()

    put(lambda c: t.at[:, c], lambda d: t_out.at[:, :, d])
    put(lambda c: s.at[:, c], lambda d: s_out.at[:, :, d])

    for ref in (eta, bu, bv):
        ref[:, 0:SUB, :] = jnp.zeros((nt + 1, SUB, LANES), F32)
        ref[:, count + SUB:, :] = jnp.zeros((nt + 1, SUB, LANES), F32)
    tiles = range(0, count, SUB)
    eta[:, SUB:count + SUB, :] = flat[0, :, 0:count, :]
    bu[:, SUB:count + SUB, :] = flat[1, :, 0:count, :]
    bv[:, SUB:count + SUB, :] = flat[2, :, 0:count, :]
    for r in tiles:
        d = flat[5, :, r:r + SUB, :]
        hx[:, r:r + SUB, :] = jnp.minimum(d, east_all(d, lane))
        hy[:, r:r + SUB, :] = jnp.minimum(d, flat[5, :, r + 1:r + SUB + 1, :])
    for sub in range(NSUB):
        for r in tiles:
            here, below = slice(SUB + r, 2 * SUB + r), slice(SUB + r - 1, 2 * SUB + r - 1)
            x = bu[:, here, :]
            eta[:, here, :] = eta[:, here, :] - HEIGHT_FACTOR * (
                x - west_all(x, lane) + (bv[:, here, :] - bv[:, below, :]))
        for r in tiles:
            here, above = slice(SUB + r, 2 * SUB + r), slice(SUB + r + 1, 2 * SUB + r + 1)
            raw = slice(r, r + SUB)
            x = eta[:, here, :]
            bu[:, here, :] = (bu[:, here, :] + (1.0 / NSUB) * flat[3, :, raw, :]
                              - SLOPE_FACTOR * hx[:, raw, :] * (east_all(x, lane) - x))
            bv[:, here, :] = (bv[:, here, :] + (1.0 / NSUB) * flat[4, :, raw, :]
                              - SLOPE_FACTOR * hy[:, raw, :] * (eta[:, above, :] - x))
    mid = pl.ds(SUB + NSUB, rows)
    put(lambda c: eta.at[c, mid, :], lambda d: eta_out.at[:, d])
    put(lambda c: bu.at[c, mid, :], lambda d: tx_out.at[:, d])
    put(lambda c: bv.at[c, mid, :], lambda d: ty_out.at[:, d])

    for r in range(0, rows, SUB):
        raw = slice(NSUB + r, NSUB + r + SUB)
        hu, hv = hx[0:nt, raw, :], hy[0:nt, raw, :]
        done = slice(SUB + NSUB + r, 2 * SUB + NSUB + r)
        out = slice(r, r + SUB)
        cor[0, :, out, :] = (bu[0:nt, done, :] - (flat[3, 0:nt, raw, :] + flat[1, 0:nt, raw, :])) / jnp.maximum(hu, 1.0)
        cor[1, :, out, :] = (bv[0:nt, done, :] - (flat[4, 0:nt, raw, :] + flat[2, 0:nt, raw, :])) / jnp.maximum(hv, 1.0)
        cor[2, :, out, :] = hu
        cor[3, :, out, :] = hv

    @pl.loop(0, levels)
    def _(k):
        kf = k.astype(F32)
        un[k] = jnp.where(cor[2] > kf, ut[k] + cor[0], 0.0)
        vn[k] = jnp.where(cor[3] > kf, vt[k] + cor[1], 0.0)

    put(lambda c: un.at[:, c], lambda d: u_out.at[:, :, d])
    put(lambda c: vn.at[:, c], lambda d: v_out.at[:, :, d])
    for c in copies:
        c.wait()


def body(*args):
    levels, rows, cols = args[0].shape
    nt = cols // LANES
    erows = rows + 2 * SUB
    count = rows + 2 * NSUB

    def vmem(*shape):
        return pltpu.VMEM(shape, F32)

    def out(*shape):
        return jax.ShapeDtypeStruct(shape, F32)

    block = pl.BlockSpec(memory_space=pltpu.VMEM)
    far = pl.BlockSpec(memory_space=pltpu.HBM)
    raw = vmem(levels, nt, erows, LANES)
    own = vmem(levels, nt, rows, LANES)
    wide = vmem(levels, nt + 1, erows, LANES)
    ints = pltpu.VMEM((nt, rows, LANES), jnp.int32)
    n1, n2 = 2 + 8 + 6 + 6, 2 + 6
    cube = (levels, nt, rows, LANES)
    parts = pl.pallas_call(
        functools.partial(kernel, rows * lax.axis_size("lat")),
        out_shape=(out(*cube),) * 4 + (out(FLAT, nt + 1, count + SUB, LANES),),
        in_specs=[far] * 9,
        out_specs=(block,) * 5,
        scratch_shapes=(
            [raw] * 6 + [wide] * 3 + [own, own, raw, raw, own]
            + [vmem(nt, rows, LANES)] * 2 + [ints] * 2
            + [vmem(nt + 1, erows + SUB, LANES)] + [vmem(nt + 1, erows, LANES)] * 2
            + [vmem(FLAT, nt, erows, LANES)]
            + [vmem(rows // SUB, SUB, LANES)] * 2
            + [vmem(rows, LANES), vmem(erows, LANES), vmem(erows, LANES)]
            + [vmem(2, rows, LANES), vmem(2, erows, LANES), vmem(2, erows, LANES)]
            + [vmem(rows, LANES), vmem(erows, LANES), vmem(erows, LANES), vmem(rows, LANES)]
            + [pltpu.SemaphoreType.DMA((9 * nt,))]
            + [pltpu.SemaphoreType.DMA((n1,))] * 2
            + [pltpu.SemaphoreType.DMA((n2,))] * 2
        ),
        compiler_params=pltpu.CompilerParams(
            collective_id=0, has_side_effects=True, vmem_limit_bytes=32 * 1024 * 1024),
    )(*[pltpu.with_memory_space_constraint(a, pltpu.HBM) for a in args])
    cube, plane = (levels, rows, cols), (rows, cols)
    return pl.pallas_call(
        tail,
        out_shape=(pltpu.HBM(cube, F32),) * 4 + (pltpu.HBM(plane, F32),) * 3,
        in_specs=[block] * 5,
        out_specs=(far,) * 7,
        scratch_shapes=(
            [vmem(nt + 1, count + 2 * SUB, LANES)] * 3 + [vmem(nt + 1, count, LANES)] * 2
            + [own, own, vmem(4, nt, rows, LANES)]
            + [pltpu.SemaphoreType.DMA((7 * nt,))]
        ),
        compiler_params=pltpu.CompilerParams(vmem_limit_bytes=32 * 1024 * 1024),
    )(*parts)


def solution(mesh):
    cube, plane = P(None, "lat", "lon"), P("lat", "lon")
    return jax.shard_map(
        body,
        mesh=mesh,
        in_specs=(cube,) * 4 + (plane,) * 5,
        out_specs=(cube,) * 4 + (plane,) * 3,
        check_vma=False,
    )
```

```python
import functools

import jax
import jax.numpy as jnp
from jax import lax
from jax.experimental import pallas as pl
from jax.experimental.pallas import tpu as pltpu
from jax.sharding import PartitionSpec as P

NSUB = 4
TIME_STEP = 0.4
TRACER_DIFF = 0.05
MOMENTUM_DIFF = 0.05
BOTTOM_DRAG = 0.05
WIND_FACTOR = 0.5
CORIOLIS_SCALE = 0.5
LATITUDE_SPAN = 2.6
GRAVITY_FACTOR = 0.3
THERMAL_COEF = 0.2
HALINE_COEF = 0.8
BACKGROUND_MIX = 0.05
CONVECTIVE_MIX = 1.5
STABILITY_FACTOR = 5.0
HEIGHT_FACTOR = 0.2
SLOPE_FACTOR = 0.15

LANES = 128
SUB = 8
FLAT = 6
MESH = pl.DeviceIdType.MESH
F32 = jnp.float32


def lane_of(shape):
    return lax.broadcasted_iota(jnp.int32, shape, len(shape) - 1)


def east(x, lane, s=1):
    r = pltpu.roll(x, LANES - s, 2)
    return jnp.where(lane < LANES - s, r[:-1], r[1:])


def west(x, lane):
    r = pltpu.roll(x, 1, 2)
    return jnp.where(lane >= 1, r[:-1], jnp.concatenate([r[-1:], r[:-2]], axis=0))


def east_all(x, lane, s=1):
    r = pltpu.roll(x, LANES - s, 2)
    return jnp.where(lane < LANES - s, r, jnp.concatenate([r[1:], r[:1]], axis=0))


def west_all(x, lane):
    r = pltpu.roll(x, 1, 2)
    return jnp.where(lane >= 1, r, jnp.concatenate([r[-1:], r[:-1]], axis=0))


def step_loop(first, last, unroll, body, carry):
    n = (last - first) // unroll

    def group(g, c):
        for i in range(unroll):
            c = body(first + g * unroll + i, c)
        return c

    carry = lax.fori_loop(0, n, group, carry)
    for k in range(first + n * unroll, last):
        carry = body(jnp.int32(k), carry)
    return carry


def east_in(x, lane, s):
    r = pltpu.roll(x, LANES - s, 2)
    return jnp.where(lane < LANES - s, r, jnp.concatenate([r[1:], jnp.zeros_like(r[:1])], axis=0))


def west_in(x, lane):
    r = pltpu.roll(x, 1, 2)
    return jnp.where(lane >= 1, r, jnp.concatenate([jnp.zeros_like(r[:1]), r[:-1]], axis=0))


def face_weights(speed, opening):
    p = speed * (TIME_STEP / 12.0)
    q = jnp.abs(p)
    m = 3.0 * q - jnp.where(opening, TIME_STEP * TRACER_DIFF, 0.0)
    p7 = 7.0 * p
    return p7 - m, p7 + m, p + q, q - p


def kernel(
    lat_total,
    t_in, s_in, u_in, v_in, eta_in, zt_in, mt_in, wi_in, bi_in,
    t_out, s_out, u_out, v_out, flat_out,
    tr, sr, ur, vr, tm, sm, um, vm, pm, wu, ev, xt, xs, yt, ys, ratio,
    zt, mt, wi, bi, de, hue, hve, flat, fu_ref, fv_ref,
    strip0, fe0, fw0, strip1, fe1, fw1, strip2, fe2, fw2, mend, edge_b, acc,
    load_sem, send1, recv1, send2, recv2,
):
    levels, nt, rows, _ = t_out.shape
    end = SUB + rows
    zero = jnp.zeros((nt, SUB, LANES), F32)
    nr = rows // SUB
    lon, lat = lax.axis_index("lon"), lax.axis_index("lat")
    nlon, nlat = lax.axis_size("lon"), lax.axis_size("lat")
    wst, est = lax.rem(lon + nlon - 1, nlon), lax.rem(lon + 1, nlon)
    nth, sth = lax.rem(lat + 1, nlat), lax.rem(lat + nlat - 1, nlat)
    has_n, has_s = lat < nlat - 1, lat > 0
    own = pl.ds(SUB, rows)

    barrier = pltpu.get_barrier_semaphore()

    def greet(lo, la):
        pl.semaphore_signal(barrier, inc=1, device_id=(lo, la), device_id_type=MESH)

    greet(wst, lat)
    greet(est, lat)

    @pl.when(has_n)
    def _():
        greet(wst, nth)
        greet(lon, nth)
        greet(est, nth)

    @pl.when(has_s)
    def _():
        greet(wst, sth)
        greet(lon, sth)
        greet(est, sth)

    loads = []

    def load(src, dst):
        group = []
        for c in range(nt):
            cols = pl.ds(c * LANES, LANES)
            group.append(pltpu.make_async_copy(
                src(cols), dst(c), load_sem.at[len(loads) * nt + c]))
            group[-1].start()
        loads.append(group)
        return group

    ld_wi = load(lambda s: wi_in.at[:, s], lambda c: wi.at[c])
    ld_bi = load(lambda s: bi_in.at[:, s], lambda c: bi.at[c])
    ld_t = load(lambda s: t_in.at[:, :, s], lambda c: tr.at[:, c, own, :])
    ld_s = load(lambda s: s_in.at[:, :, s], lambda c: sr.at[:, c, own, :])
    ld_u = load(lambda s: u_in.at[:, :, s], lambda c: ur.at[:, c, own, :])
    ld_v = load(lambda s: v_in.at[:, :, s], lambda c: vr.at[:, c, own, :])
    ld_e = load(lambda s: eta_in.at[:, s], lambda c: flat.at[0, c, own, :])
    ld_z = load(lambda s: zt_in.at[:, s], lambda c: zt.at[c])
    ld_m = load(lambda s: mt_in.at[:, s], lambda c: mt.at[c])

    def arrived(*groups):
        for g in groups:
            for c in g:
                c.wait()

    def clear(first):
        beyond = slice(first, first + SUB)
        de[:, beyond, :] = jnp.zeros((nt + 1, SUB, LANES), F32)
        for ref in (fe0, fw0, fe2, fw2):
            ref[beyond, :] = jnp.zeros((SUB, LANES), F32)
        for ref in (fe1, fw1):
            ref[:, beyond, :] = jnp.zeros((2, SUB, LANES), F32)
        for f in range(FLAT):
            flat[f, :, beyond, :] = jnp.zeros((nt, SUB, LANES), F32)

    @pl.when(jnp.logical_not(has_s))
    def _():
        clear(0)

    @pl.when(jnp.logical_not(has_n))
    def _():
        clear(end)

    def copier(send, recv):
        made = []

        def cp(src, dst, lo, la):
            n = len(made)
            made.append(pltpu.make_async_remote_copy(
                src_ref=src, dst_ref=dst, send_sem=send.at[n], recv_sem=recv.at[n],
                device_id=(lo, la), device_id_type=MESH))
            return made[-1]

        return cp

    def start_ns(up, down):
        @pl.when(has_n)
        def _():
            for c in up:
                c.start()

        @pl.when(has_s)
        def _():
            for c in down:
                c.start()

    def recv_ns(up, down):
        @pl.when(has_s)
        def _():
            for c in up:
                c.wait_recv()

        @pl.when(has_n)
        def _():
            for c in down:
                c.wait_recv()

    def sent_ns(up, down):
        @pl.when(has_n)
        def _():
            for c in up:
                c.wait_send()

        @pl.when(has_s)
        def _():
            for c in down:
                c.wait_send()

    cp = copier(send1, recv1)

    def rows_up(ref, n, at):
        return cp(at(ref, end - n, n), at(ref, SUB - n, n), lon, nth)

    def rows_down(ref, n, at):
        return cp(at(ref, SUB, n), at(ref, end, n), lon, sth)

    def cube_rows(ref, first, n):
        return ref.at[:, 0:nt, pl.ds(first, n), :]

    def plane_rows(ref, first, n):
        return ref.at[0:nt, pl.ds(first, n), :]

    depth_up, depth_down = [rows_up(de, 2, plane_rows)], [rows_down(de, 2, plane_rows)]
    field_up = [rows_up(r, n, cube_rows) for r, n in ((tr, 2), (sr, 2), (ur, 1), (vr, 1))]
    field_down = [rows_down(r, n, cube_rows) for r, n in ((tr, 2), (sr, 2), (ur, 1), (vr, 1))]

    def strips(cp, strip, fe, fw, at, n):
        along = [cp(at(strip, 0, rows), at(fe, SUB, rows), wst, lat),
                 cp(at(strip, 0, rows), at(fw, SUB, rows), est, lat)]
        up = [cp(at(strip, rows - n, n), at(fe, SUB - n, n), wst, nth),
              cp(at(strip, rows - n, n), at(fw, SUB - n, n), est, nth)]
        down = [cp(at(strip, 0, n), at(fe, end, n), wst, sth),
                cp(at(strip, 0, n), at(fw, end, n), est, sth)]
        return along, up, down

    along0, corner_up0, corner_down0 = strips(
        cp, strip0, fe0, fw0, lambda r, a, n: r.at[pl.ds(a, n), :], 2)
    along1, corner_up1, corner_down1 = strips(
        cp, strip1, fe1, fw1, lambda r, a, n: r.at[:, pl.ds(a, n), :], 2)

    lane = lane_of((SUB, LANES))
    tall = lane_of((rows, LANES))

    for k in range(levels):
        for ref in (um, vm):
            ref[k, :, 0:SUB, :] = zero
            ref[k, :, end:, :] = zero
        pm[k, :, end:, :] = zero
        wu[k, :, end:, :] = zero
        ev[k, :, 0:SUB, :] = zero
    acc[...] = jnp.zeros_like(acc)

    sub = lax.broadcasted_iota(jnp.int32, (SUB, LANES), 0)
    j = (lat * rows + sub + SUB * lax.rem(lane, nr)).astype(F32)
    j = j + jnp.where(lane < LANES // 2, 0.5, 1.0)
    f = CORIOLIS_SCALE * jnp.sin(LATITUDE_SPAN * (j / lat_total - 0.5)) * (0.25 * TIME_STEP)
    for r in range(nr):
        fu_ref[r] = jnp.broadcast_to(f[:, r:r + 1], (SUB, LANES))
        at = LANES // 2 - (LANES // 2) % nr + nr + r
        fv_ref[r] = jnp.broadcast_to(f[:, at:at + 1], (SUB, LANES))
    fu_south = jnp.broadcast_to(f[0:1, 0:1], (SUB, LANES))
    fv_north = jnp.broadcast_to(f[SUB - 1:SUB, at:at + 1], (SUB, LANES))

    def edge(first, last, p):
        return pltpu.roll(jnp.where(tall < LANES // 2, first, last), 4 * p + 2, 1)

    arrived(ld_wi, ld_bi)
    depth = (wi[...] * bi[...]).astype(F32)
    de[0:nt, own, :] = depth
    strip0[...] = edge(depth[0], depth[nt - 1], 0)
    pl.semaphore_wait(barrier, 2 + 3 * has_n.astype(jnp.int32) + 3 * has_s.astype(jnp.int32))
    for c in along0:
        c.start()
    start_ns(depth_up + corner_up0, depth_down + corner_down0)
    for n, group in enumerate((ld_t, ld_s, ld_u, ld_v)):
        arrived(group)
        start_ns(field_up[n:n + 1], field_down[n:n + 1])

    HALF = 0.5 * GRAVITY_FACTOR * TIME_STEP

    def pressure(t, s, total):
        h = (HALF * HALINE_COEF) * s - (HALF * THERMAL_COEF) * t
        p = total + h
        return p, p + h

    place = lax.shift_right_logical(tall, 2)
    group_a = jnp.zeros((rows, LANES), F32)
    group_b = jnp.zeros((rows, LANES), F32)
    total = jnp.zeros((nt, rows, LANES), F32)
    for k in range(levels):
        wet = de[0:nt, own, :] > k
        t = jnp.where(wet, tr[k, :, own, :], 0.0)
        s = jnp.where(wet, sr[k, :, own, :], 0.0)
        tm[k, :, own, :] = t
        sm[k, :, own, :] = s
        p, total = pressure(t, s, total)
        pm[k, :, own, :] = p
        group_a = jnp.where(place == 2 * k, edge(t[0], t[nt - 1], 2 * k), group_a)
        group_a = jnp.where(place == 2 * k + 1, edge(s[0], s[nt - 1], 2 * k + 1), group_a)
        group_b = jnp.where(place == 2 * k, edge(ur[k, 0, own, :], ur[k, nt - 1, own, :], 2 * k), group_b)
        group_b = jnp.where(place == 2 * k + 1, edge(vr[k, 0, own, :], vr[k, nt - 1, own, :], 2 * k + 1), group_b)
        group_b = jnp.where(tall == 8 * k + 7, pltpu.roll(p[0], 8 * k + 7, 1), group_b)
    strip1[0] = group_a
    strip1[1] = group_b
    for c in along1:
        c.start()
    start_ns(corner_up1, corner_down1)
    arrived(ld_e, ld_z, ld_m)
    flat[5, :, own, :] = depth

    for c in along0:
        c.wait_recv()
    recv_ns(depth_up + corner_up0, depth_down + corner_down0)
    high = lane_of((end + SUB, LANES))
    pair = (high & 3) >= 2
    de[nt, 0:end + SUB, :] = pltpu.roll(jnp.where(pair, fe0[...], fw0[...]), LANES - 2, 1)
    for r in range(0, end + SUB, SUB):
        d = de[:, r:r + SUB, :]
        hue[:, r:r + SUB, :] = jnp.minimum(d, east_all(d, lane))
        hve[:, r:r + SUB, :] = jnp.minimum(d, de[:, r + 1:r + SUB + 1, :])

    MIX = TIME_STEP * MOMENTUM_DIFF
    KEEP = 1.0 - TIME_STEP * BOTTOM_DRAG - 4.0 * MIX

    @pl.loop(0, levels)
    def _(k):
        kf = k.astype(F32)
        um[k, :, own, :] = jnp.where(hue[0:nt, own, :] > kf, ur[k, :, own, :], 0.0)
        vm[k, :, own, :] = jnp.where(hve[0:nt, own, :] > kf, vr[k, :, own, :], 0.0)

    @pl.loop(0, levels)
    def _(k):
        kf = k.astype(F32)
        for at in range(SUB, end, SUB):
            here = slice(at, at + SUB)
            wu[k, :, here, :] = west_in(um[k, :, here, :], lane)
            ev[k, :, here, :] = east_in(vm[k, :, here, :], lane, 1)
        for r in range(nr):
            at = SUB + SUB * r
            here, above, below = slice(at, at + SUB), slice(at + 1, at + SUB + 1), slice(at - 1, at + SUB - 1)
            out = slice(SUB * r, SUB * r + SUB)
            u, un, w = um[k, :, here, :], um[k, :, above, :], wu[k, :, here, :]
            v, vs, e = vm[k, :, here, :], vm[k, :, below, :], ev[k, :, here, :]
            p = pm[k, :, here, :]
            around_u = (east_in(u, lane, 1) + w) + (un + um[k, :, below, :])
            around_v = (west_in(v, lane) + e) + (vs + vm[k, :, above, :])
            vbar = (v + vs) + (e + ev[k, :, below, :])
            ubar = (u + un) + (w + wu[k, :, above, :])
            ut = KEEP * u + MIX * around_u + fu_ref[r] * vbar - (east_in(p, lane, 1) - p)
            vt = KEEP * v + MIX * around_v - fv_ref[r] * ubar - (pm[k, :, above, :] - p)
            ut = jnp.where(hue[0:nt, here, :] > kf, ut, 0.0)
            vt = jnp.where(hve[0:nt, here, :] > kf, vt, 0.0)
            u_out[k, :, out, :] = ut
            v_out[k, :, out, :] = vt
            for n, x in enumerate((u, v, ut, vt)):
                acc[n, :, out, :] += x

    wind_u = jnp.where(hue[0:nt, own, :] > 0.0, (TIME_STEP * WIND_FACTOR) * zt[...], 0.0)
    wind_v = jnp.where(hve[0:nt, own, :] > 0.0, (TIME_STEP * WIND_FACTOR) * mt[...], 0.0)
    u_out[0, :, 0:rows, :] += wind_u
    v_out[0, :, 0:rows, :] += wind_v
    flat[1, :, own, :] = acc[0]
    flat[2, :, own, :] = acc[1]
    flat[3, :, own, :] = acc[2] - acc[0] + wind_u
    flat[4, :, own, :] = acc[3] - acc[1] + wind_v

    for c in along1:
        c.wait_recv()
    recv_ns(corner_up1, corner_down1)
    level = lax.shift_right_logical(tall, 3).astype(F32)

    def by_lane(at, one, two, five, six):
        return jnp.where(at == 1, one, jnp.where(at == 2, two, jnp.where(at == 5, five, six)))

    def column(ref, c, at, which=own, n=rows):
        return jnp.broadcast_to(ref[c, which, at:at + 1], (n, LANES))

    LAST = LANES - 1
    for r in range(0, end + SUB, SUB):
        here = slice(r, r + SUB)
        limit = by_lane(lane & 7, *(column(ref, nt, at, here, SUB) for ref in (hue, hve) for at in (LAST, 0)))
        limit = jnp.where((lane & 7) == 7, float(levels), limit)
        x = jnp.where((lane & 3) >= 2, fe1[1, here, :], fw1[1, here, :])
        edge_b[here, :] = jnp.where(limit > lax.shift_right_logical(lane, 3).astype(F32), x, 0.0)
    x = edge_b[own, :]
    spot = tall & 7
    near = jnp.where((spot & 1) == 1, pltpu.roll(x, LAST, 1), pltpu.roll(x, 1, 1))
    above, below = slice(SUB + 1, end + 1), slice(SUB - 1, end - 1)
    turn_u = fu_ref[...].reshape(rows, LANES) * pltpu.roll(x + edge_b[below, :], LANES - 5, 1) - pltpu.roll(x, LANES - 6, 1)
    turn_v = fv_ref[...].reshape(rows, LANES) * pltpu.roll(x + edge_b[above, :], 5, 1)
    extra = MIX * near + jnp.where(spot == 1, turn_u, 0.0) - jnp.where(spot == 6, turn_v, 0.0)
    limit = by_lane(spot, column(hue, nt - 1, LAST), column(hue, 0, 0), column(hve, nt - 1, LAST), column(hve, 0, 0))
    extra = jnp.where(limit > level, extra, 0.0)
    total_u = jnp.zeros((rows, LANES), F32)
    total_v = jnp.zeros((rows, LANES), F32)
    for k in range(levels):
        du = pltpu.roll(extra, LANES - 2 - 8 * k, 1)
        dv = pltpu.roll(extra, LANES - 6 - 8 * k, 1)
        for ref, d in ((u_out, du), (v_out, dv)):
            ref[k, 0, 0:rows, :] += jnp.where(tall == 0, d, 0.0)
            ref[k, nt - 1, 0:rows, :] += jnp.where(tall == LAST, d, 0.0)
        total_u = total_u + du
        total_v = total_v + dv
    for f, d in ((3, total_u), (4, total_v)):
        flat[f, 0, own, :] += jnp.where(tall == 0, d, 0.0)
        flat[f, nt - 1, own, :] += jnp.where(tall == LAST, d, 0.0)

    recv_ns(field_up, field_down)
    top = lax.broadcasted_iota(jnp.int32, (SUB, LANES), 0) == 0

    def far_rows(k, carry):
        total, nu, nv, su, sv = carry
        kf = k.astype(F32)
        for a in (0, end):
            out = slice(a, a + SUB)
            wet = de[0:nt, out, :] > kf
            tm[k, :, out, :] = jnp.where(wet, tr[k, :, out, :], 0.0)
            sm[k, :, out, :] = jnp.where(wet, sr[k, :, out, :], 0.0)
        out = slice(0, SUB)
        vm[k, :, out, :] = jnp.where(hve[0:nt, out, :] > kf, vr[k, :, out, :], 0.0)

        out = slice(end, end + SUB)
        wet = de[0:nt, out, :] > kf
        p, total = pressure(jnp.where(wet, tr[k, :, out, :], 0.0), jnp.where(wet, sr[k, :, out, :], 0.0), total)
        u = jnp.where(hue[0:nt, out, :] > kf, ur[k, :, out, :], 0.0)
        v = jnp.where(hve[0:nt, out, :] > kf, vr[k, :, out, :], 0.0)
        edge_row = slice(end - 1, end + SUB - 1)
        du = jnp.where(top & (hue[0:nt, edge_row, :] > kf), MIX * u, 0.0)
        dv = jnp.where(top & (hve[0:nt, edge_row, :] > kf),
                       MIX * v - fv_north * (u + west_in(u, lane)) - p, 0.0)
        row = slice(rows - 1, rows + SUB - 1)
        u_out[k, :, row, :] += du
        v_out[k, :, row, :] += dv
        nu, nv = nu + du, nv + dv

        out = slice(SUB - 1, 2 * SUB - 1)
        u = jnp.where(hue[0:nt, out, :] > kf, ur[k, :, out, :], 0.0)
        v = jnp.where(hve[0:nt, out, :] > kf, vr[k, :, out, :], 0.0)
        edge_row = slice(SUB, 2 * SUB)
        du = jnp.where(top & (hue[0:nt, edge_row, :] > kf),
                       MIX * u + fu_south * (v + east_in(v, lane, 1)), 0.0)
        dv = jnp.where(top & (hve[0:nt, edge_row, :] > kf), MIX * v, 0.0)
        u_out[k, :, 0:SUB, :] += du
        v_out[k, :, 0:SUB, :] += dv
        return total, nu, nv, su + du, sv + dv

    _, nu, nv, su, sv = step_loop(0, levels, 2, far_rows, (zero,) * 5)
    for f, north, south in ((3, nu, su), (4, nv, sv)):
        flat[f, :, SUB:2 * SUB, :] += south
        flat[f, :, end - SUB:end, :] += pltpu.roll(north, SUB - 1, 1)

    spot = lax.shift_right_logical(tall, 3)
    group = jnp.zeros((rows, LANES), F32)
    for f in range(FLAT):
        x = jnp.where(tall < LANES // 2, flat[f, 0, own, :], flat[f, nt - 1, own, :])
        group = jnp.where(spot == f, pltpu.roll(x, 8 * f + 4, 1), group)
    strip2[...] = group
    cp = copier(send2, recv2)
    flat_up = [cp(cube_rows(flat, end - NSUB, NSUB), cube_rows(flat, SUB - NSUB, NSUB), lon, nth)]
    flat_down = [cp(cube_rows(flat, SUB, NSUB), cube_rows(flat, end, NSUB), lon, sth)]
    along2, corner_up2, corner_down2 = strips(
        cp, strip2, fe2, fw2, lambda r, a, n: r.at[pl.ds(a, n), :], NSUB)
    start_ns(flat_up, flat_down)
    for c in along2:
        c.start()
    start_ns(corner_up2, corner_down2)

    starts = list(range(SUB - 1, end - SUB, SUB)) + [end - SUB]

    @pl.loop(0, levels)
    def _(k):
        kf = k.astype(F32)
        for r in range(SUB, end, SUB):
            here = slice(r, r + SUB)
            w0, w1, w2, w3 = face_weights(um[k, :, here, :], hue[0:nt, here, :] > kf)
            for ref, to in ((tm, xt), (sm, xs)):
                c = ref[k, :, here, :]
                fx = (w0 * c + w1 * east_in(c, lane, 1)
                      - w2 * east_in(c, lane, 2) + w3 * west_in(c, lane))
                to[k, :, r - SUB:r, :] = c - (fx - west_in(fx, lane))
        for a in starts:
            here = slice(a, a + SUB)
            w0, w1, w2, w3 = face_weights(vm[k, :, here, :], hve[0:nt, here, :] > kf)
            for ref, to in ((tm, yt), (sm, ys)):
                to[k, :, here, :] = (
                    w0 * ref[k, :, here, :] + w1 * ref[k, :, a + 1:a + SUB + 1, :]
                    - w2 * ref[k, :, a + 2:a + SUB + 2, :] + w3 * ref[k, :, a - 1:a + SUB - 1, :])

    q = tall & 3

    def speeds(x, limit):
        x = jnp.where((tall & 7) < 4, x, pltpu.roll(x, 4, 1))
        opening = limit > level
        return face_weights(jnp.where(opening, x, 0.0), opening)

    mine = strip1[0]
    a = jnp.where(q < 2, mine, fe1[0, own, :])
    b = jnp.where(q < 2, fw1[0, own, :], mine)
    _, w1, w2, w3 = speeds(strip1[1], jnp.where(
        q == 0, column(hue, nt - 1, LANES - 2), jnp.where(q == 1, column(hue, nt - 1, LAST), column(hue, 0, 0))))
    b_west = pltpu.roll(b, 1, 1)
    flux = jnp.where(q == 1, w1 * pltpu.roll(a, LANES - 1, 1), 0.0) - w2 * pltpu.roll(a, LANES - 2, 1)
    flux = jnp.where(q < 2, flux, jnp.where(q == 2, w3 * b_west, 0.0))
    w0, w1, w2, w3 = speeds(fw1[1, own, :], column(hue, nt, LAST))
    first = w0 * b + w1 * pltpu.roll(b, LANES - 1, 1) - w2 * pltpu.roll(b, LANES - 2, 1) + w3 * b_west
    mend[...] = flux - pltpu.roll(jnp.where(q == 1, first, flux), 1, 1)

    def mended(x, m):
        edge_lane = lane_of(m.shape)
        first = x[:1] - jnp.where(edge_lane < 2, m, 0.0)[None]
        last = x[-1:] - jnp.where(edge_lane >= LANES - 2, m, 0.0)[None]
        return jnp.concatenate([first, x[1:-1], last], axis=0)

    span = 2 * SUB if rows % (2 * SUB) == 0 else SUB
    DIFF = TIME_STEP * STABILITY_FACTOR * BACKGROUND_MIX
    BASE = TIME_STEP * (BACKGROUND_MIX + CONVECTIVE_MIX)
    for r in range(0, rows, span):
        out = slice(r, r + span)
        here, below = slice(SUB + r, SUB + r + span), slice(SUB + r - 1, SUB + r + span - 1)

        def star(k):
            t = xt[k, :, out, :] - (yt[k, :, here, :] - yt[k, :, below, :])
            s = xs[k, :, out, :] - (ys[k, :, here, :] - ys[k, :, below, :])
            t = mended(t, pltpu.roll(mend[out, :], LANES - 2 - 8 * k, 1))
            s = mended(s, pltpu.roll(mend[out, :], LANES - 6 - 8 * k, 1))
            return t, s, HALINE_COEF * s - THERMAL_COEF * t

        def forward(k, carry):
            t, s, dens, lower, qt, qs = carry
            tn, sn, densn = star(k)
            rise = jnp.maximum(densn - dens, 0.0)
            e = 1.0 + STABILITY_FACTOR * rise
            n = jnp.where(de[0:nt, here, :] > k.astype(F32), BASE + DIFF * rise, 0.0)
            w = 1.0 / (e * lower + n)
            rat = n * w
            ew = e * w
            gt, gs = t + qt, s + qs
            t_out[k - 1, :, out, :] = gt * ew
            s_out[k - 1, :, out, :] = gs * ew
            ratio[k - 1, :, out, :] = rat
            return tn, sn, densn, 1.0 + rat * lower, rat * gt, rat * gs

        zero = jnp.zeros((nt, span, LANES), F32)
        carry = star(0) + (zero + 1.0, zero, zero)
        t, s, _, lower, qt, qs = lax.fori_loop(1, levels, forward, carry)
        w = 1.0 / lower
        t, s = (t + qt) * w, (s + qs) * w
        t_out[levels - 1, :, out, :] = t
        s_out[levels - 1, :, out, :] = s

        def backward(i, carry):
            t, s = carry
            k = levels - 2 - i
            rat = ratio[k, :, out, :]
            t = t_out[k, :, out, :] + rat * t
            s = s_out[k, :, out, :] + rat * s
            t_out[k, :, out, :] = t
            s_out[k, :, out, :] = s
            return t, s

        lax.fori_loop(0, levels - 1, backward, (t, s))

    recv_ns(flat_up, flat_down)
    for c in along2:
        c.wait_recv()
    recv_ns(corner_up2, corner_down2)
    wide = slice(SUB - NSUB, end + NSUB)
    count = rows + 2 * NSUB
    halo = jnp.where((lane_of((count, LANES)) & 7) >= 4, fe2[wide, :], fw2[wide, :])
    for f in range(FLAT):
        flat_out[f, 0:nt, 0:count] = flat[f, :, wide, :]
        flat_out[f, nt, 0:count] = pltpu.roll(halo, LANES - 8 * f - 4, 1)
    flat_out[5, :, count:, :] = jnp.zeros((nt + 1, SUB, LANES), F32)

    for c in along0 + along1 + along2:
        c.wait_send()
    sent_ns(depth_up + corner_up0 + field_up + corner_up1 + flat_up + corner_up2,
            depth_down + corner_down0 + field_down + corner_down1 + flat_down + corner_down2)


def tail(
    t, s, ut, vt, flat,
    t_out, s_out, u_out, v_out, eta_out, tx_out, ty_out,
    eta, bu, bv, hx, hy, un, vn, cor, sem,
):
    levels, nt, rows, _ = t.shape
    count = rows + 2 * NSUB
    lane = lane_of((SUB, LANES))
    copies = []

    def put(src, dst):
        for c in range(nt):
            copies.append(pltpu.make_async_copy(
                src(c), dst(pl.ds(c * LANES, LANES)), sem.at[len(copies)]))
            copies[-1].start()

    put(lambda c: t.at[:, c], lambda d: t_out.at[:, :, d])
    put(lambda c: s.at[:, c], lambda d: s_out.at[:, :, d])

    for ref in (eta, bu, bv):
        ref[:, 0:SUB, :] = jnp.zeros((nt + 1, SUB, LANES), F32)
        ref[:, count + SUB:, :] = jnp.zeros((nt + 1, SUB, LANES), F32)
    tiles = range(0, count, SUB)
    eta[:, SUB:count + SUB, :] = flat[0, :, 0:count, :]
    bu[:, SUB:count + SUB, :] = flat[1, :, 0:count, :]
    bv[:, SUB:count + SUB, :] = flat[2, :, 0:count, :]
    for r in tiles:
        d = flat[5, :, r:r + SUB, :]
        hx[:, r:r + SUB, :] = jnp.minimum(d, east_all(d, lane))
        hy[:, r:r + SUB, :] = jnp.minimum(d, flat[5, :, r + 1:r + SUB + 1, :])
    for sub in range(NSUB):
        for r in tiles:
            here, below = slice(SUB + r, 2 * SUB + r), slice(SUB + r - 1, 2 * SUB + r - 1)
            x = bu[:, here, :]
            eta[:, here, :] = eta[:, here, :] - HEIGHT_FACTOR * (
                x - west_all(x, lane) + (bv[:, here, :] - bv[:, below, :]))
        for r in tiles:
            here, above = slice(SUB + r, 2 * SUB + r), slice(SUB + r + 1, 2 * SUB + r + 1)
            raw = slice(r, r + SUB)
            x = eta[:, here, :]
            bu[:, here, :] = (bu[:, here, :] + (1.0 / NSUB) * flat[3, :, raw, :]
                              - SLOPE_FACTOR * hx[:, raw, :] * (east_all(x, lane) - x))
            bv[:, here, :] = (bv[:, here, :] + (1.0 / NSUB) * flat[4, :, raw, :]
                              - SLOPE_FACTOR * hy[:, raw, :] * (eta[:, above, :] - x))
    mid = pl.ds(SUB + NSUB, rows)
    put(lambda c: eta.at[c, mid, :], lambda d: eta_out.at[:, d])
    put(lambda c: bu.at[c, mid, :], lambda d: tx_out.at[:, d])
    put(lambda c: bv.at[c, mid, :], lambda d: ty_out.at[:, d])

    for r in range(0, rows, SUB):
        raw = slice(NSUB + r, NSUB + r + SUB)
        hu, hv = hx[0:nt, raw, :], hy[0:nt, raw, :]
        done = slice(SUB + NSUB + r, 2 * SUB + NSUB + r)
        out = slice(r, r + SUB)
        cor[0, :, out, :] = (bu[0:nt, done, :] - (flat[3, 0:nt, raw, :] + flat[1, 0:nt, raw, :])) / jnp.maximum(hu, 1.0)
        cor[1, :, out, :] = (bv[0:nt, done, :] - (flat[4, 0:nt, raw, :] + flat[2, 0:nt, raw, :])) / jnp.maximum(hv, 1.0)
        cor[2, :, out, :] = hu
        cor[3, :, out, :] = hv

    @pl.loop(0, levels)
    def _(k):
        kf = k.astype(F32)
        un[k] = jnp.where(cor[2] > kf, ut[k, :, 0:rows, :] + cor[0], 0.0)
        vn[k] = jnp.where(cor[3] > kf, vt[k, :, 0:rows, :] + cor[1], 0.0)

    put(lambda c: un.at[:, c], lambda d: u_out.at[:, :, d])
    put(lambda c: vn.at[:, c], lambda d: v_out.at[:, :, d])
    for c in copies:
        c.wait()


def body(*args):
    levels, rows, cols = args[0].shape
    nt = cols // LANES
    erows = rows + 2 * SUB
    count = rows + 2 * NSUB

    def vmem(*shape):
        return pltpu.VMEM(shape, F32)

    def out(*shape):
        return jax.ShapeDtypeStruct(shape, F32)

    block = pl.BlockSpec(memory_space=pltpu.VMEM)
    far = pl.BlockSpec(memory_space=pltpu.HBM)
    raw = vmem(levels, nt, erows, LANES)
    own = vmem(levels, nt, rows, LANES)
    ints = pltpu.VMEM((nt, rows, LANES), jnp.int32)
    n1, n2 = 2 + 8 + 6 + 6, 2 + 6
    cube = (levels, nt, rows, LANES)
    parts = pl.pallas_call(
        functools.partial(kernel, rows * lax.axis_size("lat")),
        out_shape=(out(*cube),) * 2 + (out(levels, nt, rows + SUB, LANES),) * 2 + (out(FLAT, nt + 1, count + SUB, LANES),),
        in_specs=[far] * 9,
        out_specs=(block,) * 5,
        scratch_shapes=(
            [raw] * 11 + [own, own, raw, raw, own]
            + [vmem(nt, rows, LANES)] * 2 + [ints] * 2
            + [vmem(nt + 1, erows + SUB, LANES)] + [vmem(nt + 1, erows, LANES)] * 2
            + [vmem(FLAT, nt, erows, LANES)]
            + [vmem(rows // SUB, SUB, LANES)] * 2
            + [vmem(rows, LANES), vmem(erows, LANES), vmem(erows, LANES)]
            + [vmem(2, rows, LANES), vmem(2, erows, LANES), vmem(2, erows, LANES)]
            + [vmem(rows, LANES), vmem(erows, LANES), vmem(erows, LANES), vmem(rows, LANES)]
            + [vmem(erows, LANES), vmem(4, nt, rows, LANES)]
            + [pltpu.SemaphoreType.DMA((9 * nt,))]
            + [pltpu.SemaphoreType.DMA((n1,))] * 2
            + [pltpu.SemaphoreType.DMA((n2,))] * 2
        ),
        compiler_params=pltpu.CompilerParams(
            collective_id=0, has_side_effects=True, vmem_limit_bytes=32 * 1024 * 1024),
    )(*[pltpu.with_memory_space_constraint(a, pltpu.HBM) for a in args])
    cube, plane = (levels, rows, cols), (rows, cols)
    return pl.pallas_call(
        tail,
        out_shape=(pltpu.HBM(cube, F32),) * 4 + (pltpu.HBM(plane, F32),) * 3,
        in_specs=[block] * 5,
        out_specs=(far,) * 7,
        scratch_shapes=(
            [vmem(nt + 1, count + 2 * SUB, LANES)] * 3 + [vmem(nt + 1, count, LANES)] * 2
            + [own, own, vmem(4, nt, rows, LANES)]
            + [pltpu.SemaphoreType.DMA((7 * nt,))]
        ),
        compiler_params=pltpu.CompilerParams(vmem_limit_bytes=32 * 1024 * 1024),
    )(*parts)


def solution(mesh):
    cube, plane = P(None, "lat", "lon"), P("lat", "lon")
    return jax.shard_map(
        body,
        mesh=mesh,
        in_specs=(cube,) * 4 + (plane,) * 5,
        out_specs=(cube,) * 4 + (plane,) * 3,
        check_vma=False,
    )
```

```python
import functools

import jax
import jax.numpy as jnp
from jax import lax
from jax.experimental import pallas as pl
from jax.experimental.pallas import tpu as pltpu
from jax.sharding import PartitionSpec as P

NSUB = 4
TIME_STEP = 0.4
TRACER_DIFF = 0.05
MOMENTUM_DIFF = 0.05
BOTTOM_DRAG = 0.05
WIND_FACTOR = 0.5
CORIOLIS_SCALE = 0.5
LATITUDE_SPAN = 2.6
GRAVITY_FACTOR = 0.3
THERMAL_COEF = 0.2
HALINE_COEF = 0.8
BACKGROUND_MIX = 0.05
CONVECTIVE_MIX = 1.5
STABILITY_FACTOR = 5.0
HEIGHT_FACTOR = 0.2
SLOPE_FACTOR = 0.15

LANES = 128
SUB = 8
FLAT = 6
MESH = pl.DeviceIdType.MESH
F32 = jnp.float32


def lane_of(shape):
    return lax.broadcasted_iota(jnp.int32, shape, len(shape) - 1)


def east(x, lane, s=1):
    r = pltpu.roll(x, LANES - s, 2)
    return jnp.where(lane < LANES - s, r[:-1], r[1:])


def west(x, lane):
    r = pltpu.roll(x, 1, 2)
    return jnp.where(lane >= 1, r[:-1], jnp.concatenate([r[-1:], r[:-2]], axis=0))


def east_all(x, lane, s=1):
    r = pltpu.roll(x, LANES - s, 2)
    return jnp.where(lane < LANES - s, r, jnp.concatenate([r[1:], r[:1]], axis=0))


def west_all(x, lane):
    r = pltpu.roll(x, 1, 2)
    return jnp.where(lane >= 1, r, jnp.concatenate([r[-1:], r[:-1]], axis=0))


def step_loop(first, last, unroll, body, carry):
    n = (last - first) // unroll

    def group(g, c):
        for i in range(unroll):
            c = body(first + g * unroll + i, c)
        return c

    carry = lax.fori_loop(0, n, group, carry)
    for k in range(first + n * unroll, last):
        carry = body(jnp.int32(k), carry)
    return carry


def east_in(x, lane, s):
    r = pltpu.roll(x, LANES - s, 2)
    return jnp.where(lane < LANES - s, r, jnp.concatenate([r[1:], jnp.zeros_like(r[:1])], axis=0))


def west_in(x, lane):
    r = pltpu.roll(x, 1, 2)
    return jnp.where(lane >= 1, r, jnp.concatenate([jnp.zeros_like(r[:1]), r[:-1]], axis=0))


def face_weights(speed, opening):
    p = speed * (TIME_STEP / 12.0)
    q = jnp.abs(p)
    m = 3.0 * q - jnp.where(opening, TIME_STEP * TRACER_DIFF, 0.0)
    p7 = 7.0 * p
    return p7 - m, p7 + m, p + q, q - p


def kernel(
    lat_total,
    t_in, s_in, u_in, v_in, eta_in, zt_in, mt_in, wi_in, bi_in,
    t_out, s_out, u_out, v_out, flat_out,
    tr, sr, ur, vr, tm, sm, um, vm, pm, wu, ev, xt, xs, yt, ys, ratio,
    zt, mt, wi, bi, de, hue, hve, flat, fu_ref, fv_ref,
    strip0, fe0, fw0, strip_a, fe_a, fw_a, strip_b, fe_b, fw_b, strip_c, fe_c,
    strip2, fe2, fw2, mend, edge_b, acc, pn,
    load_sem, send1, recv1, send2, recv2,
):
    levels, nt, rows, _ = t_out.shape
    end = SUB + rows
    zero = jnp.zeros((nt, SUB, LANES), F32)
    nr = rows // SUB
    lon, lat = lax.axis_index("lon"), lax.axis_index("lat")
    nlon, nlat = lax.axis_size("lon"), lax.axis_size("lat")
    wst, est = lax.rem(lon + nlon - 1, nlon), lax.rem(lon + 1, nlon)
    nth, sth = lax.rem(lat + 1, nlat), lax.rem(lat + nlat - 1, nlat)
    has_n, has_s = lat < nlat - 1, lat > 0
    own = pl.ds(SUB, rows)

    barrier = pltpu.get_barrier_semaphore()

    def greet(lo, la):
        pl.semaphore_signal(barrier, inc=1, device_id=(lo, la), device_id_type=MESH)

    greet(wst, lat)
    greet(est, lat)

    @pl.when(has_n)
    def _():
        greet(wst, nth)
        greet(lon, nth)
        greet(est, nth)

    @pl.when(has_s)
    def _():
        greet(wst, sth)
        greet(lon, sth)
        greet(est, sth)

    loads = []

    def load(src, dst):
        group = []
        for c in range(nt):
            cols = pl.ds(c * LANES, LANES)
            group.append(pltpu.make_async_copy(
                src(cols), dst(c), load_sem.at[len(loads) * nt + c]))
            group[-1].start()
        loads.append(group)
        return group

    ld_wi = load(lambda s: wi_in.at[:, s], lambda c: wi.at[c])
    ld_bi = load(lambda s: bi_in.at[:, s], lambda c: bi.at[c])
    ld_u = load(lambda s: u_in.at[:, :, s], lambda c: ur.at[:, c, own, :])
    ld_v = load(lambda s: v_in.at[:, :, s], lambda c: vr.at[:, c, own, :])
    ld_t = load(lambda s: t_in.at[:, :, s], lambda c: tr.at[:, c, own, :])
    ld_s = load(lambda s: s_in.at[:, :, s], lambda c: sr.at[:, c, own, :])
    ld_e = load(lambda s: eta_in.at[:, s], lambda c: flat.at[0, c, own, :])
    ld_z = load(lambda s: zt_in.at[:, s], lambda c: zt.at[c])
    ld_m = load(lambda s: mt_in.at[:, s], lambda c: mt.at[c])

    def arrived(*groups):
        for g in groups:
            for c in g:
                c.wait()

    def clear(first):
        beyond = slice(first, first + SUB)
        de[:, beyond, :] = jnp.zeros((nt + 1, SUB, LANES), F32)
        for ref in (fe0, fw0, fe_b, fw_b, fe2, fw2):
            ref[beyond, :] = jnp.zeros((SUB, LANES), F32)
        for f in range(FLAT):
            flat[f, :, beyond, :] = jnp.zeros((nt, SUB, LANES), F32)

    @pl.when(jnp.logical_not(has_s))
    def _():
        clear(0)

    @pl.when(jnp.logical_not(has_n))
    def _():
        clear(end)

    def copier(send, recv):
        made = []

        def cp(src, dst, lo, la):
            n = len(made)
            made.append(pltpu.make_async_remote_copy(
                src_ref=src, dst_ref=dst, send_sem=send.at[n], recv_sem=recv.at[n],
                device_id=(lo, la), device_id_type=MESH))
            return made[-1]

        return cp

    def start_ns(up, down):
        @pl.when(has_n)
        def _():
            for c in up:
                c.start()

        @pl.when(has_s)
        def _():
            for c in down:
                c.start()

    def recv_ns(up, down):
        @pl.when(has_s)
        def _():
            for c in up:
                c.wait_recv()

        @pl.when(has_n)
        def _():
            for c in down:
                c.wait_recv()

    def sent_ns(up, down):
        @pl.when(has_n)
        def _():
            for c in up:
                c.wait_send()

        @pl.when(has_s)
        def _():
            for c in down:
                c.wait_send()

    cp = copier(send1, recv1)

    def rows_up(ref, n, at):
        return cp(at(ref, end - n, n), at(ref, SUB - n, n), lon, nth)

    def rows_down(ref, n, at):
        return cp(at(ref, SUB, n), at(ref, end, n), lon, sth)

    def cube_rows(ref, first, n):
        return ref.at[:, 0:nt, pl.ds(first, n), :]

    def plane_rows(ref, first, n):
        return ref.at[0:nt, pl.ds(first, n), :]

    depth_up, depth_down = [rows_up(de, 2, plane_rows)], [rows_down(de, 2, plane_rows)]
    flow_up = [rows_up(r, 1, cube_rows) for r in (ur, vr)]
    flow_down = [rows_down(r, 1, cube_rows) for r in (ur, vr)]
    tracer_up = [rows_up(r, 2, cube_rows) for r in (tr, sr)]
    tracer_down = [rows_down(r, 2, cube_rows) for r in (tr, sr)]
    press_down = [cp(cube_rows(pm, SUB, 1), cube_rows(pn, 0, 1), lon, sth)]

    def strips(cp, strip, fe, fw, n):
        def at(ref, first, size):
            return ref.at[pl.ds(first, size), :]

        along = [cp(at(strip, 0, rows), at(fe, SUB, rows), wst, lat),
                 cp(at(strip, 0, rows), at(fw, SUB, rows), est, lat)]
        up = [cp(at(strip, rows - n, n), at(fe, SUB - n, n), wst, nth),
              cp(at(strip, rows - n, n), at(fw, SUB - n, n), est, nth)]
        down = [cp(at(strip, 0, n), at(fe, end, n), wst, sth),
                cp(at(strip, 0, n), at(fw, end, n), est, sth)]
        return along, up, down

    along0, corner_up0, corner_down0 = strips(
        cp, strip0, fe0, fw0, 2)
    along_b = [cp(strip_b, fe_b.at[own, :], wst, lat), cp(strip_b, fw_b.at[own, :], est, lat)]
    corner_up_b = [cp(strip_b.at[pl.ds(rows - 1, 1), :], fe_b.at[pl.ds(SUB - 1, 1), :], wst, nth)]
    corner_down_b = [cp(strip_b.at[pl.ds(0, 1), :], fw_b.at[pl.ds(end, 1), :], est, sth)]
    along_a = [cp(strip_a, fe_a, wst, lat), cp(strip_a, fw_a, est, lat)]
    along_c = [cp(strip_c, fe_c, wst, lat)]

    lane = lane_of((SUB, LANES))
    tall = lane_of((rows, LANES))

    for k in range(levels):
        for ref in (um, vm):
            ref[k, :, 0:SUB, :] = zero
            ref[k, :, end:, :] = zero
        pm[k, :, end:, :] = zero
        wu[k, :, end:, :] = zero
        ev[k, :, 0:SUB, :] = zero
    acc[...] = jnp.zeros_like(acc)

    sub = lax.broadcasted_iota(jnp.int32, (SUB, LANES), 0)
    j = (lat * rows + sub + SUB * lax.rem(lane, nr)).astype(F32)
    j = j + jnp.where(lane < LANES // 2, 0.5, 1.0)
    f = CORIOLIS_SCALE * jnp.sin(LATITUDE_SPAN * (j / lat_total - 0.5)) * (0.25 * TIME_STEP)
    for r in range(nr):
        fu_ref[r] = jnp.broadcast_to(f[:, r:r + 1], (SUB, LANES))
        at = LANES // 2 - (LANES // 2) % nr + nr + r
        fv_ref[r] = jnp.broadcast_to(f[:, at:at + 1], (SUB, LANES))
    fu_south = jnp.broadcast_to(f[0:1, 0:1], (SUB, LANES))
    fv_north = jnp.broadcast_to(f[SUB - 1:SUB, at:at + 1], (SUB, LANES))

    def edge(first, last, p):
        return pltpu.roll(jnp.where(tall < LANES // 2, first, last), 4 * p + 2, 1)

    arrived(ld_wi, ld_bi)
    depth = (wi[...] * bi[...]).astype(F32)
    de[0:nt, own, :] = depth
    strip0[...] = edge(depth[0], depth[nt - 1], 0)
    pl.semaphore_wait(barrier, 2 + 3 * has_n.astype(jnp.int32) + 3 * has_s.astype(jnp.int32))
    for c in along0:
        c.start()
    start_ns(depth_up + corner_up0, depth_down + corner_down0)
    for n, group in enumerate((ld_u, ld_v)):
        arrived(group)
        start_ns(flow_up[n:n + 1], flow_down[n:n + 1])

    place = lax.shift_right_logical(tall, 2)
    group = jnp.zeros((rows, LANES), F32)
    for k in range(levels):
        for n, ref in enumerate((ur, vr)):
            group = jnp.where(place == 2 * k + n, edge(ref[k, 0, own, :], ref[k, nt - 1, own, :], 2 * k + n), group)
    strip_b[...] = group
    for c in along_b:
        c.start()
    start_ns(corner_up_b, corner_down_b)

    HALF = 0.5 * GRAVITY_FACTOR * TIME_STEP
    arrived(ld_t, ld_s)
    group = jnp.zeros((rows, LANES), F32)
    total = jnp.zeros((nt, rows, LANES), F32)
    for k in range(levels):
        wet = de[0:nt, own, :] > k
        t = jnp.where(wet, tr[k, :, own, :], 0.0)
        s = jnp.where(wet, sr[k, :, own, :], 0.0)
        tm[k, :, own, :] = t
        sm[k, :, own, :] = s
        h = (HALF * HALINE_COEF) * s - (HALF * THERMAL_COEF) * t
        p = total + h
        total = p + h
        pm[k, :, own, :] = p
        group = jnp.where(tall == 8 * k + 1, pltpu.roll(p[0], 8 * k + 1, 1), group)
    strip_c[...] = group
    start_ns([], press_down)
    for c in along_c:
        c.start()
    start_ns(tracer_up, tracer_down)
    group = jnp.zeros((rows, LANES), F32)
    for k in range(levels):
        for n, ref in enumerate((tm, sm)):
            group = jnp.where(place == 2 * k + n, edge(ref[k, 0, own, :], ref[k, nt - 1, own, :], 2 * k + n), group)
    strip_a[...] = group
    for c in along_a:
        c.start()
    arrived(ld_e, ld_z, ld_m)
    flat[5, :, own, :] = depth

    def faces(first, last):
        for r in range(first, last, SUB):
            d = de[:, r:r + SUB, :]
            hue[:, r:r + SUB, :] = jnp.minimum(d, east_all(d, lane))
            hve[:, r:r + SUB, :] = jnp.minimum(d, de[:, r + 1:r + SUB + 1, :])

    for c in along0:
        c.wait_recv()
    recv_ns(depth_up, depth_down)
    de[nt, own, :] = pltpu.roll(jnp.where((tall & 3) >= 2, fe0[own, :], fw0[own, :]), LANES - 2, 1)
    faces(SUB, end)

    MIX = TIME_STEP * MOMENTUM_DIFF
    KEEP = 1.0 - TIME_STEP * BOTTOM_DRAG - 4.0 * MIX

    def momentum(k, carry):
        kf = k.astype(F32)
        for at in range(SUB, end, SUB):
            here = slice(at, at + SUB)
            u = jnp.where(hue[0:nt, here, :] > kf, ur[k, :, here, :], 0.0)
            v = jnp.where(hve[0:nt, here, :] > kf, vr[k, :, here, :], 0.0)
            um[k, :, here, :] = u
            vm[k, :, here, :] = v
            wu[k, :, here, :] = west_in(u, lane)
            ev[k, :, here, :] = east_in(v, lane, 1)
        for r in range(nr):
            at = SUB + SUB * r
            here, above, below = slice(at, at + SUB), slice(at + 1, at + SUB + 1), slice(at - 1, at + SUB - 1)
            out = slice(SUB * r, SUB * r + SUB)
            u, un, w = um[k, :, here, :], um[k, :, above, :], wu[k, :, here, :]
            v, vs, e = vm[k, :, here, :], vm[k, :, below, :], ev[k, :, here, :]
            p = pm[k, :, here, :]
            around_u = (east_in(u, lane, 1) + w) + (un + um[k, :, below, :])
            around_v = (west_in(v, lane) + e) + (vs + vm[k, :, above, :])
            vbar = (v + vs) + (e + ev[k, :, below, :])
            ubar = (u + un) + (w + wu[k, :, above, :])
            ut = KEEP * u + MIX * around_u + fu_ref[r] * vbar - (east_in(p, lane, 1) - p)
            vt = KEEP * v + MIX * around_v - fv_ref[r] * ubar - (pm[k, :, above, :] - p)
            ut = jnp.where(hue[0:nt, here, :] > kf, ut, 0.0)
            vt = jnp.where(hve[0:nt, here, :] > kf, vt, 0.0)
            u_out[k, :, out, :] = ut
            v_out[k, :, out, :] = vt
            for n, x in enumerate((u, v, ut, vt)):
                acc[n, :, out, :] += x
        return carry

    step_loop(0, levels, 2, momentum, 0)
    wind_u = jnp.where(hue[0:nt, own, :] > 0.0, (TIME_STEP * WIND_FACTOR) * zt[...], 0.0)
    wind_v = jnp.where(hve[0:nt, own, :] > 0.0, (TIME_STEP * WIND_FACTOR) * mt[...], 0.0)
    u_out[0, :, 0:rows, :] += wind_u
    v_out[0, :, 0:rows, :] += wind_v
    flat[1, :, own, :] = acc[0]
    flat[2, :, own, :] = acc[1]
    flat[3, :, own, :] = acc[2] - acc[0] + wind_u
    flat[4, :, own, :] = acc[3] - acc[1] + wind_v

    recv_ns(corner_up0, corner_down0)
    for out in (slice(0, SUB), slice(end, end + SUB)):
        de[nt, out, :] = pltpu.roll(jnp.where((lane & 3) >= 2, fe0[out, :], fw0[out, :]), LANES - 2, 1)
    faces(0, SUB)
    faces(end - SUB, end + SUB)
    for c in along_b + along_c:
        c.wait_recv()
    recv_ns(corner_up_b, corner_down_b)
    level = lax.shift_right_logical(tall, 3).astype(F32)

    def by_lane(at, one, two, five, six):
        return jnp.where(at == 1, one, jnp.where(at == 2, two, jnp.where(at == 5, five, six)))

    def column(ref, c, at, which=own, n=rows):
        return jnp.broadcast_to(ref[c, which, at:at + 1], (n, LANES))

    LAST = LANES - 1
    for r in range(0, end + SUB, SUB):
        here = slice(r, r + SUB)
        limit = by_lane(lane & 7, *(column(ref, nt, at, here, SUB) for ref in (hue, hve) for at in (LAST, 0)))
        x = jnp.where((lane & 3) >= 2, fe_b[here, :], fw_b[here, :])
        edge_b[here, :] = jnp.where(limit > lax.shift_right_logical(lane, 3).astype(F32), x, 0.0)
    x = edge_b[own, :]
    spot = tall & 7
    near = jnp.where((spot & 1) == 1, pltpu.roll(x, LAST, 1), pltpu.roll(x, 1, 1))
    above, below = slice(SUB + 1, end + 1), slice(SUB - 1, end - 1)
    turn_u = fu_ref[...].reshape(rows, LANES) * pltpu.roll(x + edge_b[below, :], LANES - 5, 1) - fe_c[...]
    turn_v = fv_ref[...].reshape(rows, LANES) * pltpu.roll(x + edge_b[above, :], 5, 1)
    extra = MIX * near + jnp.where(spot == 1, turn_u, 0.0) - jnp.where(spot == 6, turn_v, 0.0)
    limit = by_lane(spot, column(hue, nt - 1, LAST), column(hue, 0, 0), column(hve, nt - 1, LAST), column(hve, 0, 0))
    extra = jnp.where(limit > level, extra, 0.0)
    total_u = jnp.zeros((rows, LANES), F32)
    total_v = jnp.zeros((rows, LANES), F32)
    for k in range(levels):
        du = pltpu.roll(extra, LANES - 2 - 8 * k, 1)
        dv = pltpu.roll(extra, LANES - 6 - 8 * k, 1)
        for ref, d in ((u_out, du), (v_out, dv)):
            ref[k, 0, 0:rows, :] += jnp.where(tall == 0, d, 0.0)
            ref[k, nt - 1, 0:rows, :] += jnp.where(tall == LAST, d, 0.0)
        total_u = total_u + du
        total_v = total_v + dv
    for f, d in ((3, total_u), (4, total_v)):
        flat[f, 0, own, :] += jnp.where(tall == 0, d, 0.0)
        flat[f, nt - 1, own, :] += jnp.where(tall == LAST, d, 0.0)

    recv_ns(flow_up, flow_down)
    recv_ns([], press_down)
    top = lax.broadcasted_iota(jnp.int32, (SUB, LANES), 0) == 0

    def far_rows(k, carry):
        nu, nv, su, sv = carry
        kf = k.astype(F32)
        out = slice(end, end + SUB)
        u = jnp.where(hue[0:nt, out, :] > kf, ur[k, :, out, :], 0.0)
        v = jnp.where(hve[0:nt, out, :] > kf, vr[k, :, out, :], 0.0)
        edge_row = slice(end - 1, end + SUB - 1)
        du = jnp.where(top & (hue[0:nt, edge_row, :] > kf), MIX * u, 0.0)
        dv = jnp.where(top & (hve[0:nt, edge_row, :] > kf),
                       MIX * v - fv_north * (u + west_in(u, lane)) - pn[k], 0.0)
        row = slice(rows - 1, rows + SUB - 1)
        u_out[k, :, row, :] += du
        v_out[k, :, row, :] += dv
        nu, nv = nu + du, nv + dv

        out = slice(SUB - 1, 2 * SUB - 1)
        u = jnp.where(hue[0:nt, out, :] > kf, ur[k, :, out, :], 0.0)
        v = jnp.where(hve[0:nt, out, :] > kf, vr[k, :, out, :], 0.0)
        edge_row = slice(SUB, 2 * SUB)
        du = jnp.where(top & (hue[0:nt, edge_row, :] > kf),
                       MIX * u + fu_south * (v + east_in(v, lane, 1)), 0.0)
        dv = jnp.where(top & (hve[0:nt, edge_row, :] > kf), MIX * v, 0.0)
        u_out[k, :, 0:SUB, :] += du
        v_out[k, :, 0:SUB, :] += dv
        return nu, nv, su + du, sv + dv

    nu, nv, su, sv = step_loop(0, levels, 2, far_rows, (zero,) * 4)
    for f, north, south in ((3, nu, su), (4, nv, sv)):
        flat[f, :, SUB:2 * SUB, :] += south
        flat[f, :, end - SUB:end, :] += pltpu.roll(north, SUB - 1, 1)

    spot = lax.shift_right_logical(tall, 3)
    group = jnp.zeros((rows, LANES), F32)
    for f in range(FLAT):
        x = jnp.where(tall < LANES // 2, flat[f, 0, own, :], flat[f, nt - 1, own, :])
        group = jnp.where(spot == f, pltpu.roll(x, 8 * f + 4, 1), group)
    strip2[...] = group
    cp = copier(send2, recv2)
    flat_up = [cp(cube_rows(flat, end - NSUB, NSUB), cube_rows(flat, SUB - NSUB, NSUB), lon, nth)]
    flat_down = [cp(cube_rows(flat, SUB, NSUB), cube_rows(flat, end, NSUB), lon, sth)]
    along2, corner_up2, corner_down2 = strips(
        cp, strip2, fe2, fw2, NSUB)
    start_ns(flat_up, flat_down)
    for c in along2:
        c.start()
    start_ns(corner_up2, corner_down2)

    recv_ns(tracer_up, tracer_down)

    def tracer_rows(k, carry):
        kf = k.astype(F32)
        for a in (0, end):
            out = slice(a, a + SUB)
            wet = de[0:nt, out, :] > kf
            tm[k, :, out, :] = jnp.where(wet, tr[k, :, out, :], 0.0)
            sm[k, :, out, :] = jnp.where(wet, sr[k, :, out, :], 0.0)
        vm[k, :, 0:SUB, :] = jnp.where(hve[0:nt, 0:SUB, :] > kf, vr[k, :, 0:SUB, :], 0.0)
        return carry

    step_loop(0, levels, 2, tracer_rows, 0)

    starts = list(range(SUB - 1, end - SUB, SUB)) + [end - SUB]

    def fluxes(k, carry):
        kf = k.astype(F32)
        for r in range(SUB, end, SUB):
            here = slice(r, r + SUB)
            w0, w1, w2, w3 = face_weights(um[k, :, here, :], hue[0:nt, here, :] > kf)
            for ref, to in ((tm, xt), (sm, xs)):
                c = ref[k, :, here, :]
                fx = (w0 * c + w1 * east_in(c, lane, 1)
                      - w2 * east_in(c, lane, 2) + w3 * west_in(c, lane))
                to[k, :, r - SUB:r, :] = fx
        for a in starts:
            here = slice(a, a + SUB)
            w0, w1, w2, w3 = face_weights(vm[k, :, here, :], hve[0:nt, here, :] > kf)
            for ref, to in ((tm, yt), (sm, ys)):
                to[k, :, here, :] = (
                    w0 * ref[k, :, here, :] + w1 * ref[k, :, a + 1:a + SUB + 1, :]
                    - w2 * ref[k, :, a + 2:a + SUB + 2, :] + w3 * ref[k, :, a - 1:a + SUB - 1, :])
        return carry

    step_loop(0, levels, 1, fluxes, 0)
    for c in along_a:
        c.wait_recv()

    q = tall & 3

    def speeds(x, limit):
        x = jnp.where((tall & 7) < 4, x, pltpu.roll(x, 4, 1))
        opening = limit > level
        return face_weights(jnp.where(opening, x, 0.0), opening)

    mine = strip_a[...]
    a = jnp.where(q < 2, mine, fe_a[...])
    b = jnp.where(q < 2, fw_a[...], mine)
    _, w1, w2, w3 = speeds(strip_b[...], jnp.where(
        q == 0, column(hue, nt - 1, LANES - 2), jnp.where(q == 1, column(hue, nt - 1, LAST), column(hue, 0, 0))))
    b_west = pltpu.roll(b, 1, 1)
    flux = jnp.where(q == 1, w1 * pltpu.roll(a, LANES - 1, 1), 0.0) - w2 * pltpu.roll(a, LANES - 2, 1)
    flux = jnp.where(q < 2, flux, jnp.where(q == 2, w3 * b_west, 0.0))
    w0, w1, w2, w3 = speeds(fw_b[own, :], column(hue, nt, LAST))
    first = w0 * b + w1 * pltpu.roll(b, LANES - 1, 1) - w2 * pltpu.roll(b, LANES - 2, 1) + w3 * b_west
    mend[...] = flux - pltpu.roll(jnp.where(q == 1, first, flux), 1, 1)

    def mended(x, m):
        edge_lane = lane_of(m.shape)
        first = x[:1] - jnp.where(edge_lane < 2, m, 0.0)[None]
        last = x[-1:] - jnp.where(edge_lane >= LANES - 2, m, 0.0)[None]
        return jnp.concatenate([first, x[1:-1], last], axis=0)

    span = 2 * SUB if rows % (2 * SUB) == 0 else SUB
    long = lane_of((span, LANES))
    DIFF = TIME_STEP * STABILITY_FACTOR * BACKGROUND_MIX
    BASE = TIME_STEP * (BACKGROUND_MIX + CONVECTIVE_MIX)
    for r in range(0, rows, span):
        out = slice(r, r + span)
        here, below = slice(SUB + r, SUB + r + span), slice(SUB + r - 1, SUB + r + span - 1)

        def star(k):
            fx = xt[k, :, out, :]
            t = tm[k, :, here, :] - (fx - west_in(fx, long)) - (yt[k, :, here, :] - yt[k, :, below, :])
            fx = xs[k, :, out, :]
            s = sm[k, :, here, :] - (fx - west_in(fx, long)) - (ys[k, :, here, :] - ys[k, :, below, :])
            t = mended(t, pltpu.roll(mend[out, :], LANES - 2 - 8 * k, 1))
            s = mended(s, pltpu.roll(mend[out, :], LANES - 6 - 8 * k, 1))
            return t, s, HALINE_COEF * s - THERMAL_COEF * t

        def forward(k, carry):
            t, s, dens, lower, qt, qs = carry
            tn, sn, densn = star(k)
            rise = jnp.maximum(densn - dens, 0.0)
            e = 1.0 + STABILITY_FACTOR * rise
            n = jnp.where(de[0:nt, here, :] > k.astype(F32), BASE + DIFF * rise, 0.0)
            w = 1.0 / (e * lower + n)
            rat = n * w
            ew = e * w
            gt, gs = t + qt, s + qs
            t_out[k - 1, :, out, :] = gt * ew
            s_out[k - 1, :, out, :] = gs * ew
            ratio[k - 1, :, out, :] = rat
            return tn, sn, densn, 1.0 + rat * lower, rat * gt, rat * gs

        zero = jnp.zeros((nt, span, LANES), F32)
        carry = star(0) + (zero + 1.0, zero, zero)
        t, s, _, lower, qt, qs = lax.fori_loop(1, levels, forward, carry)
        w = 1.0 / lower
        t, s = (t + qt) * w, (s + qs) * w
        t_out[levels - 1, :, out, :] = t
        s_out[levels - 1, :, out, :] = s

        def backward(i, carry):
            t, s = carry
            k = levels - 2 - i
            rat = ratio[k, :, out, :]
            t = t_out[k, :, out, :] + rat * t
            s = s_out[k, :, out, :] + rat * s
            t_out[k, :, out, :] = t
            s_out[k, :, out, :] = s
            return t, s

        lax.fori_loop(0, levels - 1, backward, (t, s))

    for c in along0 + along_a + along_b + along_c:
        c.wait_send()
    sent_ns(depth_up + corner_up0 + flow_up + tracer_up + corner_up_b,
            depth_down + corner_down0 + flow_down + tracer_down + corner_down_b + press_down)
    recv_ns(flat_up, flat_down)
    for c in along2:
        c.wait_recv()
    recv_ns(corner_up2, corner_down2)
    wide = slice(SUB - NSUB, end + NSUB)
    count = rows + 2 * NSUB
    halo = jnp.where((lane_of((count, LANES)) & 7) >= 4, fe2[wide, :], fw2[wide, :])
    for f in range(FLAT):
        flat_out[f, 0:nt, 0:count] = flat[f, :, wide, :]
        flat_out[f, nt, 0:count] = pltpu.roll(halo, LANES - 8 * f - 4, 1)
    flat_out[5, :, count:, :] = jnp.zeros((nt + 1, SUB, LANES), F32)

    for c in along2:
        c.wait_send()
    sent_ns(flat_up + corner_up2, flat_down + corner_down2)


def tail(
    t, s, ut, vt, flat,
    t_out, s_out, u_out, v_out, eta_out, tx_out, ty_out,
    eta, bu, bv, hx, hy, un, vn, cor, sem,
):
    levels, nt, rows, _ = t.shape
    count = rows + 2 * NSUB
    lane = lane_of((SUB, LANES))
    copies = []

    def put(src, dst):
        for c in range(nt):
            copies.append(pltpu.make_async_copy(
                src(c), dst(pl.ds(c * LANES, LANES)), sem.at[len(copies)]))
            copies[-1].start()

    put(lambda c: t.at[:, c], lambda d: t_out.at[:, :, d])
    put(lambda c: s.at[:, c], lambda d: s_out.at[:, :, d])

    for ref in (eta, bu, bv):
        ref[:, 0:SUB, :] = jnp.zeros((nt + 1, SUB, LANES), F32)
        ref[:, count + SUB:, :] = jnp.zeros((nt + 1, SUB, LANES), F32)
    tiles = range(0, count, SUB)
    eta[:, SUB:count + SUB, :] = flat[0, :, 0:count, :]
    bu[:, SUB:count + SUB, :] = flat[1, :, 0:count, :]
    bv[:, SUB:count + SUB, :] = flat[2, :, 0:count, :]
    for r in tiles:
        d = flat[5, :, r:r + SUB, :]
        hx[:, r:r + SUB, :] = jnp.minimum(d, east_all(d, lane))
        hy[:, r:r + SUB, :] = jnp.minimum(d, flat[5, :, r + 1:r + SUB + 1, :])
    for sub in range(NSUB):
        for r in tiles:
            here, below = slice(SUB + r, 2 * SUB + r), slice(SUB + r - 1, 2 * SUB + r - 1)
            x = bu[:, here, :]
            eta[:, here, :] = eta[:, here, :] - HEIGHT_FACTOR * (
                x - west_all(x, lane) + (bv[:, here, :] - bv[:, below, :]))
        for r in tiles:
            here, above = slice(SUB + r, 2 * SUB + r), slice(SUB + r + 1, 2 * SUB + r + 1)
            raw = slice(r, r + SUB)
            x = eta[:, here, :]
            bu[:, here, :] = (bu[:, here, :] + (1.0 / NSUB) * flat[3, :, raw, :]
                              - SLOPE_FACTOR * hx[:, raw, :] * (east_all(x, lane) - x))
            bv[:, here, :] = (bv[:, here, :] + (1.0 / NSUB) * flat[4, :, raw, :]
                              - SLOPE_FACTOR * hy[:, raw, :] * (eta[:, above, :] - x))
    mid = pl.ds(SUB + NSUB, rows)
    put(lambda c: eta.at[c, mid, :], lambda d: eta_out.at[:, d])
    put(lambda c: bu.at[c, mid, :], lambda d: tx_out.at[:, d])
    put(lambda c: bv.at[c, mid, :], lambda d: ty_out.at[:, d])

    for r in range(0, rows, SUB):
        raw = slice(NSUB + r, NSUB + r + SUB)
        hu, hv = hx[0:nt, raw, :], hy[0:nt, raw, :]
        done = slice(SUB + NSUB + r, 2 * SUB + NSUB + r)
        out = slice(r, r + SUB)
        cor[0, :, out, :] = (bu[0:nt, done, :] - (flat[3, 0:nt, raw, :] + flat[1, 0:nt, raw, :])) / jnp.maximum(hu, 1.0)
        cor[1, :, out, :] = (bv[0:nt, done, :] - (flat[4, 0:nt, raw, :] + flat[2, 0:nt, raw, :])) / jnp.maximum(hv, 1.0)
        cor[2, :, out, :] = hu
        cor[3, :, out, :] = hv

    @pl.loop(0, levels)
    def _(k):
        kf = k.astype(F32)
        un[k] = jnp.where(cor[2] > kf, ut[k, :, 0:rows, :] + cor[0], 0.0)
        vn[k] = jnp.where(cor[3] > kf, vt[k, :, 0:rows, :] + cor[1], 0.0)

    put(lambda c: un.at[:, c], lambda d: u_out.at[:, :, d])
    put(lambda c: vn.at[:, c], lambda d: v_out.at[:, :, d])
    for c in copies:
        c.wait()


def body(*args):
    levels, rows, cols = args[0].shape
    nt = cols // LANES
    erows = rows + 2 * SUB
    count = rows + 2 * NSUB

    def vmem(*shape):
        return pltpu.VMEM(shape, F32)

    def out(*shape):
        return jax.ShapeDtypeStruct(shape, F32)

    block = pl.BlockSpec(memory_space=pltpu.VMEM)
    far = pl.BlockSpec(memory_space=pltpu.HBM)
    raw = vmem(levels, nt, erows, LANES)
    own = vmem(levels, nt, rows, LANES)
    ints = pltpu.VMEM((nt, rows, LANES), jnp.int32)
    n1, n2 = 2 + 8 + 1 + 6 + 4 + 3, 2 + 6
    cube = (levels, nt, rows, LANES)
    parts = pl.pallas_call(
        functools.partial(kernel, rows * lax.axis_size("lat")),
        out_shape=(out(*cube),) * 2 + (out(levels, nt, rows + SUB, LANES),) * 2 + (out(FLAT, nt + 1, count + SUB, LANES),),
        in_specs=[far] * 9,
        out_specs=(block,) * 5,
        scratch_shapes=(
            [raw] * 11 + [own, own, raw, raw, own]
            + [vmem(nt, rows, LANES)] * 2 + [ints] * 2
            + [vmem(nt + 1, erows + SUB, LANES)] + [vmem(nt + 1, erows, LANES)] * 2
            + [vmem(FLAT, nt, erows, LANES)]
            + [vmem(rows // SUB, SUB, LANES)] * 2
            + [vmem(rows, LANES), vmem(erows, LANES), vmem(erows, LANES)]
            + [vmem(rows, LANES)] * 3
            + [vmem(rows, LANES), vmem(erows, LANES), vmem(erows, LANES)]
            + [vmem(rows, LANES)] * 2
            + [vmem(rows, LANES), vmem(erows, LANES), vmem(erows, LANES), vmem(rows, LANES)]
            + [vmem(erows, LANES), vmem(4, nt, rows, LANES), vmem(levels, nt, SUB, LANES)]
            + [pltpu.SemaphoreType.DMA((9 * nt,))]
            + [pltpu.SemaphoreType.DMA((n1,))] * 2
            + [pltpu.SemaphoreType.DMA((n2,))] * 2
        ),
        compiler_params=pltpu.CompilerParams(
            collective_id=0, has_side_effects=True, vmem_limit_bytes=32 * 1024 * 1024),
    )(*[pltpu.with_memory_space_constraint(a, pltpu.HBM) for a in args])
    cube, plane = (levels, rows, cols), (rows, cols)
    return pl.pallas_call(
        tail,
        out_shape=(pltpu.HBM(cube, F32),) * 4 + (pltpu.HBM(plane, F32),) * 3,
        in_specs=[block] * 5,
        out_specs=(far,) * 7,
        scratch_shapes=(
            [vmem(nt + 1, count + 2 * SUB, LANES)] * 3 + [vmem(nt + 1, count, LANES)] * 2
            + [own, own, vmem(4, nt, rows, LANES)]
            + [pltpu.SemaphoreType.DMA((7 * nt,))]
        ),
        compiler_params=pltpu.CompilerParams(vmem_limit_bytes=32 * 1024 * 1024),
    )(*parts)


def solution(mesh):
    cube, plane = P(None, "lat", "lon"), P("lat", "lon")
    return jax.shard_map(
        body,
        mesh=mesh,
        in_specs=(cube,) * 4 + (plane,) * 5,
        out_specs=(cube,) * 4 + (plane,) * 3,
        check_vma=False,
    )
```

```python
import functools

import jax
import jax.numpy as jnp
from jax import lax
from jax.experimental import pallas as pl
from jax.experimental.pallas import tpu as pltpu
from jax.sharding import PartitionSpec as P

NSUB = 4
TIME_STEP = 0.4
TRACER_DIFF = 0.05
MOMENTUM_DIFF = 0.05
BOTTOM_DRAG = 0.05
WIND_FACTOR = 0.5
CORIOLIS_SCALE = 0.5
LATITUDE_SPAN = 2.6
GRAVITY_FACTOR = 0.3
THERMAL_COEF = 0.2
HALINE_COEF = 0.8
BACKGROUND_MIX = 0.05
CONVECTIVE_MIX = 1.5
STABILITY_FACTOR = 5.0
HEIGHT_FACTOR = 0.2
SLOPE_FACTOR = 0.15

LANES = 128
SUB = 8
FLAT = 6
MESH = pl.DeviceIdType.MESH
F32 = jnp.float32


def lane_of(shape):
    return lax.broadcasted_iota(jnp.int32, shape, len(shape) - 1)


def east(x, lane, s=1):
    r = pltpu.roll(x, LANES - s, 2)
    return jnp.where(lane < LANES - s, r[:-1], r[1:])


def west(x, lane):
    r = pltpu.roll(x, 1, 2)
    return jnp.where(lane >= 1, r[:-1], jnp.concatenate([r[-1:], r[:-2]], axis=0))


def east_all(x, lane, s=1):
    r = pltpu.roll(x, LANES - s, 2)
    return jnp.where(lane < LANES - s, r, jnp.concatenate([r[1:], r[:1]], axis=0))


def west_all(x, lane):
    r = pltpu.roll(x, 1, 2)
    return jnp.where(lane >= 1, r, jnp.concatenate([r[-1:], r[:-1]], axis=0))


def step_loop(first, last, unroll, body, carry):
    n = (last - first) // unroll

    def group(g, c):
        for i in range(unroll):
            c = body(first + g * unroll + i, c)
        return c

    carry = lax.fori_loop(0, n, group, carry)
    for k in range(first + n * unroll, last):
        carry = body(jnp.int32(k), carry)
    return carry


def east_in(x, lane, s):
    r = pltpu.roll(x, LANES - s, 2)
    return jnp.where(lane < LANES - s, r, jnp.concatenate([r[1:], jnp.zeros_like(r[:1])], axis=0))


def west_in(x, lane):
    r = pltpu.roll(x, 1, 2)
    return jnp.where(lane >= 1, r, jnp.concatenate([jnp.zeros_like(r[:1]), r[:-1]], axis=0))


def face_weights(speed, opening):
    p = speed * (TIME_STEP / 12.0)
    q = jnp.abs(p)
    m = 3.0 * q - jnp.where(opening, TIME_STEP * TRACER_DIFF, 0.0)
    p7 = 7.0 * p
    return p7 - m, p7 + m, p + q, q - p


def kernel(
    lat_total,
    t_in, s_in, u_in, v_in, eta_in, zt_in, mt_in, wi_in, bi_in,
    t_out, s_out, u_out, v_out, flat_out,
    tr, sr, ur, vr, tm, sm, um, vm, pm, wu, ev, xt, xs, yt, ys, ratio,
    zt, mt, wi, bi, de, hue, hve, flat, fu_ref, fv_ref,
    strip0, fe0, fw0, strip_a, fe_a, fw_a, strip_b, fe_b, fw_b, strip_c, fe_c,
    strip2, fe2, fw2, mend, edge_b, acc, pn,
    load_sem, send1, recv1, send2, recv2,
):
    levels, nt, rows, _ = t_out.shape
    end = SUB + rows
    zero = jnp.zeros((nt, SUB, LANES), F32)
    nr = rows // SUB
    lon, lat = lax.axis_index("lon"), lax.axis_index("lat")
    nlon, nlat = lax.axis_size("lon"), lax.axis_size("lat")
    wst, est = lax.rem(lon + nlon - 1, nlon), lax.rem(lon + 1, nlon)
    nth, sth = lax.rem(lat + 1, nlat), lax.rem(lat + nlat - 1, nlat)
    has_n, has_s = lat < nlat - 1, lat > 0
    own = pl.ds(SUB, rows)

    barrier = pltpu.get_barrier_semaphore()

    def greet(lo, la):
        pl.semaphore_signal(barrier, inc=1, device_id=(lo, la), device_id_type=MESH)

    greet(wst, lat)
    greet(est, lat)

    @pl.when(has_n)
    def _():
        greet(wst, nth)
        greet(lon, nth)
        greet(est, nth)

    @pl.when(has_s)
    def _():
        greet(wst, sth)
        greet(lon, sth)
        greet(est, sth)

    loads = []

    def load(src, dst):
        group = []
        for c in range(nt):
            cols = pl.ds(c * LANES, LANES)
            group.append(pltpu.make_async_copy(
                src(cols), dst(c), load_sem.at[len(loads) * nt + c]))
            group[-1].start()
        loads.append(group)
        return group

    ld_wi = load(lambda s: wi_in.at[:, s], lambda c: wi.at[c])
    ld_bi = load(lambda s: bi_in.at[:, s], lambda c: bi.at[c])
    ld_u = load(lambda s: u_in.at[:, :, s], lambda c: ur.at[:, c, own, :])
    ld_v = load(lambda s: v_in.at[:, :, s], lambda c: vr.at[:, c, own, :])
    ld_t = load(lambda s: t_in.at[:, :, s], lambda c: tr.at[:, c, own, :])
    ld_s = load(lambda s: s_in.at[:, :, s], lambda c: sr.at[:, c, own, :])
    ld_e = load(lambda s: eta_in.at[:, s], lambda c: flat.at[0, c, own, :])
    ld_z = load(lambda s: zt_in.at[:, s], lambda c: zt.at[c])
    ld_m = load(lambda s: mt_in.at[:, s], lambda c: mt.at[c])

    def arrived(*groups):
        for g in groups:
            for c in g:
                c.wait()

    def clear(first):
        beyond = slice(first, first + SUB)
        de[:, beyond, :] = jnp.zeros((nt + 1, SUB, LANES), F32)
        for ref in (fe0, fw0, fe_b, fw_b, fe2, fw2):
            ref[beyond, :] = jnp.zeros((SUB, LANES), F32)
        for f in range(FLAT):
            flat[f, :, beyond, :] = jnp.zeros((nt, SUB, LANES), F32)

    @pl.when(jnp.logical_not(has_s))
    def _():
        clear(0)

    @pl.when(jnp.logical_not(has_n))
    def _():
        clear(end)

    def copier(send, recv):
        made = []

        def cp(src, dst, lo, la):
            n = len(made)
            made.append(pltpu.make_async_remote_copy(
                src_ref=src, dst_ref=dst, send_sem=send.at[n], recv_sem=recv.at[n],
                device_id=(lo, la), device_id_type=MESH))
            return made[-1]

        return cp

    def start_ns(up, down):
        @pl.when(has_n)
        def _():
            for c in up:
                c.start()

        @pl.when(has_s)
        def _():
            for c in down:
                c.start()

    def recv_ns(up, down):
        @pl.when(has_s)
        def _():
            for c in up:
                c.wait_recv()

        @pl.when(has_n)
        def _():
            for c in down:
                c.wait_recv()

    def sent_ns(up, down):
        @pl.when(has_n)
        def _():
            for c in up:
                c.wait_send()

        @pl.when(has_s)
        def _():
            for c in down:
                c.wait_send()

    cp = copier(send1, recv1)

    def rows_up(ref, n, at):
        return cp(at(ref, end - n, n), at(ref, SUB - n, n), lon, nth)

    def rows_down(ref, n, at):
        return cp(at(ref, SUB, n), at(ref, end, n), lon, sth)

    def cube_rows(ref, first, n):
        return ref.at[:, 0:nt, pl.ds(first, n), :]

    def plane_rows(ref, first, n):
        return ref.at[0:nt, pl.ds(first, n), :]

    depth_up, depth_down = [rows_up(de, 2, plane_rows)], [rows_down(de, 2, plane_rows)]
    flow_up = [rows_up(r, 1, cube_rows) for r in (ur, vr)]
    flow_down = [rows_down(r, 1, cube_rows) for r in (ur, vr)]
    tracer_up = [rows_up(r, 2, cube_rows) for r in (tr, sr)]
    tracer_down = [rows_down(r, 2, cube_rows) for r in (tr, sr)]
    press_down = [cp(cube_rows(pm, SUB, 1), cube_rows(pn, 0, 1), lon, sth)]

    def strips(cp, strip, fe, fw, n):
        def at(ref, first, size):
            return ref.at[pl.ds(first, size), :]

        along = [cp(at(strip, 0, rows), at(fe, SUB, rows), wst, lat),
                 cp(at(strip, 0, rows), at(fw, SUB, rows), est, lat)]
        up = [cp(at(strip, rows - n, n), at(fe, SUB - n, n), wst, nth),
              cp(at(strip, rows - n, n), at(fw, SUB - n, n), est, nth)]
        down = [cp(at(strip, 0, n), at(fe, end, n), wst, sth),
                cp(at(strip, 0, n), at(fw, end, n), est, sth)]
        return along, up, down

    along0, corner_up0, corner_down0 = strips(
        cp, strip0, fe0, fw0, 2)
    along_b = [cp(strip_b, fe_b.at[own, :], wst, lat), cp(strip_b, fw_b.at[own, :], est, lat)]
    corner_up_b = [cp(strip_b.at[pl.ds(rows - 1, 1), :], fe_b.at[pl.ds(SUB - 1, 1), :], wst, nth)]
    corner_down_b = [cp(strip_b.at[pl.ds(0, 1), :], fw_b.at[pl.ds(end, 1), :], est, sth)]
    along_a = [cp(strip_a, fe_a, wst, lat), cp(strip_a, fw_a, est, lat)]
    along_c = [cp(strip_c, fe_c, wst, lat)]

    lane = lane_of((SUB, LANES))
    tall = lane_of((rows, LANES))

    for k in range(levels):
        for ref in (um, vm):
            ref[k, :, 0:SUB, :] = zero
            ref[k, :, end:, :] = zero
        pm[k, :, end:, :] = zero
        wu[k, :, end:, :] = zero
        ev[k, :, 0:SUB, :] = zero
    acc[...] = jnp.zeros_like(acc)

    sub = lax.broadcasted_iota(jnp.int32, (SUB, LANES), 0)
    j = (lat * rows + sub + SUB * lax.rem(lane, nr)).astype(F32)
    j = j + jnp.where(lane < LANES // 2, 0.5, 1.0)
    f = CORIOLIS_SCALE * jnp.sin(LATITUDE_SPAN * (j / lat_total - 0.5)) * (0.25 * TIME_STEP)
    for r in range(nr):
        fu_ref[r] = jnp.broadcast_to(f[:, r:r + 1], (SUB, LANES))
        at = LANES // 2 - (LANES // 2) % nr + nr + r
        fv_ref[r] = jnp.broadcast_to(f[:, at:at + 1], (SUB, LANES))
    fu_south = jnp.broadcast_to(f[0:1, 0:1], (SUB, LANES))
    fv_north = jnp.broadcast_to(f[SUB - 1:SUB, at:at + 1], (SUB, LANES))

    def edge(first, last, p):
        return pltpu.roll(jnp.where(tall < LANES // 2, first, last), 4 * p + 2, 1)

    arrived(ld_wi, ld_bi)
    depth = (wi[...] * bi[...]).astype(F32)
    de[0:nt, own, :] = depth
    strip0[...] = edge(depth[0], depth[nt - 1], 0)
    pl.semaphore_wait(barrier, 2 + 3 * has_n.astype(jnp.int32) + 3 * has_s.astype(jnp.int32))
    for c in along0:
        c.start()
    start_ns(depth_up + corner_up0, depth_down + corner_down0)
    for n, group in enumerate((ld_u, ld_v)):
        arrived(group)
        start_ns(flow_up[n:n + 1], flow_down[n:n + 1])

    place = lax.shift_right_logical(tall, 2)
    group = jnp.zeros((rows, LANES), F32)
    for k in range(levels):
        for n, ref in enumerate((ur, vr)):
            group = jnp.where(place == 2 * k + n, edge(ref[k, 0, own, :], ref[k, nt - 1, own, :], 2 * k + n), group)
    strip_b[...] = group
    for c in along_b:
        c.start()
    start_ns(corner_up_b, corner_down_b)

    HALF = 0.5 * GRAVITY_FACTOR * TIME_STEP
    arrived(ld_t, ld_s)
    group = jnp.zeros((rows, LANES), F32)
    total = jnp.zeros((nt, rows, LANES), F32)
    for k in range(levels):
        wet = de[0:nt, own, :] > k
        t = jnp.where(wet, tr[k, :, own, :], 0.0)
        s = jnp.where(wet, sr[k, :, own, :], 0.0)
        tm[k, :, own, :] = t
        sm[k, :, own, :] = s
        h = (HALF * HALINE_COEF) * s - (HALF * THERMAL_COEF) * t
        p = total + h
        total = p + h
        pm[k, :, own, :] = p
        group = jnp.where(tall == 8 * k + 1, pltpu.roll(p[0], 8 * k + 1, 1), group)
    strip_c[...] = group
    start_ns([], press_down)
    for c in along_c:
        c.start()
    start_ns(tracer_up, tracer_down)
    group = jnp.zeros((rows, LANES), F32)
    for k in range(levels):
        for n, ref in enumerate((tm, sm)):
            group = jnp.where(place == 2 * k + n, edge(ref[k, 0, own, :], ref[k, nt - 1, own, :], 2 * k + n), group)
    strip_a[...] = group
    for c in along_a:
        c.start()
    arrived(ld_e, ld_z, ld_m)
    flat[5, :, own, :] = depth

    def faces(first, last):
        for r in range(first, last, SUB):
            d = de[:, r:r + SUB, :]
            hue[:, r:r + SUB, :] = jnp.minimum(d, east_all(d, lane))
            hve[:, r:r + SUB, :] = jnp.minimum(d, de[:, r + 1:r + SUB + 1, :])

    for r in range(SUB, end, SUB):
        d = de[0:nt, r:r + SUB, :]
        hue[0:nt, r:r + SUB, :] = jnp.minimum(d, east_in(d, lane, 1))

    def east_fluxes(k, carry):
        kf = k.astype(F32)
        for r in range(SUB, end, SUB):
            here = slice(r, r + SUB)
            opening = hue[0:nt, here, :] > kf
            w0, w1, w2, w3 = face_weights(jnp.where(opening, ur[k, :, here, :], 0.0), opening)
            for ref, to in ((tm, xt), (sm, xs)):
                c = ref[k, :, here, :]
                to[k, :, r - SUB:r, :] = (w0 * c + w1 * east_in(c, lane, 1)
                                          - w2 * east_in(c, lane, 2) + w3 * west_in(c, lane))
        return carry

    step_loop(0, levels, 1, east_fluxes, 0)

    for c in along0:
        c.wait_recv()
    recv_ns(depth_up, depth_down)
    de[nt, own, :] = pltpu.roll(jnp.where((tall & 3) >= 2, fe0[own, :], fw0[own, :]), LANES - 2, 1)
    faces(SUB, end)

    MIX = TIME_STEP * MOMENTUM_DIFF
    KEEP = 1.0 - TIME_STEP * BOTTOM_DRAG - 4.0 * MIX

    def momentum(k, carry):
        kf = k.astype(F32)
        for at in range(SUB, end, SUB):
            here = slice(at, at + SUB)
            u = jnp.where(hue[0:nt, here, :] > kf, ur[k, :, here, :], 0.0)
            v = jnp.where(hve[0:nt, here, :] > kf, vr[k, :, here, :], 0.0)
            um[k, :, here, :] = u
            vm[k, :, here, :] = v
            wu[k, :, here, :] = west_in(u, lane)
            ev[k, :, here, :] = east_in(v, lane, 1)
        for r in range(nr):
            at = SUB + SUB * r
            here, above, below = slice(at, at + SUB), slice(at + 1, at + SUB + 1), slice(at - 1, at + SUB - 1)
            out = slice(SUB * r, SUB * r + SUB)
            u, un, w = um[k, :, here, :], um[k, :, above, :], wu[k, :, here, :]
            v, vs, e = vm[k, :, here, :], vm[k, :, below, :], ev[k, :, here, :]
            p = pm[k, :, here, :]
            around_u = (east_in(u, lane, 1) + w) + (un + um[k, :, below, :])
            around_v = (west_in(v, lane) + e) + (vs + vm[k, :, above, :])
            vbar = (v + vs) + (e + ev[k, :, below, :])
            ubar = (u + un) + (w + wu[k, :, above, :])
            ut = KEEP * u + MIX * around_u + fu_ref[r] * vbar - (east_in(p, lane, 1) - p)
            vt = KEEP * v + MIX * around_v - fv_ref[r] * ubar - (pm[k, :, above, :] - p)
            ut = jnp.where(hue[0:nt, here, :] > kf, ut, 0.0)
            vt = jnp.where(hve[0:nt, here, :] > kf, vt, 0.0)
            u_out[k, :, out, :] = ut
            v_out[k, :, out, :] = vt
            for n, x in enumerate((u, v, ut, vt)):
                acc[n, :, out, :] += x
        return carry

    step_loop(0, levels, 2, momentum, 0)
    wind_u = jnp.where(hue[0:nt, own, :] > 0.0, (TIME_STEP * WIND_FACTOR) * zt[...], 0.0)
    wind_v = jnp.where(hve[0:nt, own, :] > 0.0, (TIME_STEP * WIND_FACTOR) * mt[...], 0.0)
    u_out[0, :, 0:rows, :] += wind_u
    v_out[0, :, 0:rows, :] += wind_v
    flat[1, :, own, :] = acc[0]
    flat[2, :, own, :] = acc[1]
    flat[3, :, own, :] = acc[2] - acc[0] + wind_u
    flat[4, :, own, :] = acc[3] - acc[1] + wind_v

    recv_ns(corner_up0, corner_down0)
    for out in (slice(0, SUB), slice(end, end + SUB)):
        de[nt, out, :] = pltpu.roll(jnp.where((lane & 3) >= 2, fe0[out, :], fw0[out, :]), LANES - 2, 1)
    faces(0, SUB)
    faces(end - SUB, end + SUB)
    for c in along_b + along_c:
        c.wait_recv()
    recv_ns(corner_up_b, corner_down_b)
    level = lax.shift_right_logical(tall, 3).astype(F32)

    def by_lane(at, one, two, five, six):
        return jnp.where(at == 1, one, jnp.where(at == 2, two, jnp.where(at == 5, five, six)))

    def column(ref, c, at, which=own, n=rows):
        return jnp.broadcast_to(ref[c, which, at:at + 1], (n, LANES))

    LAST = LANES - 1
    for r in range(0, end + SUB, SUB):
        here = slice(r, r + SUB)
        limit = by_lane(lane & 7, *(column(ref, nt, at, here, SUB) for ref in (hue, hve) for at in (LAST, 0)))
        x = jnp.where((lane & 3) >= 2, fe_b[here, :], fw_b[here, :])
        edge_b[here, :] = jnp.where(limit > lax.shift_right_logical(lane, 3).astype(F32), x, 0.0)
    x = edge_b[own, :]
    spot = tall & 7
    near = jnp.where((spot & 1) == 1, pltpu.roll(x, LAST, 1), pltpu.roll(x, 1, 1))
    above, below = slice(SUB + 1, end + 1), slice(SUB - 1, end - 1)
    turn_u = fu_ref[...].reshape(rows, LANES) * pltpu.roll(x + edge_b[below, :], LANES - 5, 1) - fe_c[...]
    turn_v = fv_ref[...].reshape(rows, LANES) * pltpu.roll(x + edge_b[above, :], 5, 1)
    extra = MIX * near + jnp.where(spot == 1, turn_u, 0.0) - jnp.where(spot == 6, turn_v, 0.0)
    limit = by_lane(spot, column(hue, nt - 1, LAST), column(hue, 0, 0), column(hve, nt - 1, LAST), column(hve, 0, 0))
    extra = jnp.where(limit > level, extra, 0.0)
    total = jnp.zeros((rows, LANES), F32)
    for k in range(levels):
        total = total + (pltpu.roll(extra, LANES - 8 * k, 1) if k else extra)
    total_u, total_v = pltpu.roll(total, LANES - 2, 1), pltpu.roll(total, LANES - 6, 1)
    for f, d in ((3, total_u), (4, total_v)):
        flat[f, 0, own, :] += jnp.where(tall == 0, d, 0.0)
        flat[f, nt - 1, own, :] += jnp.where(tall == LAST, d, 0.0)

    recv_ns(flow_up, flow_down)
    recv_ns([], press_down)
    top = lax.broadcasted_iota(jnp.int32, (SUB, LANES), 0) == 0

    def far_rows(k, carry):
        nu, nv, su, sv = carry
        kf = k.astype(F32)
        out = slice(end, end + SUB)
        u = jnp.where(hue[0:nt, out, :] > kf, ur[k, :, out, :], 0.0)
        v = jnp.where(hve[0:nt, out, :] > kf, vr[k, :, out, :], 0.0)
        edge_row = slice(end - 1, end + SUB - 1)
        du = jnp.where(top & (hue[0:nt, edge_row, :] > kf), MIX * u, 0.0)
        dv = jnp.where(top & (hve[0:nt, edge_row, :] > kf),
                       MIX * v - fv_north * (u + west_in(u, lane)) - pn[k], 0.0)
        row = slice(rows - 1, rows + SUB - 1)
        u_out[k, :, row, :] += du
        v_out[k, :, row, :] += dv
        nu, nv = nu + du, nv + dv

        out = slice(SUB - 1, 2 * SUB - 1)
        u = jnp.where(hue[0:nt, out, :] > kf, ur[k, :, out, :], 0.0)
        v = jnp.where(hve[0:nt, out, :] > kf, vr[k, :, out, :], 0.0)
        edge_row = slice(SUB, 2 * SUB)
        du = jnp.where(top & (hue[0:nt, edge_row, :] > kf),
                       MIX * u + fu_south * (v + east_in(v, lane, 1)), 0.0)
        dv = jnp.where(top & (hve[0:nt, edge_row, :] > kf), MIX * v, 0.0)
        u_out[k, :, 0:SUB, :] += du
        v_out[k, :, 0:SUB, :] += dv
        return nu, nv, su + du, sv + dv

    nu, nv, su, sv = step_loop(0, levels, 2, far_rows, (zero,) * 4)
    for f, north, south in ((3, nu, su), (4, nv, sv)):
        flat[f, :, SUB:2 * SUB, :] += south
        flat[f, :, end - SUB:end, :] += pltpu.roll(north, SUB - 1, 1)

    spot = lax.shift_right_logical(tall, 3)
    group = jnp.zeros((rows, LANES), F32)
    for f in range(FLAT):
        x = jnp.where(tall < LANES // 2, flat[f, 0, own, :], flat[f, nt - 1, own, :])
        group = jnp.where(spot == f, pltpu.roll(x, 8 * f + 4, 1), group)
    strip2[...] = group
    cp = copier(send2, recv2)
    flat_up = [cp(cube_rows(flat, end - NSUB, NSUB), cube_rows(flat, SUB - NSUB, NSUB), lon, nth)]
    flat_down = [cp(cube_rows(flat, SUB, NSUB), cube_rows(flat, end, NSUB), lon, sth)]
    along2, corner_up2, corner_down2 = strips(
        cp, strip2, fe2, fw2, NSUB)
    start_ns(flat_up, flat_down)
    for c in along2:
        c.start()
    start_ns(corner_up2, corner_down2)

    for k in range(levels):
        du = pltpu.roll(extra, LANES - 2 - 8 * k, 1)
        dv = pltpu.roll(extra, LANES - 6 - 8 * k, 1)
        for ref, d in ((u_out, du), (v_out, dv)):
            ref[k, 0, 0:rows, :] += jnp.where(tall == 0, d, 0.0)
            ref[k, nt - 1, 0:rows, :] += jnp.where(tall == LAST, d, 0.0)

    recv_ns(tracer_up, tracer_down)

    def tracer_rows(k, carry):
        kf = k.astype(F32)
        for a in (0, end):
            out = slice(a, a + SUB)
            wet = de[0:nt, out, :] > kf
            tm[k, :, out, :] = jnp.where(wet, tr[k, :, out, :], 0.0)
            sm[k, :, out, :] = jnp.where(wet, sr[k, :, out, :], 0.0)
        vm[k, :, 0:SUB, :] = jnp.where(hve[0:nt, 0:SUB, :] > kf, vr[k, :, 0:SUB, :], 0.0)
        return carry

    step_loop(0, levels, 2, tracer_rows, 0)

    starts = list(range(SUB - 1, end - SUB, SUB)) + [end - SUB]

    def north_fluxes(k, carry):
        kf = k.astype(F32)
        for a in starts:
            here = slice(a, a + SUB)
            w0, w1, w2, w3 = face_weights(vm[k, :, here, :], hve[0:nt, here, :] > kf)
            for ref, to in ((tm, yt), (sm, ys)):
                to[k, :, here, :] = (
                    w0 * ref[k, :, here, :] + w1 * ref[k, :, a + 1:a + SUB + 1, :]
                    - w2 * ref[k, :, a + 2:a + SUB + 2, :] + w3 * ref[k, :, a - 1:a + SUB - 1, :])
        return carry

    step_loop(0, levels, 1, north_fluxes, 0)
    for c in along_a:
        c.wait_recv()

    q = tall & 3

    def speeds(x, limit):
        x = jnp.where((tall & 7) < 4, x, pltpu.roll(x, 4, 1))
        opening = limit > level
        return face_weights(jnp.where(opening, x, 0.0), opening)

    mine = strip_a[...]
    a = jnp.where(q < 2, mine, fe_a[...])
    b = jnp.where(q < 2, fw_a[...], mine)
    w0, w1, w2, w3 = speeds(strip_b[...], jnp.where(
        q == 0, column(hue, nt - 1, LANES - 2), jnp.where(q == 1, column(hue, nt - 1, LAST), column(hue, 0, 0))))
    b_west = pltpu.roll(b, 1, 1)
    flux = (jnp.where(q == 1, w0 * a + w1 * pltpu.roll(a, LANES - 1, 1) + w3 * pltpu.roll(a, 1, 1), 0.0)
            - w2 * pltpu.roll(a, LANES - 2, 1))
    flux = jnp.where(q < 2, flux, jnp.where(q == 2, w3 * b_west, 0.0))
    w0, w1, w2, w3 = speeds(fw_b[own, :], column(hue, nt, LAST))
    first = w0 * b + w1 * pltpu.roll(b, LANES - 1, 1) - w2 * pltpu.roll(b, LANES - 2, 1) + w3 * b_west
    mend[...] = flux - pltpu.roll(jnp.where(q == 1, first, flux), 1, 1)

    def mended(x, m):
        edge_lane = lane_of(m.shape)
        first = x[:1] - jnp.where(edge_lane < 2, m, 0.0)[None]
        last = x[-1:] - jnp.where(edge_lane >= LANES - 2, m, 0.0)[None]
        return jnp.concatenate([first, x[1:-1], last], axis=0)

    span = 2 * SUB if rows % (2 * SUB) == 0 else SUB
    long = lane_of((span, LANES))
    DIFF = TIME_STEP * STABILITY_FACTOR * BACKGROUND_MIX
    BASE = TIME_STEP * (BACKGROUND_MIX + CONVECTIVE_MIX)
    for r in range(0, rows, span):
        out = slice(r, r + span)
        here, below = slice(SUB + r, SUB + r + span), slice(SUB + r - 1, SUB + r + span - 1)

        def star(k):
            fx = xt[k, :, out, :]
            t = tm[k, :, here, :] - (fx - west_in(fx, long)) - (yt[k, :, here, :] - yt[k, :, below, :])
            fx = xs[k, :, out, :]
            s = sm[k, :, here, :] - (fx - west_in(fx, long)) - (ys[k, :, here, :] - ys[k, :, below, :])
            t = mended(t, pltpu.roll(mend[out, :], LANES - 2 - 8 * k, 1))
            s = mended(s, pltpu.roll(mend[out, :], LANES - 6 - 8 * k, 1))
            return t, s, HALINE_COEF * s - THERMAL_COEF * t

        def forward(k, carry):
            t, s, dens, lower, qt, qs = carry
            tn, sn, densn = star(k)
            rise = jnp.maximum(densn - dens, 0.0)
            e = 1.0 + STABILITY_FACTOR * rise
            n = jnp.where(de[0:nt, here, :] > k.astype(F32), BASE + DIFF * rise, 0.0)
            w = 1.0 / (e * lower + n)
            rat = n * w
            ew = e * w
            gt, gs = t + qt, s + qs
            t_out[k - 1, :, out, :] = gt * ew
            s_out[k - 1, :, out, :] = gs * ew
            ratio[k - 1, :, out, :] = rat
            return tn, sn, densn, 1.0 + rat * lower, rat * gt, rat * gs

        zero = jnp.zeros((nt, span, LANES), F32)
        carry = star(0) + (zero + 1.0, zero, zero)
        t, s, _, lower, qt, qs = lax.fori_loop(1, levels, forward, carry)
        w = 1.0 / lower
        t, s = (t + qt) * w, (s + qs) * w
        t_out[levels - 1, :, out, :] = t
        s_out[levels - 1, :, out, :] = s

        def backward(i, carry):
            t, s = carry
            k = levels - 2 - i
            rat = ratio[k, :, out, :]
            t = t_out[k, :, out, :] + rat * t
            s = s_out[k, :, out, :] + rat * s
            t_out[k, :, out, :] = t
            s_out[k, :, out, :] = s
            return t, s

        lax.fori_loop(0, levels - 1, backward, (t, s))

    for c in along0 + along_a + along_b + along_c:
        c.wait_send()
    sent_ns(depth_up + corner_up0 + flow_up + tracer_up + corner_up_b,
            depth_down + corner_down0 + flow_down + tracer_down + corner_down_b + press_down)
    recv_ns(flat_up, flat_down)
    for c in along2:
        c.wait_recv()
    recv_ns(corner_up2, corner_down2)
    wide = slice(SUB - NSUB, end + NSUB)
    count = rows + 2 * NSUB
    halo = jnp.where((lane_of((count, LANES)) & 7) >= 4, fe2[wide, :], fw2[wide, :])
    for f in range(FLAT):
        flat_out[f, 0:nt, 0:count] = flat[f, :, wide, :]
        flat_out[f, nt, 0:count] = pltpu.roll(halo, LANES - 8 * f - 4, 1)
    flat_out[5, :, count:, :] = jnp.zeros((nt + 1, SUB, LANES), F32)

    for c in along2:
        c.wait_send()
    sent_ns(flat_up + corner_up2, flat_down + corner_down2)


def tail(
    t, s, ut, vt, flat,
    t_out, s_out, u_out, v_out, eta_out, tx_out, ty_out,
    eta, bu, bv, hx, hy, un, vn, cor, sem,
):
    levels, nt, rows, _ = t.shape
    count = rows + 2 * NSUB
    lane = lane_of((SUB, LANES))
    copies = []

    def put(src, dst):
        for c in range(nt):
            copies.append(pltpu.make_async_copy(
                src(c), dst(pl.ds(c * LANES, LANES)), sem.at[len(copies)]))
            copies[-1].start()

    put(lambda c: t.at[:, c], lambda d: t_out.at[:, :, d])
    put(lambda c: s.at[:, c], lambda d: s_out.at[:, :, d])

    for ref in (eta, bu, bv):
        ref[:, 0:SUB, :] = jnp.zeros((nt + 1, SUB, LANES), F32)
        ref[:, count + SUB:, :] = jnp.zeros((nt + 1, SUB, LANES), F32)
    tiles = range(0, count, SUB)
    eta[:, SUB:count + SUB, :] = flat[0, :, 0:count, :]
    bu[:, SUB:count + SUB, :] = flat[1, :, 0:count, :]
    bv[:, SUB:count + SUB, :] = flat[2, :, 0:count, :]
    for r in tiles:
        d = flat[5, :, r:r + SUB, :]
        hx[:, r:r + SUB, :] = jnp.minimum(d, east_all(d, lane))
        hy[:, r:r + SUB, :] = jnp.minimum(d, flat[5, :, r + 1:r + SUB + 1, :])
    for sub in range(NSUB):
        for r in tiles:
            here, below = slice(SUB + r, 2 * SUB + r), slice(SUB + r - 1, 2 * SUB + r - 1)
            x = bu[:, here, :]
            eta[:, here, :] = eta[:, here, :] - HEIGHT_FACTOR * (
                x - west_all(x, lane) + (bv[:, here, :] - bv[:, below, :]))
        for r in tiles:
            here, above = slice(SUB + r, 2 * SUB + r), slice(SUB + r + 1, 2 * SUB + r + 1)
            raw = slice(r, r + SUB)
            x = eta[:, here, :]
            bu[:, here, :] = (bu[:, here, :] + (1.0 / NSUB) * flat[3, :, raw, :]
                              - SLOPE_FACTOR * hx[:, raw, :] * (east_all(x, lane) - x))
            bv[:, here, :] = (bv[:, here, :] + (1.0 / NSUB) * flat[4, :, raw, :]
                              - SLOPE_FACTOR * hy[:, raw, :] * (eta[:, above, :] - x))
    mid = pl.ds(SUB + NSUB, rows)
    put(lambda c: eta.at[c, mid, :], lambda d: eta_out.at[:, d])
    put(lambda c: bu.at[c, mid, :], lambda d: tx_out.at[:, d])
    put(lambda c: bv.at[c, mid, :], lambda d: ty_out.at[:, d])

    for r in range(0, rows, SUB):
        raw = slice(NSUB + r, NSUB + r + SUB)
        hu, hv = hx[0:nt, raw, :], hy[0:nt, raw, :]
        done = slice(SUB + NSUB + r, 2 * SUB + NSUB + r)
        out = slice(r, r + SUB)
        cor[0, :, out, :] = (bu[0:nt, done, :] - (flat[3, 0:nt, raw, :] + flat[1, 0:nt, raw, :])) / jnp.maximum(hu, 1.0)
        cor[1, :, out, :] = (bv[0:nt, done, :] - (flat[4, 0:nt, raw, :] + flat[2, 0:nt, raw, :])) / jnp.maximum(hv, 1.0)
        cor[2, :, out, :] = hu
        cor[3, :, out, :] = hv

    @pl.loop(0, levels)
    def _(k):
        kf = k.astype(F32)
        un[k] = jnp.where(cor[2] > kf, ut[k, :, 0:rows, :] + cor[0], 0.0)
        vn[k] = jnp.where(cor[3] > kf, vt[k, :, 0:rows, :] + cor[1], 0.0)

    put(lambda c: un.at[:, c], lambda d: u_out.at[:, :, d])
    put(lambda c: vn.at[:, c], lambda d: v_out.at[:, :, d])
    for c in copies:
        c.wait()


def body(*args):
    levels, rows, cols = args[0].shape
    nt = cols // LANES
    erows = rows + 2 * SUB
    count = rows + 2 * NSUB

    def vmem(*shape):
        return pltpu.VMEM(shape, F32)

    def out(*shape):
        return jax.ShapeDtypeStruct(shape, F32)

    block = pl.BlockSpec(memory_space=pltpu.VMEM)
    far = pl.BlockSpec(memory_space=pltpu.HBM)
    raw = vmem(levels, nt, erows, LANES)
    own = vmem(levels, nt, rows, LANES)
    ints = pltpu.VMEM((nt, rows, LANES), jnp.int32)
    n1, n2 = 2 + 8 + 1 + 6 + 4 + 3, 2 + 6
    cube = (levels, nt, rows, LANES)
    parts = pl.pallas_call(
        functools.partial(kernel, rows * lax.axis_size("lat")),
        out_shape=(out(*cube),) * 2 + (out(levels, nt, rows + SUB, LANES),) * 2 + (out(FLAT, nt + 1, count + SUB, LANES),),
        in_specs=[far] * 9,
        out_specs=(block,) * 5,
        scratch_shapes=(
            [raw] * 11 + [own, own, raw, raw, own]
            + [vmem(nt, rows, LANES)] * 2 + [ints] * 2
            + [vmem(nt + 1, erows + SUB, LANES)] + [vmem(nt + 1, erows, LANES)] * 2
            + [vmem(FLAT, nt, erows, LANES)]
            + [vmem(rows // SUB, SUB, LANES)] * 2
            + [vmem(rows, LANES), vmem(erows, LANES), vmem(erows, LANES)]
            + [vmem(rows, LANES)] * 3
            + [vmem(rows, LANES), vmem(erows, LANES), vmem(erows, LANES)]
            + [vmem(rows, LANES)] * 2
            + [vmem(rows, LANES), vmem(erows, LANES), vmem(erows, LANES), vmem(rows, LANES)]
            + [vmem(erows, LANES), vmem(4, nt, rows, LANES), vmem(levels, nt, SUB, LANES)]
            + [pltpu.SemaphoreType.DMA((9 * nt,))]
            + [pltpu.SemaphoreType.DMA((n1,))] * 2
            + [pltpu.SemaphoreType.DMA((n2,))] * 2
        ),
        compiler_params=pltpu.CompilerParams(
            collective_id=0, has_side_effects=True, vmem_limit_bytes=32 * 1024 * 1024),
    )(*[pltpu.with_memory_space_constraint(a, pltpu.HBM) for a in args])
    cube, plane = (levels, rows, cols), (rows, cols)
    return pl.pallas_call(
        tail,
        out_shape=(pltpu.HBM(cube, F32),) * 4 + (pltpu.HBM(plane, F32),) * 3,
        in_specs=[block] * 5,
        out_specs=(far,) * 7,
        scratch_shapes=(
            [vmem(nt + 1, count + 2 * SUB, LANES)] * 3 + [vmem(nt + 1, count, LANES)] * 2
            + [own, own, vmem(4, nt, rows, LANES)]
            + [pltpu.SemaphoreType.DMA((7 * nt,))]
        ),
        compiler_params=pltpu.CompilerParams(vmem_limit_bytes=32 * 1024 * 1024),
    )(*parts)


def solution(mesh):
    cube, plane = P(None, "lat", "lon"), P("lat", "lon")
    return jax.shard_map(
        body,
        mesh=mesh,
        in_specs=(cube,) * 4 + (plane,) * 5,
        out_specs=(cube,) * 4 + (plane,) * 3,
        check_vma=False,
    )
```

```python
import functools

import jax
import jax.numpy as jnp
from jax import lax
from jax.experimental import pallas as pl
from jax.experimental.pallas import tpu as pltpu
from jax.sharding import PartitionSpec as P

NSUB = 4
TIME_STEP = 0.4
TRACER_DIFF = 0.05
MOMENTUM_DIFF = 0.05
BOTTOM_DRAG = 0.05
WIND_FACTOR = 0.5
CORIOLIS_SCALE = 0.5
LATITUDE_SPAN = 2.6
GRAVITY_FACTOR = 0.3
THERMAL_COEF = 0.2
HALINE_COEF = 0.8
BACKGROUND_MIX = 0.05
CONVECTIVE_MIX = 1.5
STABILITY_FACTOR = 5.0
HEIGHT_FACTOR = 0.2
SLOPE_FACTOR = 0.15

LANES = 128
SUB = 8
FLAT = 6
EARLY = 12
MESH = pl.DeviceIdType.MESH
F32 = jnp.float32


def lane_of(shape):
    return lax.broadcasted_iota(jnp.int32, shape, len(shape) - 1)


def east(x, lane, s=1):
    r = pltpu.roll(x, LANES - s, 2)
    return jnp.where(lane < LANES - s, r[:-1], r[1:])


def west(x, lane):
    r = pltpu.roll(x, 1, 2)
    return jnp.where(lane >= 1, r[:-1], jnp.concatenate([r[-1:], r[:-2]], axis=0))


def east_all(x, lane, s=1):
    r = pltpu.roll(x, LANES - s, 2)
    return jnp.where(lane < LANES - s, r, jnp.concatenate([r[1:], r[:1]], axis=0))


def west_all(x, lane):
    r = pltpu.roll(x, 1, 2)
    return jnp.where(lane >= 1, r, jnp.concatenate([r[-1:], r[:-1]], axis=0))


def step_loop(first, last, unroll, body, carry):
    n = (last - first) // unroll

    def group(g, c):
        for i in range(unroll):
            c = body(first + g * unroll + i, c)
        return c

    carry = lax.fori_loop(0, n, group, carry)
    for k in range(first + n * unroll, last):
        carry = body(jnp.int32(k), carry)
    return carry


def east_in(x, lane, s):
    r = pltpu.roll(x, LANES - s, 2)
    beyond = jnp.zeros_like(r[:1])
    beyond = jnp.concatenate([r[1:], beyond], axis=0) if x.shape[0] > 1 else beyond
    return jnp.where(lane < LANES - s, r, beyond)


def west_in(x, lane):
    r = pltpu.roll(x, 1, 2)
    return jnp.where(lane >= 1, r, jnp.concatenate([jnp.zeros_like(r[:1]), r[:-1]], axis=0))


def face_weights(speed, opening):
    p = speed * (TIME_STEP / 12.0)
    q = jnp.abs(p)
    m = 3.0 * q - jnp.where(opening, TIME_STEP * TRACER_DIFF, 0.0)
    p7 = 7.0 * p
    return p7 - m, p7 + m, p + q, q - p


def kernel(
    lat_total,
    t_in, s_in, u_in, v_in, eta_in, zt_in, mt_in, wi_in, bi_in,
    t_out, s_out, u_out, v_out, flat_out,
    tr, sr, ur, vr, tm, sm, um, vm, pm, wu, ev, xu, xv, px, huc, hvc, dz, xt, xs, yt, ys, ratio,
    zt, mt, wi, bi, de, hue, hve, flat, fu_ref, fv_ref,
    strip0, fe0, fw0, strip_a, fe_a, fw_a, strip_b, fe_b, fw_b, strip_c, fe_c,
    strip2, fe2, fw2, mend, edge_b, acc, pn,
    load_sem, send1, recv1, send2, recv2,
):
    levels, nt, rows, _ = t_out.shape
    end = SUB + rows
    zero = jnp.zeros((nt, SUB, LANES), F32)
    early = EARLY * levels // 12
    nr = rows // SUB
    lon, lat = lax.axis_index("lon"), lax.axis_index("lat")
    nlon, nlat = lax.axis_size("lon"), lax.axis_size("lat")
    wst, est = lax.rem(lon + nlon - 1, nlon), lax.rem(lon + 1, nlon)
    nth, sth = lax.rem(lat + 1, nlat), lax.rem(lat + nlat - 1, nlat)
    has_n, has_s = lat < nlat - 1, lat > 0
    own = pl.ds(SUB, rows)

    barrier = pltpu.get_barrier_semaphore()

    def greet(lo, la):
        pl.semaphore_signal(barrier, inc=1, device_id=(lo, la), device_id_type=MESH)

    greet(wst, lat)
    greet(est, lat)

    @pl.when(has_n)
    def _():
        greet(wst, nth)
        greet(lon, nth)
        greet(est, nth)

    @pl.when(has_s)
    def _():
        greet(wst, sth)
        greet(lon, sth)
        greet(est, sth)

    loads = []

    def load(src, dst):
        group = []
        for c in range(nt):
            cols = pl.ds(c * LANES, LANES)
            group.append(pltpu.make_async_copy(
                src(cols), dst(c), load_sem.at[len(loads) * nt + c]))
            group[-1].start()
        loads.append(group)
        return group

    ld_wi = load(lambda s: wi_in.at[:, s], lambda c: wi.at[c])
    ld_bi = load(lambda s: bi_in.at[:, s], lambda c: bi.at[c])
    ld_u = load(lambda s: u_in.at[:, :, s], lambda c: ur.at[:, c, own, :])
    ld_v = load(lambda s: v_in.at[:, :, s], lambda c: vr.at[:, c, own, :])
    ld_t = load(lambda s: t_in.at[:, :, s], lambda c: tr.at[:, c, own, :])
    ld_s = load(lambda s: s_in.at[:, :, s], lambda c: sr.at[:, c, own, :])
    ld_e = load(lambda s: eta_in.at[:, s], lambda c: flat.at[0, c, own, :])
    ld_z = load(lambda s: zt_in.at[:, s], lambda c: zt.at[c])
    ld_m = load(lambda s: mt_in.at[:, s], lambda c: mt.at[c])

    def arrived(*groups):
        for g in groups:
            for c in g:
                c.wait()

    def clear(first):
        beyond = slice(first, first + SUB)
        de[:, beyond, :] = jnp.zeros((nt + 1, SUB, LANES), F32)
        for ref in (fe0, fw0, fe_b, fw_b, fe2, fw2):
            ref[beyond, :] = jnp.zeros((SUB, LANES), F32)
        for f in range(FLAT):
            flat[f, :, beyond, :] = jnp.zeros((nt, SUB, LANES), F32)

    @pl.when(jnp.logical_not(has_s))
    def _():
        clear(0)

    @pl.when(jnp.logical_not(has_n))
    def _():
        clear(end)

    def copier(send, recv):
        made = []

        def cp(src, dst, lo, la):
            n = len(made)
            made.append(pltpu.make_async_remote_copy(
                src_ref=src, dst_ref=dst, send_sem=send.at[n], recv_sem=recv.at[n],
                device_id=(lo, la), device_id_type=MESH))
            return made[-1]

        return cp

    def start_ns(up, down):
        @pl.when(has_n)
        def _():
            for c in up:
                c.start()

        @pl.when(has_s)
        def _():
            for c in down:
                c.start()

    def recv_ns(up, down):
        @pl.when(has_s)
        def _():
            for c in up:
                c.wait_recv()

        @pl.when(has_n)
        def _():
            for c in down:
                c.wait_recv()

    def sent_ns(up, down):
        @pl.when(has_n)
        def _():
            for c in up:
                c.wait_send()

        @pl.when(has_s)
        def _():
            for c in down:
                c.wait_send()

    cp = copier(send1, recv1)

    def rows_up(ref, n, at):
        return cp(at(ref, end - n, n), at(ref, SUB - n, n), lon, nth)

    def rows_down(ref, n, at):
        return cp(at(ref, SUB, n), at(ref, end, n), lon, sth)

    def cube_rows(ref, first, n):
        return ref.at[:, 0:nt, pl.ds(first, n), :]

    def plane_rows(ref, first, n):
        return ref.at[0:nt, pl.ds(first, n), :]

    depth_up, depth_down = [rows_up(de, 2, plane_rows)], [rows_down(de, 2, plane_rows)]
    flow_up = [rows_up(r, 1, cube_rows) for r in (ur, vr)]
    flow_down = [rows_down(r, 1, cube_rows) for r in (ur, vr)]
    tracer_up = [rows_up(r, 2, cube_rows) for r in (tr, sr)]
    tracer_down = [rows_down(r, 2, cube_rows) for r in (tr, sr)]
    press_down = [cp(cube_rows(pm, SUB, 1), cube_rows(pn, 0, 1), lon, sth)]

    def strips(cp, strip, fe, fw, n):
        def at(ref, first, size):
            return ref.at[pl.ds(first, size), :]

        along = [cp(at(strip, 0, rows), at(fe, SUB, rows), wst, lat),
                 cp(at(strip, 0, rows), at(fw, SUB, rows), est, lat)]
        up = [cp(at(strip, rows - n, n), at(fe, SUB - n, n), wst, nth),
              cp(at(strip, rows - n, n), at(fw, SUB - n, n), est, nth)]
        down = [cp(at(strip, 0, n), at(fe, end, n), wst, sth),
                cp(at(strip, 0, n), at(fw, end, n), est, sth)]
        return along, up, down

    along0, corner_up0, corner_down0 = strips(
        cp, strip0, fe0, fw0, 2)
    along_b = [cp(strip_b, fe_b.at[own, :], wst, lat), cp(strip_b, fw_b.at[own, :], est, lat)]
    corner_up_b = [cp(strip_b.at[pl.ds(rows - 1, 1), :], fe_b.at[pl.ds(SUB - 1, 1), :], wst, nth)]
    corner_down_b = [cp(strip_b.at[pl.ds(0, 1), :], fw_b.at[pl.ds(end, 1), :], est, sth)]
    along_a = [cp(strip_a, fe_a, wst, lat), cp(strip_a, fw_a, est, lat)]
    along_c = [cp(strip_c, fe_c, wst, lat)]

    lane = lane_of((SUB, LANES))
    tall = lane_of((rows, LANES))

    for k in range(levels):
        for ref in (um, vm):
            ref[k, :, 0:SUB, :] = zero
            ref[k, :, end:, :] = zero
        pm[k, :, end:, :] = zero
        wu[k, :, end:, :] = zero
        ev[k, :, 0:SUB, :] = zero
    acc[...] = jnp.zeros_like(acc)

    sub = lax.broadcasted_iota(jnp.int32, (SUB, LANES), 0)
    j = (lat * rows + sub + SUB * lax.rem(lane, nr)).astype(F32)
    j = j + jnp.where(lane < LANES // 2, 0.5, 1.0)
    f = CORIOLIS_SCALE * jnp.sin(LATITUDE_SPAN * (j / lat_total - 0.5)) * (0.25 * TIME_STEP)
    for r in range(nr):
        fu_ref[r] = jnp.broadcast_to(f[:, r:r + 1], (SUB, LANES))
        at = LANES // 2 - (LANES // 2) % nr + nr + r
        fv_ref[r] = jnp.broadcast_to(f[:, at:at + 1], (SUB, LANES))
    fu_south = jnp.broadcast_to(f[0:1, 0:1], (SUB, LANES))
    fv_north = jnp.broadcast_to(f[SUB - 1:SUB, at:at + 1], (SUB, LANES))

    def edge(first, last, p):
        return pltpu.roll(jnp.where(tall < LANES // 2, first, last), 4 * p + 2, 1)

    arrived(ld_wi, ld_bi)
    depth = (wi[...] * bi[...]).astype(F32)
    de[0:nt, own, :] = depth
    strip0[...] = edge(depth[0], depth[nt - 1], 0)
    pl.semaphore_wait(barrier, 2 + 3 * has_n.astype(jnp.int32) + 3 * has_s.astype(jnp.int32))
    for c in along0:
        c.start()
    start_ns(depth_up + corner_up0, depth_down + corner_down0)
    for n, group in enumerate((ld_u, ld_v)):
        arrived(group)
        start_ns(flow_up[n:n + 1], flow_down[n:n + 1])

    place = lax.shift_right_logical(tall, 2)
    group = jnp.zeros((rows, LANES), F32)
    for k in range(levels):
        for n, ref in enumerate((ur, vr)):
            group = jnp.where(place == 2 * k + n, edge(ref[k, 0, own, :], ref[k, nt - 1, own, :], 2 * k + n), group)
    strip_b[...] = group
    for c in along_b:
        c.start()
    start_ns(corner_up_b, corner_down_b)

    HALF = 0.5 * GRAVITY_FACTOR * TIME_STEP
    arrived(ld_t, ld_s)
    group = jnp.zeros((rows, LANES), F32)
    total = jnp.zeros((nt, rows, LANES), F32)
    for k in range(levels):
        wet = de[0:nt, own, :] > k
        t = jnp.where(wet, tr[k, :, own, :], 0.0)
        s = jnp.where(wet, sr[k, :, own, :], 0.0)
        tm[k, :, own, :] = t
        sm[k, :, own, :] = s
        h = (HALF * HALINE_COEF) * s - (HALF * THERMAL_COEF) * t
        p = total + h
        total = p + h
        pm[k, :, own, :] = p
        group = jnp.where(tall == 8 * k + 1, pltpu.roll(p[0], 8 * k + 1, 1), group)
    strip_c[...] = group
    start_ns([], press_down)
    for c in along_c:
        c.start()
    start_ns(tracer_up, tracer_down)
    group = jnp.zeros((rows, LANES), F32)
    for k in range(levels):
        for n, ref in enumerate((tm, sm)):
            group = jnp.where(place == 2 * k + n, edge(ref[k, 0, own, :], ref[k, nt - 1, own, :], 2 * k + n), group)
    strip_a[...] = group
    for c in along_a:
        c.start()
    arrived(ld_e, ld_z, ld_m)
    flat[5, :, own, :] = depth

    def faces(first, last):
        for r in range(first, last, SUB):
            d = de[:, r:r + SUB, :]
            hue[:, r:r + SUB, :] = jnp.minimum(d, east_all(d, lane))
            hve[:, r:r + SUB, :] = jnp.minimum(d, de[:, r + 1:r + SUB + 1, :])

    dz[:, 0:rows, :] = depth
    dz[:, rows:, :] = zero
    for r in range(SUB, end, SUB):
        d = dz[:, r - SUB:r, :]
        huc[:, r - SUB:r, :] = jnp.minimum(d, east_in(d, lane, 1))
        hvc[:, r - SUB:r, :] = jnp.minimum(d, dz[:, r - SUB + 1:r + 1, :])

    def east_fluxes(k, carry):
        kf = k.astype(F32)
        for r in range(SUB, end, SUB):
            here = slice(r, r + SUB)
            opening = huc[:, r - SUB:r, :] > kf
            w0, w1, w2, w3 = face_weights(jnp.where(opening, ur[k, :, here, :], 0.0), opening)
            for ref, to in ((tm, xt), (sm, xs)):
                c = ref[k, :, here, :]
                to[k, :, r - SUB:r, :] = (w0 * c + w1 * east_in(c, lane, 1)
                                          - w2 * east_in(c, lane, 2) + w3 * west_in(c, lane))
        return carry

    MIX = TIME_STEP * MOMENTUM_DIFF
    KEEP = 1.0 - TIME_STEP * BOTTOM_DRAG - 4.0 * MIX

    def sides(k, carry):
        kf = k.astype(F32)
        for r in range(0, rows, SUB):
            here, out = slice(SUB + r, 2 * SUB + r), slice(r, r + SUB)
            u = jnp.where(huc[:, out, :] > kf, ur[k, :, here, :], 0.0)
            v = jnp.where(hvc[:, out, :] > kf, vr[k, :, here, :], 0.0)
            w, e = west_in(u, lane), east_in(v, lane, 1)
            um[k, :, here, :] = u
            vm[k, :, here, :] = v
            wu[k, :, here, :] = w
            ev[k, :, here, :] = e
            xu[k, :, out, :] = east_in(u, lane, 1) + w
            xv[k, :, out, :] = west_in(v, lane) + e
            p = pm[k, :, here, :]
            px[k, :, out, :] = east_in(p, lane, 1) - p
        return carry

    def momentum(k, r, tiles):
        kf = k.astype(F32)
        at = SUB + SUB * r
        here, above, below = slice(at, at + SUB), slice(at + 1, at + SUB + 1), slice(at - 1, at + SUB - 1)
        out = slice(SUB * r, SUB * r + SUB)
        u, un, w = um[k, tiles, here, :], um[k, tiles, above, :], wu[k, tiles, here, :]
        v, vs, e = vm[k, tiles, here, :], vm[k, tiles, below, :], ev[k, tiles, here, :]
        around_u = xu[k, tiles, out, :] + (un + um[k, tiles, below, :])
        around_v = xv[k, tiles, out, :] + (vs + vm[k, tiles, above, :])
        vbar = (v + vs) + (e + ev[k, tiles, below, :])
        ubar = (u + un) + (w + wu[k, tiles, above, :])
        py = pm[k, tiles, above, :] - pm[k, tiles, here, :]
        ut = KEEP * u + MIX * around_u + fu_ref[r] * vbar - px[k, tiles, out, :]
        vt = KEEP * v + MIX * around_v - fv_ref[r] * ubar - py
        ut = jnp.where(hue[tiles, here, :] > kf, ut, 0.0)
        vt = jnp.where(hve[tiles, here, :] > kf, vt, 0.0)
        u_out[k, tiles, out, :] = ut
        v_out[k, tiles, out, :] = vt
        for n, x in enumerate((u, v, ut, vt)):
            acc[n, tiles, out, :] += x

    inner, rim = slice(0, nt - 1), slice(nt - 1, nt)
    hue[0:nt, own, :] = huc[...]
    hve[0:nt, own, :] = hvc[...]
    step_loop(0, levels, 6, sides, 0)

    def inside(k, carry):
        for r in range(nr - 1):
            momentum(k, r, inner)
        return carry

    step_loop(0, levels, 2, inside, 0)
    step_loop(0, early, 4, east_fluxes, 0)

    for c in along0:
        c.wait_recv()
    recv_ns(depth_up, depth_down)
    de[nt, own, :] = pltpu.roll(jnp.where((tall & 3) >= 2, fe0[own, :], fw0[own, :]), LANES - 2, 1)
    faces(SUB, end)


    def last_sides(k, carry):
        kf = k.astype(F32)
        u = jnp.where(hue[rim, own, :] > kf, ur[k, rim, own, :], 0.0)
        um[k, rim, own, :] = u
        xu[k, rim, :, :] = east_in(u, tall, 1) + wu[k, rim, own, :]
        here, out = slice(end - SUB, end), slice(rows - SUB, rows)
        v = jnp.where(hve[0:nt, here, :] > kf, vr[k, :, here, :], 0.0)
        e = east_in(v, lane, 1)
        vm[k, :, here, :] = v
        ev[k, :, here, :] = e
        xv[k, :, out, :] = west_in(v, lane) + e
        return carry

    def outside(k, carry):
        for r in range(nr - 1):
            momentum(k, r, rim)
        momentum(k, nr - 1, slice(0, nt))
        return carry

    step_loop(0, levels, 6, last_sides, 0)
    step_loop(0, levels, 4, outside, 0)
    wind_u = jnp.where(hue[0:nt, own, :] > 0.0, (TIME_STEP * WIND_FACTOR) * zt[...], 0.0)
    wind_v = jnp.where(hve[0:nt, own, :] > 0.0, (TIME_STEP * WIND_FACTOR) * mt[...], 0.0)
    u_out[0, :, 0:rows, :] += wind_u
    v_out[0, :, 0:rows, :] += wind_v
    flat[1, :, own, :] = acc[0]
    flat[2, :, own, :] = acc[1]
    flat[3, :, own, :] = acc[2] - acc[0] + wind_u
    flat[4, :, own, :] = acc[3] - acc[1] + wind_v

    recv_ns(corner_up0, corner_down0)
    for out in (slice(0, SUB), slice(end, end + SUB)):
        de[nt, out, :] = pltpu.roll(jnp.where((lane & 3) >= 2, fe0[out, :], fw0[out, :]), LANES - 2, 1)
    faces(0, SUB)
    faces(end - SUB, end + SUB)
    for c in along_b + along_c:
        c.wait_recv()
    recv_ns(corner_up_b, corner_down_b)
    level = lax.shift_right_logical(tall, 3).astype(F32)

    def by_lane(at, one, two, five, six):
        return jnp.where(at == 1, one, jnp.where(at == 2, two, jnp.where(at == 5, five, six)))

    def column(ref, c, at, which=own, n=rows):
        return jnp.broadcast_to(ref[c, which, at:at + 1], (n, LANES))

    LAST = LANES - 1
    for r in range(0, end + SUB, SUB):
        here = slice(r, r + SUB)
        limit = by_lane(lane & 7, *(column(ref, nt, at, here, SUB) for ref in (hue, hve) for at in (LAST, 0)))
        x = jnp.where((lane & 3) >= 2, fe_b[here, :], fw_b[here, :])
        edge_b[here, :] = jnp.where(limit > lax.shift_right_logical(lane, 3).astype(F32), x, 0.0)
    x = edge_b[own, :]
    spot = tall & 7
    near = jnp.where((spot & 1) == 1, pltpu.roll(x, LAST, 1), pltpu.roll(x, 1, 1))
    above, below = slice(SUB + 1, end + 1), slice(SUB - 1, end - 1)
    turn_u = fu_ref[...].reshape(rows, LANES) * pltpu.roll(x + edge_b[below, :], LANES - 5, 1) - fe_c[...]
    turn_v = fv_ref[...].reshape(rows, LANES) * pltpu.roll(x + edge_b[above, :], 5, 1)
    extra = MIX * near + jnp.where(spot == 1, turn_u, 0.0) - jnp.where(spot == 6, turn_v, 0.0)
    limit = by_lane(spot, column(hue, nt - 1, LAST), column(hue, 0, 0), column(hve, nt - 1, LAST), column(hve, 0, 0))
    extra = jnp.where(limit > level, extra, 0.0)
    total = jnp.zeros((rows, LANES), F32)
    for k in range(levels):
        total = total + (pltpu.roll(extra, LANES - 8 * k, 1) if k else extra)
    total_u, total_v = pltpu.roll(total, LANES - 2, 1), pltpu.roll(total, LANES - 6, 1)
    for f, d in ((3, total_u), (4, total_v)):
        flat[f, 0, own, :] += jnp.where(tall == 0, d, 0.0)
        flat[f, nt - 1, own, :] += jnp.where(tall == LAST, d, 0.0)

    recv_ns(flow_up, flow_down)
    recv_ns([], press_down)
    top = lax.broadcasted_iota(jnp.int32, (SUB, LANES), 0) == 0

    def far_rows(k, carry):
        nu, nv, su, sv = carry
        kf = k.astype(F32)
        out = slice(end, end + SUB)
        u = jnp.where(hue[0:nt, out, :] > kf, ur[k, :, out, :], 0.0)
        v = jnp.where(hve[0:nt, out, :] > kf, vr[k, :, out, :], 0.0)
        edge_row = slice(end - 1, end + SUB - 1)
        du = jnp.where(top & (hue[0:nt, edge_row, :] > kf), MIX * u, 0.0)
        dv = jnp.where(top & (hve[0:nt, edge_row, :] > kf),
                       MIX * v - fv_north * (u + west_in(u, lane)) - pn[k], 0.0)
        row = slice(rows - 1, rows + SUB - 1)
        u_out[k, :, row, :] += du
        v_out[k, :, row, :] += dv
        nu, nv = nu + du, nv + dv

        out = slice(SUB - 1, 2 * SUB - 1)
        u = jnp.where(hue[0:nt, out, :] > kf, ur[k, :, out, :], 0.0)
        v = jnp.where(hve[0:nt, out, :] > kf, vr[k, :, out, :], 0.0)
        edge_row = slice(SUB, 2 * SUB)
        du = jnp.where(top & (hue[0:nt, edge_row, :] > kf),
                       MIX * u + fu_south * (v + east_in(v, lane, 1)), 0.0)
        dv = jnp.where(top & (hve[0:nt, edge_row, :] > kf), MIX * v, 0.0)
        u_out[k, :, 0:SUB, :] += du
        v_out[k, :, 0:SUB, :] += dv
        return nu, nv, su + du, sv + dv

    nu, nv, su, sv = step_loop(0, levels, 4, far_rows, (zero,) * 4)
    for f, north, south in ((3, nu, su), (4, nv, sv)):
        flat[f, :, SUB:2 * SUB, :] += south
        flat[f, :, end - SUB:end, :] += pltpu.roll(north, SUB - 1, 1)

    spot = lax.shift_right_logical(tall, 3)
    group = jnp.zeros((rows, LANES), F32)
    for f in range(FLAT):
        x = jnp.where(tall < LANES // 2, flat[f, 0, own, :], flat[f, nt - 1, own, :])
        group = jnp.where(spot == f, pltpu.roll(x, 8 * f + 4, 1), group)
    strip2[...] = group
    cp = copier(send2, recv2)
    flat_up = [cp(cube_rows(flat, end - NSUB, NSUB), cube_rows(flat, SUB - NSUB, NSUB), lon, nth)]
    flat_down = [cp(cube_rows(flat, SUB, NSUB), cube_rows(flat, end, NSUB), lon, sth)]
    along2, corner_up2, corner_down2 = strips(
        cp, strip2, fe2, fw2, NSUB)
    start_ns(flat_up, flat_down)
    for c in along2:
        c.start()
    start_ns(corner_up2, corner_down2)

    for k in range(levels):
        du = pltpu.roll(extra, LANES - 2 - 8 * k, 1)
        dv = pltpu.roll(extra, LANES - 6 - 8 * k, 1)
        for ref, d in ((u_out, du), (v_out, dv)):
            ref[k, 0, 0:rows, :] += jnp.where(tall == 0, d, 0.0)
            ref[k, nt - 1, 0:rows, :] += jnp.where(tall == LAST, d, 0.0)

    recv_ns(tracer_up, tracer_down)

    def tracer_rows(k, carry):
        kf = k.astype(F32)
        for a in (0, end):
            out = slice(a, a + SUB)
            wet = de[0:nt, out, :] > kf
            tm[k, :, out, :] = jnp.where(wet, tr[k, :, out, :], 0.0)
            sm[k, :, out, :] = jnp.where(wet, sr[k, :, out, :], 0.0)
        vm[k, :, 0:SUB, :] = jnp.where(hve[0:nt, 0:SUB, :] > kf, vr[k, :, 0:SUB, :], 0.0)
        return carry

    step_loop(0, levels, 2, tracer_rows, 0)

    starts = list(range(SUB - 1, end - SUB, SUB)) + [end - SUB]

    def north_fluxes(k, carry):
        kf = k.astype(F32)
        for a in starts:
            here = slice(a, a + SUB)
            w0, w1, w2, w3 = face_weights(vm[k, :, here, :], hve[0:nt, here, :] > kf)
            for ref, to in ((tm, yt), (sm, ys)):
                to[k, :, here, :] = (
                    w0 * ref[k, :, here, :] + w1 * ref[k, :, a + 1:a + SUB + 1, :]
                    - w2 * ref[k, :, a + 2:a + SUB + 2, :] + w3 * ref[k, :, a - 1:a + SUB - 1, :])
        return carry

    step_loop(early, levels, 4, east_fluxes, 0)
    step_loop(0, levels, 1, north_fluxes, 0)
    for c in along_a:
        c.wait_recv()

    q = tall & 3

    def speeds(x, limit):
        x = jnp.where((tall & 7) < 4, x, pltpu.roll(x, 4, 1))
        opening = limit > level
        return face_weights(jnp.where(opening, x, 0.0), opening)

    mine = strip_a[...]
    a = jnp.where(q < 2, mine, fe_a[...])
    b = jnp.where(q < 2, fw_a[...], mine)
    w0, w1, w2, w3 = speeds(strip_b[...], jnp.where(
        q == 0, column(hue, nt - 1, LANES - 2), jnp.where(q == 1, column(hue, nt - 1, LAST), column(hue, 0, 0))))
    b_west = pltpu.roll(b, 1, 1)
    flux = (jnp.where(q == 1, w0 * a + w1 * pltpu.roll(a, LANES - 1, 1) + w3 * pltpu.roll(a, 1, 1), 0.0)
            - w2 * pltpu.roll(a, LANES - 2, 1))
    flux = jnp.where(q < 2, flux, jnp.where(q == 2, w3 * b_west, 0.0))
    w0, w1, w2, w3 = speeds(fw_b[own, :], column(hue, nt, LAST))
    first = w0 * b + w1 * pltpu.roll(b, LANES - 1, 1) - w2 * pltpu.roll(b, LANES - 2, 1) + w3 * b_west
    mend[...] = flux - pltpu.roll(jnp.where(q == 1, first, flux), 1, 1)

    def mended(x, m):
        edge_lane = lane_of(m.shape)
        first = x[:1] - jnp.where(edge_lane < 2, m, 0.0)[None]
        last = x[-1:] - jnp.where(edge_lane >= LANES - 2, m, 0.0)[None]
        return jnp.concatenate([first, x[1:-1], last], axis=0)

    span = 2 * SUB if rows % (2 * SUB) == 0 else SUB
    long = lane_of((span, LANES))
    DIFF = TIME_STEP * STABILITY_FACTOR * BACKGROUND_MIX
    BASE = TIME_STEP * (BACKGROUND_MIX + CONVECTIVE_MIX)
    for r in range(0, rows, span):
        out = slice(r, r + span)
        here, below = slice(SUB + r, SUB + r + span), slice(SUB + r - 1, SUB + r + span - 1)

        def star(k):
            fx = xt[k, :, out, :]
            t = tm[k, :, here, :] - (fx - west_in(fx, long)) - (yt[k, :, here, :] - yt[k, :, below, :])
            fx = xs[k, :, out, :]
            s = sm[k, :, here, :] - (fx - west_in(fx, long)) - (ys[k, :, here, :] - ys[k, :, below, :])
            t = mended(t, pltpu.roll(mend[out, :], LANES - 2 - 8 * k, 1))
            s = mended(s, pltpu.roll(mend[out, :], LANES - 6 - 8 * k, 1))
            return t, s, HALINE_COEF * s - THERMAL_COEF * t

        def forward(k, carry):
            t, s, dens, lower, qt, qs = carry
            tn, sn, densn = star(k)
            rise = jnp.maximum(densn - dens, 0.0)
            e = 1.0 + STABILITY_FACTOR * rise
            n = jnp.where(de[0:nt, here, :] > k.astype(F32), BASE + DIFF * rise, 0.0)
            w = 1.0 / (e * lower + n)
            rat = n * w
            ew = e * w
            gt, gs = t + qt, s + qs
            t_out[k - 1, :, out, :] = gt * ew
            s_out[k - 1, :, out, :] = gs * ew
            ratio[k - 1, :, out, :] = rat
            return tn, sn, densn, 1.0 + rat * lower, rat * gt, rat * gs

        zero = jnp.zeros((nt, span, LANES), F32)
        carry = star(0) + (zero + 1.0, zero, zero)
        t, s, _, lower, qt, qs = step_loop(1, levels, 2, forward, carry)
        w = 1.0 / lower
        t, s = (t + qt) * w, (s + qs) * w
        t_out[levels - 1, :, out, :] = t
        s_out[levels - 1, :, out, :] = s

        def backward(i, carry):
            t, s = carry
            k = levels - 2 - i
            rat = ratio[k, :, out, :]
            t = t_out[k, :, out, :] + rat * t
            s = s_out[k, :, out, :] + rat * s
            t_out[k, :, out, :] = t
            s_out[k, :, out, :] = s
            return t, s

        step_loop(0, levels - 1, 1, backward, (t, s))

    for c in along0 + along_a + along_b + along_c:
        c.wait_send()
    sent_ns(depth_up + corner_up0 + flow_up + tracer_up + corner_up_b,
            depth_down + corner_down0 + flow_down + tracer_down + corner_down_b + press_down)
    recv_ns(flat_up, flat_down)
    for c in along2:
        c.wait_recv()
    recv_ns(corner_up2, corner_down2)
    wide = slice(SUB - NSUB, end + NSUB)
    count = rows + 2 * NSUB
    halo = jnp.where((lane_of((count, LANES)) & 7) >= 4, fe2[wide, :], fw2[wide, :])
    for f in range(FLAT):
        flat_out[f, 0:nt, 0:count] = flat[f, :, wide, :]
        flat_out[f, nt, 0:count] = pltpu.roll(halo, LANES - 8 * f - 4, 1)
    flat_out[5, :, count:, :] = jnp.zeros((nt + 1, SUB, LANES), F32)

    for c in along2:
        c.wait_send()
    sent_ns(flat_up + corner_up2, flat_down + corner_down2)


def tail(
    t, s, ut, vt, flat,
    t_out, s_out, u_out, v_out, eta_out, tx_out, ty_out,
    eta, bu, bv, hx, hy, un, vn, cor, sem,
):
    levels, nt, rows, _ = t.shape
    count = rows + 2 * NSUB
    lane = lane_of((SUB, LANES))
    copies = []

    def put(src, dst):
        for c in range(nt):
            copies.append(pltpu.make_async_copy(
                src(c), dst(pl.ds(c * LANES, LANES)), sem.at[len(copies)]))
            copies[-1].start()

    put(lambda c: t.at[:, c], lambda d: t_out.at[:, :, d])
    put(lambda c: s.at[:, c], lambda d: s_out.at[:, :, d])

    for ref in (eta, bu, bv):
        ref[:, 0:SUB, :] = jnp.zeros((nt + 1, SUB, LANES), F32)
        ref[:, count + SUB:, :] = jnp.zeros((nt + 1, SUB, LANES), F32)
    tiles = range(0, count, SUB)
    eta[:, SUB:count + SUB, :] = flat[0, :, 0:count, :]
    bu[:, SUB:count + SUB, :] = flat[1, :, 0:count, :]
    bv[:, SUB:count + SUB, :] = flat[2, :, 0:count, :]
    for r in tiles:
        d = flat[5, :, r:r + SUB, :]
        hx[:, r:r + SUB, :] = jnp.minimum(d, east_all(d, lane))
        hy[:, r:r + SUB, :] = jnp.minimum(d, flat[5, :, r + 1:r + SUB + 1, :])
    for sub in range(NSUB):
        for r in tiles:
            here, below = slice(SUB + r, 2 * SUB + r), slice(SUB + r - 1, 2 * SUB + r - 1)
            x = bu[:, here, :]
            eta[:, here, :] = eta[:, here, :] - HEIGHT_FACTOR * (
                x - west_all(x, lane) + (bv[:, here, :] - bv[:, below, :]))
        for r in tiles:
            here, above = slice(SUB + r, 2 * SUB + r), slice(SUB + r + 1, 2 * SUB + r + 1)
            raw = slice(r, r + SUB)
            x = eta[:, here, :]
            bu[:, here, :] = (bu[:, here, :] + (1.0 / NSUB) * flat[3, :, raw, :]
                              - SLOPE_FACTOR * hx[:, raw, :] * (east_all(x, lane) - x))
            bv[:, here, :] = (bv[:, here, :] + (1.0 / NSUB) * flat[4, :, raw, :]
                              - SLOPE_FACTOR * hy[:, raw, :] * (eta[:, above, :] - x))
    mid = pl.ds(SUB + NSUB, rows)
    put(lambda c: eta.at[c, mid, :], lambda d: eta_out.at[:, d])
    put(lambda c: bu.at[c, mid, :], lambda d: tx_out.at[:, d])
    put(lambda c: bv.at[c, mid, :], lambda d: ty_out.at[:, d])

    for r in range(0, rows, SUB):
        raw = slice(NSUB + r, NSUB + r + SUB)
        hu, hv = hx[0:nt, raw, :], hy[0:nt, raw, :]
        done = slice(SUB + NSUB + r, 2 * SUB + NSUB + r)
        out = slice(r, r + SUB)
        cor[0, :, out, :] = (bu[0:nt, done, :] - (flat[3, 0:nt, raw, :] + flat[1, 0:nt, raw, :])) / jnp.maximum(hu, 1.0)
        cor[1, :, out, :] = (bv[0:nt, done, :] - (flat[4, 0:nt, raw, :] + flat[2, 0:nt, raw, :])) / jnp.maximum(hv, 1.0)
        cor[2, :, out, :] = hu
        cor[3, :, out, :] = hv

    @pl.loop(0, levels)
    def _(k):
        kf = k.astype(F32)
        un[k] = jnp.where(cor[2] > kf, ut[k, :, 0:rows, :] + cor[0], 0.0)
        vn[k] = jnp.where(cor[3] > kf, vt[k, :, 0:rows, :] + cor[1], 0.0)

    put(lambda c: un.at[:, c], lambda d: u_out.at[:, :, d])
    put(lambda c: vn.at[:, c], lambda d: v_out.at[:, :, d])
    for c in copies:
        c.wait()


def body(*args):
    levels, rows, cols = args[0].shape
    nt = cols // LANES
    erows = rows + 2 * SUB
    count = rows + 2 * NSUB

    def vmem(*shape):
        return pltpu.VMEM(shape, F32)

    def out(*shape):
        return jax.ShapeDtypeStruct(shape, F32)

    block = pl.BlockSpec(memory_space=pltpu.VMEM)
    far = pl.BlockSpec(memory_space=pltpu.HBM)
    raw = vmem(levels, nt, erows, LANES)
    own = vmem(levels, nt, rows, LANES)
    ints = pltpu.VMEM((nt, rows, LANES), jnp.int32)
    n1, n2 = 2 + 8 + 1 + 6 + 4 + 3, 2 + 6
    cube = (levels, nt, rows, LANES)
    parts = pl.pallas_call(
        functools.partial(kernel, rows * lax.axis_size("lat")),
        out_shape=(out(*cube),) * 2 + (out(levels, nt, rows + SUB, LANES),) * 2 + (out(FLAT, nt + 1, count + SUB, LANES),),
        in_specs=[far] * 9,
        out_specs=(block,) * 5,
        scratch_shapes=(
            [raw] * 11 + [own] * 3 + [vmem(nt, rows, LANES)] * 2
            + [vmem(nt, rows + SUB, LANES), own, own, raw, raw, own]
            + [vmem(nt, rows, LANES)] * 2 + [ints] * 2
            + [vmem(nt + 1, erows + SUB, LANES)] + [vmem(nt + 1, erows, LANES)] * 2
            + [vmem(FLAT, nt, erows, LANES)]
            + [vmem(rows // SUB, SUB, LANES)] * 2
            + [vmem(rows, LANES), vmem(erows, LANES), vmem(erows, LANES)]
            + [vmem(rows, LANES)] * 3
            + [vmem(rows, LANES), vmem(erows, LANES), vmem(erows, LANES)]
            + [vmem(rows, LANES)] * 2
            + [vmem(rows, LANES), vmem(erows, LANES), vmem(erows, LANES), vmem(rows, LANES)]
            + [vmem(erows, LANES), vmem(4, nt, rows, LANES), vmem(levels, nt, SUB, LANES)]
            + [pltpu.SemaphoreType.DMA((9 * nt,))]
            + [pltpu.SemaphoreType.DMA((n1,))] * 2
            + [pltpu.SemaphoreType.DMA((n2,))] * 2
        ),
        compiler_params=pltpu.CompilerParams(
            collective_id=0, has_side_effects=True, vmem_limit_bytes=32 * 1024 * 1024),
    )(*[pltpu.with_memory_space_constraint(a, pltpu.HBM) for a in args])
    cube, plane = (levels, rows, cols), (rows, cols)
    return pl.pallas_call(
        tail,
        out_shape=(pltpu.HBM(cube, F32),) * 4 + (pltpu.HBM(plane, F32),) * 3,
        in_specs=[block] * 5,
        out_specs=(far,) * 7,
        scratch_shapes=(
            [vmem(nt + 1, count + 2 * SUB, LANES)] * 3 + [vmem(nt + 1, count, LANES)] * 2
            + [own, own, vmem(4, nt, rows, LANES)]
            + [pltpu.SemaphoreType.DMA((7 * nt,))]
        ),
        compiler_params=pltpu.CompilerParams(vmem_limit_bytes=32 * 1024 * 1024),
    )(*parts)


def solution(mesh):
    cube, plane = P(None, "lat", "lon"), P("lat", "lon")
    return jax.shard_map(
        body,
        mesh=mesh,
        in_specs=(cube,) * 4 + (plane,) * 5,
        out_specs=(cube,) * 4 + (plane,) * 3,
        check_vma=False,
    )
```

```python
import functools

import jax
import jax.numpy as jnp
from jax import lax
from jax.experimental import pallas as pl
from jax.experimental.pallas import tpu as pltpu
from jax.sharding import PartitionSpec as P

NSUB = 4
TIME_STEP = 0.4
TRACER_DIFF = 0.05
MOMENTUM_DIFF = 0.05
BOTTOM_DRAG = 0.05
WIND_FACTOR = 0.5
CORIOLIS_SCALE = 0.5
LATITUDE_SPAN = 2.6
GRAVITY_FACTOR = 0.3
THERMAL_COEF = 0.2
HALINE_COEF = 0.8
BACKGROUND_MIX = 0.05
CONVECTIVE_MIX = 1.5
STABILITY_FACTOR = 5.0
HEIGHT_FACTOR = 0.2
SLOPE_FACTOR = 0.15

LANES = 128
SUB = 8
FLAT = 6
ETA, SUM_U, SUM_V, DEEP, PUSH_U, PUSH_V = range(FLAT)
SOON = 4
CHUNKS = 3
MESH = pl.DeviceIdType.MESH
F32 = jnp.float32


def lane_of(shape):
    return lax.broadcasted_iota(jnp.int32, shape, len(shape) - 1)


def east(x, lane, s=1):
    r = pltpu.roll(x, LANES - s, 2)
    return jnp.where(lane < LANES - s, r[:-1], r[1:])


def west(x, lane):
    r = pltpu.roll(x, 1, 2)
    return jnp.where(lane >= 1, r[:-1], jnp.concatenate([r[-1:], r[:-2]], axis=0))


def east_all(x, lane, s=1):
    r = pltpu.roll(x, LANES - s, 2)
    return jnp.where(lane < LANES - s, r, jnp.concatenate([r[1:], r[:1]], axis=0))


def west_all(x, lane):
    r = pltpu.roll(x, 1, 2)
    return jnp.where(lane >= 1, r, jnp.concatenate([r[-1:], r[:-1]], axis=0))


def step_loop(first, last, unroll, body, carry):
    n = (last - first) // unroll

    def group(g, c):
        for i in range(unroll):
            c = body(first + g * unroll + i, c)
        return c

    carry = lax.fori_loop(0, n, group, carry)
    for k in range(first + n * unroll, last):
        carry = body(jnp.int32(k), carry)
    return carry


def east_in(x, lane, s):
    r = pltpu.roll(x, LANES - s, 2)
    beyond = jnp.zeros_like(r[:1])
    beyond = jnp.concatenate([r[1:], beyond], axis=0) if x.shape[0] > 1 else beyond
    return jnp.where(lane < LANES - s, r, beyond)


def west_in(x, lane):
    r = pltpu.roll(x, 1, 2)
    return jnp.where(lane >= 1, r, jnp.concatenate([jnp.zeros_like(r[:1]), r[:-1]], axis=0))


def face_weights(speed, opening):
    p = speed * (TIME_STEP / 12.0)
    q = jnp.abs(p)
    m = 3.0 * q - jnp.where(opening, TIME_STEP * TRACER_DIFF, 0.0)
    p7 = 7.0 * p
    return p7 - m, p7 + m, p + q, q - p


def kernel(
    lat_total,
    t_in, s_in, u_in, v_in, eta_in, zt_in, mt_in, wi_in, bi_in,
    t_out, s_out, u_out, v_out, flat_out,
    tr, sr, ur, vr, tm, sm, um, vm, pm, wu, ev, xu, xv, px, huc, hvc, dz, xt, xs, yt, ys, ratio,
    zt, mt, wi, bi, de, hue, hve, flat, fu_ref, fv_ref,
    strip0, fe0, fw0, strip_a, fe_a, fw_a, strip_b, fe_b, fw_b, strip_c, fe_c,
    strip2, fe2, fw2, strip3, fe3, fw3, mend, edge_b, acc, pn, rim_rows,
    load_sem, send1, recv1, send2, recv2,
):
    levels, nt, rows, _ = t_out.shape
    end = SUB + rows
    zero = jnp.zeros((nt, SUB, LANES), F32)
    nr = rows // SUB
    lon, lat = lax.axis_index("lon"), lax.axis_index("lat")
    nlon, nlat = lax.axis_size("lon"), lax.axis_size("lat")
    wst, est = lax.rem(lon + nlon - 1, nlon), lax.rem(lon + 1, nlon)
    nth, sth = lax.rem(lat + 1, nlat), lax.rem(lat + nlat - 1, nlat)
    has_n, has_s = lat < nlat - 1, lat > 0
    own = pl.ds(SUB, rows)

    barrier = pltpu.get_barrier_semaphore()

    def greet(lo, la):
        pl.semaphore_signal(barrier, inc=1, device_id=(lo, la), device_id_type=MESH)

    greet(wst, lat)
    greet(est, lat)

    @pl.when(has_n)
    def _():
        greet(wst, nth)
        greet(lon, nth)
        greet(est, nth)

    @pl.when(has_s)
    def _():
        greet(wst, sth)
        greet(lon, sth)
        greet(est, sth)

    loads = []

    def load(src, dst):
        group = []
        for c in range(nt):
            cols = pl.ds(c * LANES, LANES)
            group.append(pltpu.make_async_copy(
                src(cols), dst(c), load_sem.at[len(loads) * nt + c]))
            group[-1].start()
        loads.append(group)
        return group

    ld_wi = load(lambda s: wi_in.at[:, s], lambda c: wi.at[c])
    ld_bi = load(lambda s: bi_in.at[:, s], lambda c: bi.at[c])
    ld_u = load(lambda s: u_in.at[:, :, s], lambda c: ur.at[:, c, own, :])
    ld_v = load(lambda s: v_in.at[:, :, s], lambda c: vr.at[:, c, own, :])
    ld_t = load(lambda s: t_in.at[:, :, s], lambda c: tr.at[:, c, own, :])
    ld_s = load(lambda s: s_in.at[:, :, s], lambda c: sr.at[:, c, own, :])
    ld_e = load(lambda s: eta_in.at[:, s], lambda c: flat.at[ETA, c, own, :])
    ld_z = load(lambda s: zt_in.at[:, s], lambda c: zt.at[c])
    ld_m = load(lambda s: mt_in.at[:, s], lambda c: mt.at[c])

    def arrived(*groups):
        for g in groups:
            for c in g:
                c.wait()

    def clear(first):
        beyond = slice(first, first + SUB)
        de[:, beyond, :] = jnp.zeros((nt + 1, SUB, LANES), F32)
        for ref in (fe0, fw0, fe_b, fw_b, fe2, fw2, fe3, fw3):
            ref[beyond, :] = jnp.zeros((SUB, LANES), F32)
        for f in range(FLAT):
            flat[f, :, beyond, :] = jnp.zeros((nt, SUB, LANES), F32)

    @pl.when(jnp.logical_not(has_s))
    def _():
        clear(0)

    @pl.when(jnp.logical_not(has_n))
    def _():
        clear(end)

    def copier(send, recv):
        made = []

        def cp(src, dst, lo, la):
            n = len(made)
            made.append(pltpu.make_async_remote_copy(
                src_ref=src, dst_ref=dst, send_sem=send.at[n], recv_sem=recv.at[n],
                device_id=(lo, la), device_id_type=MESH))
            return made[-1]

        return cp

    def start_ns(up, down):
        @pl.when(has_n)
        def _():
            for c in up:
                c.start()

        @pl.when(has_s)
        def _():
            for c in down:
                c.start()

    def recv_ns(up, down):
        @pl.when(has_s)
        def _():
            for c in up:
                c.wait_recv()

        @pl.when(has_n)
        def _():
            for c in down:
                c.wait_recv()

    def sent_ns(up, down):
        @pl.when(has_n)
        def _():
            for c in up:
                c.wait_send()

        @pl.when(has_s)
        def _():
            for c in down:
                c.wait_send()

    cp = copier(send1, recv1)

    def rows_up(ref, n, at):
        return cp(at(ref, end - n, n), at(ref, SUB - n, n), lon, nth)

    def rows_down(ref, n, at):
        return cp(at(ref, SUB, n), at(ref, end, n), lon, sth)

    def cube_rows(ref, first, n):
        return ref.at[:, 0:nt, pl.ds(first, n), :]

    def plane_rows(ref, first, n):
        return ref.at[0:nt, pl.ds(first, n), :]

    depth_up, depth_down = [rows_up(de, 2, plane_rows)], [rows_down(de, 2, plane_rows)]
    flow_up = [rows_up(r, 1, cube_rows) for r in (ur, vr)]
    flow_down = [rows_down(r, 1, cube_rows) for r in (ur, vr)]
    tracer_up = [rows_up(r, 2, cube_rows) for r in (tr, sr)]
    tracer_down = [rows_down(r, 2, cube_rows) for r in (tr, sr)]
    press_down = [cp(cube_rows(pm, SUB, 1), cube_rows(pn, 0, 1), lon, sth)]

    def strips(cp, strip, fe, fw, n):
        def at(ref, first, size):
            return ref.at[pl.ds(first, size), :]

        along = [cp(at(strip, 0, rows), at(fe, SUB, rows), wst, lat),
                 cp(at(strip, 0, rows), at(fw, SUB, rows), est, lat)]
        up = [cp(at(strip, rows - n, n), at(fe, SUB - n, n), wst, nth),
              cp(at(strip, rows - n, n), at(fw, SUB - n, n), est, nth)]
        down = [cp(at(strip, 0, n), at(fe, end, n), wst, sth),
                cp(at(strip, 0, n), at(fw, end, n), est, sth)]
        return along, up, down

    along0, corner_up0, corner_down0 = strips(
        cp, strip0, fe0, fw0, 2)
    along_b = [cp(strip_b, fe_b.at[own, :], wst, lat), cp(strip_b, fw_b.at[own, :], est, lat)]
    corner_up_b = [cp(strip_b.at[pl.ds(rows - 1, 1), :], fe_b.at[pl.ds(SUB - 1, 1), :], wst, nth)]
    corner_down_b = [cp(strip_b.at[pl.ds(0, 1), :], fw_b.at[pl.ds(end, 1), :], est, sth)]
    along_a = [cp(strip_a, fe_a, wst, lat), cp(strip_a, fw_a, est, lat)]
    along_c = [cp(strip_c, fe_c, wst, lat)]

    lane = lane_of((SUB, LANES))
    tall = lane_of((rows, LANES))

    for k in range(levels):
        for ref in (um, vm):
            ref[k, :, 0:SUB, :] = zero
            ref[k, :, end:, :] = zero
        pm[k, :, end:, :] = zero
        wu[k, :, end:, :] = zero
        ev[k, :, 0:SUB, :] = zero
    acc[...] = jnp.zeros_like(acc)

    sub = lax.broadcasted_iota(jnp.int32, (SUB, LANES), 0)
    j = (lat * rows + sub + SUB * lax.rem(lane, nr)).astype(F32)
    j = j + jnp.where(lane < LANES // 2, 0.5, 1.0)
    f = CORIOLIS_SCALE * jnp.sin(LATITUDE_SPAN * (j / lat_total - 0.5)) * (0.25 * TIME_STEP)
    for r in range(nr):
        fu_ref[r] = jnp.broadcast_to(f[:, r:r + 1], (SUB, LANES))
        at = LANES // 2 - (LANES // 2) % nr + nr + r
        fv_ref[r] = jnp.broadcast_to(f[:, at:at + 1], (SUB, LANES))
    fu_south = jnp.broadcast_to(f[0:1, 0:1], (SUB, LANES))
    fv_north = jnp.broadcast_to(f[SUB - 1:SUB, at:at + 1], (SUB, LANES))

    def edge(first, last, p):
        return pltpu.roll(jnp.where(tall < LANES // 2, first, last), 4 * p + 2, 1)

    arrived(ld_wi, ld_bi)
    depth = (wi[...] * bi[...]).astype(F32)
    de[0:nt, own, :] = depth
    strip0[...] = edge(depth[0], depth[nt - 1], 0)
    pl.semaphore_wait(barrier, 2 + 3 * has_n.astype(jnp.int32) + 3 * has_s.astype(jnp.int32))
    for c in along0:
        c.start()
    start_ns(depth_up + corner_up0, depth_down + corner_down0)
    for n, group in enumerate((ld_u, ld_v)):
        arrived(group)
        start_ns(flow_up[n:n + 1], flow_down[n:n + 1])

    place = lax.shift_right_logical(tall, 2)
    group = jnp.zeros((rows, LANES), F32)
    for k in range(levels):
        for n, ref in enumerate((ur, vr)):
            group = jnp.where(place == 2 * k + n, edge(ref[k, 0, own, :], ref[k, nt - 1, own, :], 2 * k + n), group)
    strip_b[...] = group
    for c in along_b:
        c.start()
    start_ns(corner_up_b, corner_down_b)

    HALF = 0.5 * GRAVITY_FACTOR * TIME_STEP
    arrived(ld_t, ld_s)
    group = jnp.zeros((rows, LANES), F32)
    total = jnp.zeros((nt, rows, LANES), F32)
    for k in range(levels):
        wet = de[0:nt, own, :] > k
        t = jnp.where(wet, tr[k, :, own, :], 0.0)
        s = jnp.where(wet, sr[k, :, own, :], 0.0)
        tm[k, :, own, :] = t
        sm[k, :, own, :] = s
        h = (HALF * HALINE_COEF) * s - (HALF * THERMAL_COEF) * t
        p = total + h
        total = p + h
        pm[k, :, own, :] = p
        group = jnp.where(tall == 8 * k + 1, pltpu.roll(p[0], 8 * k + 1, 1), group)
    strip_c[...] = group
    start_ns([], press_down)
    for c in along_c:
        c.start()
    start_ns(tracer_up, tracer_down)
    group = jnp.zeros((rows, LANES), F32)
    for k in range(levels):
        for n, ref in enumerate((tm, sm)):
            group = jnp.where(place == 2 * k + n, edge(ref[k, 0, own, :], ref[k, nt - 1, own, :], 2 * k + n), group)
    strip_a[...] = group
    for c in along_a:
        c.start()
    arrived(ld_e, ld_z, ld_m)
    flat[DEEP, :, own, :] = depth

    def faces(first, last):
        for r in range(first, last, SUB):
            d = de[:, r:r + SUB, :]
            hue[:, r:r + SUB, :] = jnp.minimum(d, east_all(d, lane))
            hve[:, r:r + SUB, :] = jnp.minimum(d, de[:, r + 1:r + SUB + 1, :])

    dz[:, 0:rows, :] = depth
    dz[:, rows:, :] = zero
    for r in range(SUB, end, SUB):
        d = dz[:, r - SUB:r, :]
        huc[:, r - SUB:r, :] = jnp.minimum(d, east_in(d, lane, 1))
        hvc[:, r - SUB:r, :] = jnp.minimum(d, dz[:, r - SUB + 1:r + 1, :])

    def east_fluxes(k, carry):
        kf = k.astype(F32)
        for r in range(SUB, end, SUB):
            here = slice(r, r + SUB)
            opening = huc[:, r - SUB:r, :] > kf
            w0, w1, w2, w3 = face_weights(jnp.where(opening, ur[k, :, here, :], 0.0), opening)
            for ref, to in ((tm, xt), (sm, xs)):
                c = ref[k, :, here, :]
                to[k, :, r - SUB:r, :] = (w0 * c + w1 * east_in(c, lane, 1)
                                          - w2 * east_in(c, lane, 2) + w3 * west_in(c, lane))
        return carry

    MIX = TIME_STEP * MOMENTUM_DIFF
    KEEP = 1.0 - TIME_STEP * BOTTOM_DRAG - 4.0 * MIX

    def sides(k, carry):
        kf = k.astype(F32)
        for r in range(0, rows, SUB):
            here, out = slice(SUB + r, 2 * SUB + r), slice(r, r + SUB)
            u = jnp.where(huc[:, out, :] > kf, ur[k, :, here, :], 0.0)
            v = jnp.where(hvc[:, out, :] > kf, vr[k, :, here, :], 0.0)
            w, e = west_in(u, lane), east_in(v, lane, 1)
            um[k, :, here, :] = u
            vm[k, :, here, :] = v
            wu[k, :, here, :] = w
            ev[k, :, here, :] = e
            xu[k, :, out, :] = east_in(u, lane, 1) + w
            xv[k, :, out, :] = west_in(v, lane) + e
            p = pm[k, :, here, :]
            px[k, :, out, :] = east_in(p, lane, 1) - p
        return carry

    def momentum(k, r, tiles):
        kf = k.astype(F32)
        at = SUB + SUB * r
        here, above, below = slice(at, at + SUB), slice(at + 1, at + SUB + 1), slice(at - 1, at + SUB - 1)
        out = slice(SUB * r, SUB * r + SUB)
        u, un, w = um[k, tiles, here, :], um[k, tiles, above, :], wu[k, tiles, here, :]
        v, vs, e = vm[k, tiles, here, :], vm[k, tiles, below, :], ev[k, tiles, here, :]
        around_u = xu[k, tiles, out, :] + (un + um[k, tiles, below, :])
        around_v = xv[k, tiles, out, :] + (vs + vm[k, tiles, above, :])
        vbar = (v + vs) + (e + ev[k, tiles, below, :])
        ubar = (u + un) + (w + wu[k, tiles, above, :])
        py = pm[k, tiles, above, :] - pm[k, tiles, here, :]
        ut = KEEP * u + MIX * around_u + fu_ref[r] * vbar - px[k, tiles, out, :]
        vt = KEEP * v + MIX * around_v - fv_ref[r] * ubar - py
        ut = jnp.where(hue[tiles, here, :] > kf, ut, 0.0)
        vt = jnp.where(hve[tiles, here, :] > kf, vt, 0.0)
        u_out[k, tiles, out, :] = ut
        v_out[k, tiles, out, :] = vt
        for n, x in enumerate((u, v, ut, vt)):
            acc[n, tiles, out, :] += x

    inner, rim = slice(0, nt - 1), slice(nt - 1, nt)
    hue[0:nt, own, :] = huc[...]
    hve[0:nt, own, :] = hvc[...]
    step_loop(0, levels, 6, sides, 0)

    def inside(k, carry):
        for r in range(nr - 1):
            momentum(k, r, inner)
        return carry

    step_loop(0, levels, 3, lambda k, c: inside(k, east_fluxes(k, c)), 0)

    for c in along0:
        c.wait_recv()
    recv_ns(depth_up, depth_down)
    de[nt, own, :] = pltpu.roll(jnp.where((tall & 3) >= 2, fe0[own, :], fw0[own, :]), LANES - 2, 1)
    faces(SUB, end)


    def last_sides(k, carry):
        kf = k.astype(F32)
        u = jnp.where(hue[rim, own, :] > kf, ur[k, rim, own, :], 0.0)
        um[k, rim, own, :] = u
        xu[k, rim, :, :] = east_in(u, tall, 1) + wu[k, rim, own, :]
        here, out = slice(end - SUB, end), slice(rows - SUB, rows)
        v = jnp.where(hve[0:nt, here, :] > kf, vr[k, :, here, :], 0.0)
        e = east_in(v, lane, 1)
        vm[k, :, here, :] = v
        ev[k, :, here, :] = e
        xv[k, :, out, :] = west_in(v, lane) + e
        return carry

    def outside(k, carry):
        for r in range(nr - 1):
            momentum(k, r, rim)
        momentum(k, nr - 1, slice(0, nt))
        return carry

    step_loop(0, levels, 6, last_sides, 0)
    step_loop(0, levels, 4, outside, 0)
    spot8 = lax.shift_right_logical(tall, 3)

    def pack(fields):
        group = jnp.zeros((rows, LANES), F32)
        for n, f in enumerate(fields):
            x = jnp.where(tall < LANES // 2, flat[f, 0, own, :], flat[f, nt - 1, own, :])
            group = jnp.where(spot8 == n, pltpu.roll(x, 8 * n + 4, 1), group)
        return group

    def far(fields, strip, fe, fw):
        def rows_of(first):
            return flat.at[fields, :, pl.ds(first, NSUB), :]

        up = [cp2(rows_of(end - NSUB), rows_of(SUB - NSUB), lon, nth)]
        down = [cp2(rows_of(SUB), rows_of(end), lon, sth)]
        along, corner_up, corner_down = strips(cp2, strip, fe, fw, NSUB)
        return along, up + corner_up, down + corner_down

    cp2 = copier(send2, recv2)
    flat[SUM_U, :, own, :] = acc[0]
    flat[SUM_V, :, own, :] = acc[1]
    strip3[...] = pack(range(SOON))
    along3, up3, down3 = far(pl.ds(0, SOON), strip3, fe3, fw3)
    for c in along3:
        c.start()
    start_ns(up3, down3)

    wind_u = jnp.where(hue[0:nt, own, :] > 0.0, (TIME_STEP * WIND_FACTOR) * zt[...], 0.0)
    wind_v = jnp.where(hve[0:nt, own, :] > 0.0, (TIME_STEP * WIND_FACTOR) * mt[...], 0.0)
    u_out[0, :, 0:rows, :] += wind_u
    v_out[0, :, 0:rows, :] += wind_v
    flat[PUSH_U, :, own, :] = acc[2] - acc[0] + wind_u
    flat[PUSH_V, :, own, :] = acc[3] - acc[1] + wind_v

    recv_ns(corner_up0, corner_down0)
    for out in (slice(0, SUB), slice(end, end + SUB)):
        de[nt, out, :] = pltpu.roll(jnp.where((lane & 3) >= 2, fe0[out, :], fw0[out, :]), LANES - 2, 1)
    faces(0, SUB)
    faces(end - SUB, end + SUB)
    level = lax.shift_right_logical(tall, 3).astype(F32)

    def by_lane(at, one, two, five, six):
        return jnp.where(at == 1, one, jnp.where(at == 2, two, jnp.where(at == 5, five, six)))

    def column(ref, c, at, which=own, n=rows):
        return jnp.broadcast_to(ref[c, which, at:at + 1], (n, LANES))

    LAST = LANES - 1
    spot = tall & 7
    for r in range(0, end + SUB, SUB):
        here = slice(r, r + SUB)
        edge_b[here, :] = by_lane(lane & 7, *(column(ref, nt, at, here, SUB) for ref in (hue, hve) for at in (LAST, 0)))
    mend[...] = by_lane(spot, column(hue, nt - 1, LAST), column(hue, 0, 0), column(hve, nt - 1, LAST), column(hve, 0, 0))

    recv_ns(flow_up, flow_down)
    recv_ns([], press_down)
    top = lax.broadcasted_iota(jnp.int32, (SUB, LANES), 0) == 0

    def far_rows(k, carry):
        nu, nv, su, sv = carry
        kf = k.astype(F32)
        out = slice(end, end + SUB)
        u = jnp.where(hue[0:nt, out, :] > kf, ur[k, :, out, :], 0.0)
        v = jnp.where(hve[0:nt, out, :] > kf, vr[k, :, out, :], 0.0)
        edge_row = slice(end - 1, end + SUB - 1)
        du = jnp.where(hue[0:nt, edge_row, :] > kf, MIX * u, 0.0)
        dv = jnp.where(hve[0:nt, edge_row, :] > kf,
                       MIX * v - fv_north * (u + west_in(u, lane)) - pn[k], 0.0)
        rim_rows[k, 0] = du
        rim_rows[k, 1] = dv
        nu, nv = nu + du, nv + dv

        out = slice(SUB - 1, 2 * SUB - 1)
        u = jnp.where(hue[0:nt, out, :] > kf, ur[k, :, out, :], 0.0)
        v = jnp.where(hve[0:nt, out, :] > kf, vr[k, :, out, :], 0.0)
        edge_row = slice(SUB, 2 * SUB)
        du = jnp.where(hue[0:nt, edge_row, :] > kf,
                       MIX * u + fu_south * (v + east_in(v, lane, 1)), 0.0)
        dv = jnp.where(hve[0:nt, edge_row, :] > kf, MIX * v, 0.0)
        rim_rows[k, 2] = du
        rim_rows[k, 3] = dv
        return nu, nv, su + du, sv + dv

    nu, nv, su, sv = step_loop(0, levels, 4, far_rows, (zero,) * 4)
    for f, north, south in ((PUSH_U, nu, su), (PUSH_V, nv, sv)):
        north, south = jnp.where(top, north, 0.0), jnp.where(top, south, 0.0)
        flat[f, :, SUB:2 * SUB, :] += south
        flat[f, :, end - SUB:end, :] += pltpu.roll(north, SUB - 1, 1)


    for c in along_b + along_c:
        c.wait_recv()
    recv_ns(corner_up_b, corner_down_b)
    for r in range(0, end + SUB, SUB):
        here = slice(r, r + SUB)
        x = jnp.where((lane & 3) >= 2, fe_b[here, :], fw_b[here, :])
        edge_b[here, :] = jnp.where(edge_b[here, :] > lax.shift_right_logical(lane, 3).astype(F32), x, 0.0)
    x = edge_b[own, :]
    near = jnp.where((spot & 1) == 1, pltpu.roll(x, LAST, 1), pltpu.roll(x, 1, 1))
    above, below = slice(SUB + 1, end + 1), slice(SUB - 1, end - 1)
    turn_u = fu_ref[...].reshape(rows, LANES) * pltpu.roll(x + edge_b[below, :], LANES - 5, 1) - fe_c[...]
    turn_v = fv_ref[...].reshape(rows, LANES) * pltpu.roll(x + edge_b[above, :], 5, 1)
    extra = MIX * near + jnp.where(spot == 1, turn_u, 0.0) - jnp.where(spot == 6, turn_v, 0.0)
    extra = jnp.where(mend[...] > level, extra, 0.0)
    total = jnp.zeros((rows, LANES), F32)
    for k in range(levels):
        total = total + (pltpu.roll(extra, LANES - 8 * k, 1) if k else extra)
    total_u, total_v = pltpu.roll(total, LANES - 2, 1), pltpu.roll(total, LANES - 6, 1)
    for f, d in ((PUSH_U, total_u), (PUSH_V, total_v)):
        flat[f, 0, own, :] += jnp.where(tall == 0, d, 0.0)
        flat[f, nt - 1, own, :] += jnp.where(tall == LAST, d, 0.0)

    strip2[...] = pack((PUSH_U, PUSH_V))
    along2, up2, down2 = far(pl.ds(SOON, FLAT - SOON), strip2, fe2, fw2)
    start_ns(up2, down2)
    for c in along2:
        c.start()

    for k in range(levels):
        du = pltpu.roll(extra, LANES - 2 - 8 * k, 1)
        dv = pltpu.roll(extra, LANES - 6 - 8 * k, 1)
        for ref, d in ((u_out, du), (v_out, dv)):
            ref[k, 0, 0:rows, :] += jnp.where(tall == 0, d, 0.0)
            ref[k, nt - 1, 0:rows, :] += jnp.where(tall == LAST, d, 0.0)

    def rim_updates(k, carry):
        row = slice(rows - 1, rows + SUB - 1)
        for n, ref in enumerate((u_out, v_out)):
            ref[k, :, row, :] += jnp.where(top, rim_rows[k, n], 0.0)
            ref[k, :, 0:SUB, :] += jnp.where(top, rim_rows[k, 2 + n], 0.0)
        return carry

    step_loop(0, levels, 3, rim_updates, 0)

    recv_ns(tracer_up, tracer_down)

    def tracer_rows(k, carry):
        kf = k.astype(F32)
        for a in (0, end):
            out = slice(a, a + SUB)
            wet = de[0:nt, out, :] > kf
            tm[k, :, out, :] = jnp.where(wet, tr[k, :, out, :], 0.0)
            sm[k, :, out, :] = jnp.where(wet, sr[k, :, out, :], 0.0)
        vm[k, :, 0:SUB, :] = jnp.where(hve[0:nt, 0:SUB, :] > kf, vr[k, :, 0:SUB, :], 0.0)
        return carry

    step_loop(0, levels, 2, tracer_rows, 0)

    starts = list(range(SUB - 1, end - SUB, SUB)) + [end - SUB]

    def north_fluxes(k, carry):
        kf = k.astype(F32)
        for a in starts:
            here = slice(a, a + SUB)
            w0, w1, w2, w3 = face_weights(vm[k, :, here, :], hve[0:nt, here, :] > kf)
            for ref, to in ((tm, yt), (sm, ys)):
                to[k, :, here, :] = (
                    w0 * ref[k, :, here, :] + w1 * ref[k, :, a + 1:a + SUB + 1, :]
                    - w2 * ref[k, :, a + 2:a + SUB + 2, :] + w3 * ref[k, :, a - 1:a + SUB - 1, :])
        return carry

    step_loop(0, levels, 1, north_fluxes, 0)
    for c in along_a:
        c.wait_recv()

    q = tall & 3

    def speeds(x, limit):
        x = jnp.where((tall & 7) < 4, x, pltpu.roll(x, 4, 1))
        opening = limit > level
        return face_weights(jnp.where(opening, x, 0.0), opening)

    mine = strip_a[...]
    a = jnp.where(q < 2, mine, fe_a[...])
    b = jnp.where(q < 2, fw_a[...], mine)
    w0, w1, w2, w3 = speeds(strip_b[...], jnp.where(
        q == 0, column(hue, nt - 1, LANES - 2), jnp.where(q == 1, column(hue, nt - 1, LAST), column(hue, 0, 0))))
    b_west = pltpu.roll(b, 1, 1)
    flux = (jnp.where(q == 1, w0 * a + w1 * pltpu.roll(a, LANES - 1, 1) + w3 * pltpu.roll(a, 1, 1), 0.0)
            - w2 * pltpu.roll(a, LANES - 2, 1))
    flux = jnp.where(q < 2, flux, jnp.where(q == 2, w3 * b_west, 0.0))
    w0, w1, w2, w3 = speeds(fw_b[own, :], column(hue, nt, LAST))
    first = w0 * b + w1 * pltpu.roll(b, LANES - 1, 1) - w2 * pltpu.roll(b, LANES - 2, 1) + w3 * b_west
    mend[...] = flux - pltpu.roll(jnp.where(q == 1, first, flux), 1, 1)

    def mended(x, m):
        edge_lane = lane_of(m.shape)
        first = x[:1] - jnp.where(edge_lane < 2, m, 0.0)[None]
        last = x[-1:] - jnp.where(edge_lane >= LANES - 2, m, 0.0)[None]
        return jnp.concatenate([first, x[1:-1], last], axis=0)

    span = 2 * SUB if rows % (2 * SUB) == 0 else SUB
    long = lane_of((span, LANES))
    DIFF = TIME_STEP * STABILITY_FACTOR * BACKGROUND_MIX
    BASE = TIME_STEP * (BACKGROUND_MIX + CONVECTIVE_MIX)
    for r in range(0, rows, span):
        out = slice(r, r + span)
        here, below = slice(SUB + r, SUB + r + span), slice(SUB + r - 1, SUB + r + span - 1)

        def star(k):
            fx = xt[k, :, out, :]
            t = tm[k, :, here, :] - (fx - west_in(fx, long)) - (yt[k, :, here, :] - yt[k, :, below, :])
            fx = xs[k, :, out, :]
            s = sm[k, :, here, :] - (fx - west_in(fx, long)) - (ys[k, :, here, :] - ys[k, :, below, :])
            t = mended(t, pltpu.roll(mend[out, :], LANES - 2 - 8 * k, 1))
            s = mended(s, pltpu.roll(mend[out, :], LANES - 6 - 8 * k, 1))
            return t, s, HALINE_COEF * s - THERMAL_COEF * t

        def forward(k, carry):
            t, s, dens, lower, qt, qs = carry
            tn, sn, densn = star(k)
            rise = jnp.maximum(densn - dens, 0.0)
            e = 1.0 + STABILITY_FACTOR * rise
            n = jnp.where(de[0:nt, here, :] > k.astype(F32), BASE + DIFF * rise, 0.0)
            w = 1.0 / (e * lower + n)
            rat = n * w
            ew = e * w
            gt, gs = t + qt, s + qs
            t_out[k - 1, :, out, :] = gt * ew
            s_out[k - 1, :, out, :] = gs * ew
            ratio[k - 1, :, out, :] = rat
            return tn, sn, densn, 1.0 + rat * lower, rat * gt, rat * gs

        zero = jnp.zeros((nt, span, LANES), F32)
        carry = star(0) + (zero + 1.0, zero, zero)
        t, s, _, lower, qt, qs = step_loop(1, levels, 2, forward, carry)
        w = 1.0 / lower
        t, s = (t + qt) * w, (s + qs) * w
        t_out[levels - 1, :, out, :] = t
        s_out[levels - 1, :, out, :] = s

        def backward(i, carry):
            t, s = carry
            k = levels - 2 - i
            rat = ratio[k, :, out, :]
            t = t_out[k, :, out, :] + rat * t
            s = s_out[k, :, out, :] + rat * s
            t_out[k, :, out, :] = t
            s_out[k, :, out, :] = s
            return t, s

        step_loop(0, levels - 1, 1, backward, (t, s))

    count = rows + 2 * NSUB
    wide = slice(SUB - NSUB, end + NSUB)
    half = (lane_of((count, LANES)) & 7) >= 4

    def finish(fields, fe, fw):
        halo = jnp.where(half, fe[wide, :], fw[wide, :])
        for n, f in enumerate(fields):
            flat_out[f, nt, 0:count] = pltpu.roll(halo, LANES - 8 * n - 4, 1)
            flat_out[f, 0:nt, 0:NSUB, :] = flat[f, :, SUB - NSUB:SUB, :]
            flat_out[f, 0:nt, rows + NSUB:count, :] = flat[f, :, end:end + NSUB, :]

    for f in range(FLAT):
        flat_out[f, 0:nt, pl.ds(NSUB, rows), :] = flat[f, :, own, :]
    flat_out[DEEP, :, count:, :] = jnp.zeros((nt + 1, SUB, LANES), F32)
    for c in along3:
        c.wait_recv()
    recv_ns(up3, down3)
    finish(range(SOON), fe3, fw3)
    for c in along0 + along_a + along_b + along_c + along2 + along3:
        c.wait_send()
    sent_ns(depth_up + corner_up0 + flow_up + tracer_up + corner_up_b + up2 + up3,
            depth_down + corner_down0 + flow_down + tracer_down + corner_down_b + press_down + down2 + down3)
    for c in along2:
        c.wait_recv()
    recv_ns(up2, down2)
    finish((PUSH_U, PUSH_V), fe2, fw2)


def tail(
    t, s, ut, vt, flat,
    t_out, s_out, u_out, v_out, eta_out, tx_out, ty_out,
    eta, bu, bv, hx, hy, un, vn, cor, sem,
):
    levels, nt, rows, _ = t.shape
    count = rows + 2 * NSUB
    lane = lane_of((SUB, LANES))
    copies = []

    def put(src, dst):
        for c in range(nt):
            copies.append(pltpu.make_async_copy(
                src(c), dst(pl.ds(c * LANES, LANES)), sem.at[len(copies)]))
            copies[-1].start()

    put(lambda c: t.at[:, c], lambda d: t_out.at[:, :, d])
    put(lambda c: s.at[:, c], lambda d: s_out.at[:, :, d])

    for ref in (eta, bu, bv):
        ref[:, 0:SUB, :] = jnp.zeros((nt + 1, SUB, LANES), F32)
        ref[:, count + SUB:, :] = jnp.zeros((nt + 1, SUB, LANES), F32)
    tiles = range(0, count, SUB)
    eta[:, SUB:count + SUB, :] = flat[ETA, :, 0:count, :]
    bu[:, SUB:count + SUB, :] = flat[SUM_U, :, 0:count, :]
    bv[:, SUB:count + SUB, :] = flat[SUM_V, :, 0:count, :]
    for r in tiles:
        d = flat[DEEP, :, r:r + SUB, :]
        hx[:, r:r + SUB, :] = jnp.minimum(d, east_all(d, lane))
        hy[:, r:r + SUB, :] = jnp.minimum(d, flat[DEEP, :, r + 1:r + SUB + 1, :])
    for sub in range(NSUB):
        for r in tiles:
            here, below = slice(SUB + r, 2 * SUB + r), slice(SUB + r - 1, 2 * SUB + r - 1)
            x = bu[:, here, :]
            eta[:, here, :] = eta[:, here, :] - HEIGHT_FACTOR * (
                x - west_all(x, lane) + (bv[:, here, :] - bv[:, below, :]))
        for r in tiles:
            here, above = slice(SUB + r, 2 * SUB + r), slice(SUB + r + 1, 2 * SUB + r + 1)
            raw = slice(r, r + SUB)
            x = eta[:, here, :]
            bu[:, here, :] = (bu[:, here, :] + (1.0 / NSUB) * flat[PUSH_U, :, raw, :]
                              - SLOPE_FACTOR * hx[:, raw, :] * (east_all(x, lane) - x))
            bv[:, here, :] = (bv[:, here, :] + (1.0 / NSUB) * flat[PUSH_V, :, raw, :]
                              - SLOPE_FACTOR * hy[:, raw, :] * (eta[:, above, :] - x))
    mid = pl.ds(SUB + NSUB, rows)
    put(lambda c: eta.at[c, mid, :], lambda d: eta_out.at[:, d])
    put(lambda c: bu.at[c, mid, :], lambda d: tx_out.at[:, d])
    put(lambda c: bv.at[c, mid, :], lambda d: ty_out.at[:, d])

    for r in range(0, rows, SUB):
        raw = slice(NSUB + r, NSUB + r + SUB)
        hu, hv = hx[0:nt, raw, :], hy[0:nt, raw, :]
        done = slice(SUB + NSUB + r, 2 * SUB + NSUB + r)
        out = slice(r, r + SUB)
        cor[0, :, out, :] = (bu[0:nt, done, :] - (flat[PUSH_U, 0:nt, raw, :] + flat[SUM_U, 0:nt, raw, :])) / jnp.maximum(hu, 1.0)
        cor[1, :, out, :] = (bv[0:nt, done, :] - (flat[PUSH_V, 0:nt, raw, :] + flat[SUM_V, 0:nt, raw, :])) / jnp.maximum(hv, 1.0)
        cor[2, :, out, :] = hu
        cor[3, :, out, :] = hv

    part = -(-levels // CHUNKS)
    for first in range(0, levels, part):
        last = min(first + part, levels)

        @pl.loop(first, last)
        def _(k):
            kf = k.astype(F32)
            un[k] = jnp.where(cor[2] > kf, ut[k, :, 0:rows, :] + cor[0], 0.0)
            vn[k] = jnp.where(cor[3] > kf, vt[k, :, 0:rows, :] + cor[1], 0.0)

        span = pl.ds(first, last - first)
        put(lambda c: un.at[span, c], lambda d: u_out.at[span, :, d])
        put(lambda c: vn.at[span, c], lambda d: v_out.at[span, :, d])
    for c in copies:
        c.wait()


def body(*args):
    levels, rows, cols = args[0].shape
    nt = cols // LANES
    erows = rows + 2 * SUB
    count = rows + 2 * NSUB

    def vmem(*shape):
        return pltpu.VMEM(shape, F32)

    def out(*shape):
        return jax.ShapeDtypeStruct(shape, F32)

    block = pl.BlockSpec(memory_space=pltpu.VMEM)
    far = pl.BlockSpec(memory_space=pltpu.HBM)
    raw = vmem(levels, nt, erows, LANES)
    own = vmem(levels, nt, rows, LANES)
    ints = pltpu.VMEM((nt, rows, LANES), jnp.int32)
    n1, n2 = 2 + 8 + 1 + 6 + 4 + 3, 2 * (2 + 6)
    cube = (levels, nt, rows, LANES)
    parts = pl.pallas_call(
        functools.partial(kernel, rows * lax.axis_size("lat")),
        out_shape=(out(*cube),) * 2 + (out(levels, nt, rows + SUB, LANES),) * 2 + (out(FLAT, nt + 1, count + SUB, LANES),),
        in_specs=[far] * 9,
        out_specs=(block,) * 5,
        scratch_shapes=(
            [raw] * 11 + [own] * 3 + [vmem(nt, rows, LANES)] * 2
            + [vmem(nt, rows + SUB, LANES), own, own, raw, raw, own]
            + [vmem(nt, rows, LANES)] * 2 + [ints] * 2
            + [vmem(nt + 1, erows + SUB, LANES)] + [vmem(nt + 1, erows, LANES)] * 2
            + [vmem(FLAT, nt, erows, LANES)]
            + [vmem(rows // SUB, SUB, LANES)] * 2
            + [vmem(rows, LANES), vmem(erows, LANES), vmem(erows, LANES)]
            + [vmem(rows, LANES)] * 3
            + [vmem(rows, LANES), vmem(erows, LANES), vmem(erows, LANES)]
            + [vmem(rows, LANES)] * 2
            + [vmem(rows, LANES), vmem(erows, LANES), vmem(erows, LANES)] * 2
            + [vmem(rows, LANES)]
            + [vmem(erows, LANES), vmem(4, nt, rows, LANES), vmem(levels, nt, SUB, LANES),
               vmem(levels, 4, nt, SUB, LANES)]
            + [pltpu.SemaphoreType.DMA((9 * nt,))]
            + [pltpu.SemaphoreType.DMA((n1,))] * 2
            + [pltpu.SemaphoreType.DMA((n2,))] * 2
        ),
        compiler_params=pltpu.CompilerParams(
            collective_id=0, has_side_effects=True, vmem_limit_bytes=32 * 1024 * 1024),
    )(*[pltpu.with_memory_space_constraint(a, pltpu.HBM) for a in args])
    cube, plane = (levels, rows, cols), (rows, cols)
    return pl.pallas_call(
        tail,
        out_shape=(pltpu.HBM(cube, F32),) * 4 + (pltpu.HBM(plane, F32),) * 3,
        in_specs=[block] * 5,
        out_specs=(far,) * 7,
        scratch_shapes=(
            [vmem(nt + 1, count + 2 * SUB, LANES)] * 3 + [vmem(nt + 1, count, LANES)] * 2
            + [own, own, vmem(4, nt, rows, LANES)]
            + [pltpu.SemaphoreType.DMA(((5 + 2 * CHUNKS) * nt,))]
        ),
        compiler_params=pltpu.CompilerParams(vmem_limit_bytes=32 * 1024 * 1024),
    )(*parts)


def solution(mesh):
    cube, plane = P(None, "lat", "lon"), P("lat", "lon")
    return jax.shard_map(
        body,
        mesh=mesh,
        in_specs=(cube,) * 4 + (plane,) * 5,
        out_specs=(cube,) * 4 + (plane,) * 3,
        check_vma=False,
    )
```

```python
import functools

import jax
import jax.numpy as jnp
from jax import lax
from jax.experimental import pallas as pl
from jax.experimental.pallas import tpu as pltpu
from jax.sharding import PartitionSpec as P

NSUB = 4
TIME_STEP = 0.4
TRACER_DIFF = 0.05
MOMENTUM_DIFF = 0.05
BOTTOM_DRAG = 0.05
WIND_FACTOR = 0.5
CORIOLIS_SCALE = 0.5
LATITUDE_SPAN = 2.6
GRAVITY_FACTOR = 0.3
THERMAL_COEF = 0.2
HALINE_COEF = 0.8
BACKGROUND_MIX = 0.05
CONVECTIVE_MIX = 1.5
STABILITY_FACTOR = 5.0
HEIGHT_FACTOR = 0.2
SLOPE_FACTOR = 0.15

LANES = 128
SUB = 8
FLAT = 6
ETA, SUM_U, SUM_V, DEEP, PUSH_U, PUSH_V = range(FLAT)
SOON = 4
CHUNKS = 3
MESH = pl.DeviceIdType.MESH
F32 = jnp.float32


def lane_of(shape):
    return lax.broadcasted_iota(jnp.int32, shape, len(shape) - 1)


def east(x, lane, s=1):
    r = pltpu.roll(x, LANES - s, 2)
    return jnp.where(lane < LANES - s, r[:-1], r[1:])


def west(x, lane):
    r = pltpu.roll(x, 1, 2)
    return jnp.where(lane >= 1, r[:-1], jnp.concatenate([r[-1:], r[:-2]], axis=0))


def east_all(x, lane, s=1):
    r = pltpu.roll(x, LANES - s, 2)
    return jnp.where(lane < LANES - s, r, jnp.concatenate([r[1:], r[:1]], axis=0))


def west_all(x, lane):
    r = pltpu.roll(x, 1, 2)
    return jnp.where(lane >= 1, r, jnp.concatenate([r[-1:], r[:-1]], axis=0))


def step_loop(first, last, unroll, body, carry):
    n = (last - first) // unroll

    def group(g, c):
        for i in range(unroll):
            c = body(first + g * unroll + i, c)
        return c

    carry = lax.fori_loop(0, n, group, carry)
    for k in range(first + n * unroll, last):
        carry = body(jnp.int32(k), carry)
    return carry


def east_in(x, lane, s):
    r = pltpu.roll(x, LANES - s, 2)
    beyond = jnp.zeros_like(r[:1])
    beyond = jnp.concatenate([r[1:], beyond], axis=0) if x.shape[0] > 1 else beyond
    return jnp.where(lane < LANES - s, r, beyond)


def west_in(x, lane):
    r = pltpu.roll(x, 1, 2)
    return jnp.where(lane >= 1, r, jnp.concatenate([jnp.zeros_like(r[:1]), r[:-1]], axis=0))


def face_weights(speed, opening):
    p = speed * (TIME_STEP / 12.0)
    q = jnp.abs(p)
    m = 3.0 * q - jnp.where(opening, TIME_STEP * TRACER_DIFF, 0.0)
    p7 = 7.0 * p
    return p7 - m, p7 + m, p + q, q - p


def kernel(
    lat_total,
    t_in, s_in, u_in, v_in, eta_in, zt_in, mt_in, wi_in, bi_in,
    t_out, s_out, u_out, v_out, flat_out,
    tr, sr, ur, vr, tm, sm, um, vm, pm, wu, ev, xu, xv, px, huc, hvc, dz, xt, xs, yt, ys, ratio,
    zt, mt, wi, bi, de, hue, hve, flat, fu_ref, fv_ref,
    strip0, fe0, fw0, strip_a, fe_a, fw_a, strip_b, fe_b, fw_b, strip_c, fe_c,
    strip2, fe2, fw2, strip3, fe3, fw3, mend, edge_b, acc, pn, rim_rows,
    load_sem, send1, recv1, send2, recv2,
):
    levels, nt, rows, _ = t_out.shape
    end = SUB + rows
    zero = jnp.zeros((nt, SUB, LANES), F32)
    nr = rows // SUB
    lon, lat = lax.axis_index("lon"), lax.axis_index("lat")
    nlon, nlat = lax.axis_size("lon"), lax.axis_size("lat")
    wst, est = lax.rem(lon + nlon - 1, nlon), lax.rem(lon + 1, nlon)
    nth, sth = lax.rem(lat + 1, nlat), lax.rem(lat + nlat - 1, nlat)
    has_n, has_s = lat < nlat - 1, lat > 0
    own = pl.ds(SUB, rows)

    barrier = pltpu.get_barrier_semaphore()

    def greet(lo, la):
        pl.semaphore_signal(barrier, inc=1, device_id=(lo, la), device_id_type=MESH)

    greet(wst, lat)
    greet(est, lat)

    @pl.when(has_n)
    def _():
        greet(wst, nth)
        greet(lon, nth)
        greet(est, nth)

    @pl.when(has_s)
    def _():
        greet(wst, sth)
        greet(lon, sth)
        greet(est, sth)

    loads = []

    def load(src, dst):
        group = []
        for c in range(nt):
            cols = pl.ds(c * LANES, LANES)
            group.append(pltpu.make_async_copy(
                src(cols), dst(c), load_sem.at[len(loads) * nt + c]))
            group[-1].start()
        loads.append(group)
        return group

    ld_wi = load(lambda s: wi_in.at[:, s], lambda c: wi.at[c])
    ld_bi = load(lambda s: bi_in.at[:, s], lambda c: bi.at[c])
    ld_u = load(lambda s: u_in.at[:, :, s], lambda c: ur.at[:, c, own, :])
    ld_v = load(lambda s: v_in.at[:, :, s], lambda c: vr.at[:, c, own, :])
    ld_t = load(lambda s: t_in.at[:, :, s], lambda c: tr.at[:, c, own, :])
    ld_s = load(lambda s: s_in.at[:, :, s], lambda c: sr.at[:, c, own, :])
    ld_e = load(lambda s: eta_in.at[:, s], lambda c: flat.at[ETA, c, own, :])
    ld_z = load(lambda s: zt_in.at[:, s], lambda c: zt.at[c])
    ld_m = load(lambda s: mt_in.at[:, s], lambda c: mt.at[c])

    def arrived(*groups):
        for g in groups:
            for c in g:
                c.wait()

    def clear(first):
        beyond = slice(first, first + SUB)
        de[:, beyond, :] = jnp.zeros((nt + 1, SUB, LANES), F32)
        for ref in (fe0, fw0, fe_b, fw_b, fe2, fw2, fe3, fw3):
            ref[beyond, :] = jnp.zeros((SUB, LANES), F32)
        for f in range(FLAT):
            flat[f, :, beyond, :] = jnp.zeros((nt, SUB, LANES), F32)

    @pl.when(jnp.logical_not(has_s))
    def _():
        clear(0)

    @pl.when(jnp.logical_not(has_n))
    def _():
        clear(end)

    def copier(send, recv):
        made = []

        def cp(src, dst, lo, la):
            n = len(made)
            made.append(pltpu.make_async_remote_copy(
                src_ref=src, dst_ref=dst, send_sem=send.at[n], recv_sem=recv.at[n],
                device_id=(lo, la), device_id_type=MESH))
            return made[-1]

        return cp

    def start_ns(up, down):
        @pl.when(has_n)
        def _():
            for c in up:
                c.start()

        @pl.when(has_s)
        def _():
            for c in down:
                c.start()

    def recv_ns(up, down):
        @pl.when(has_s)
        def _():
            for c in up:
                c.wait_recv()

        @pl.when(has_n)
        def _():
            for c in down:
                c.wait_recv()

    def sent_ns(up, down):
        @pl.when(has_n)
        def _():
            for c in up:
                c.wait_send()

        @pl.when(has_s)
        def _():
            for c in down:
                c.wait_send()

    cp = copier(send1, recv1)

    def rows_up(ref, n, at):
        return cp(at(ref, end - n, n), at(ref, SUB - n, n), lon, nth)

    def rows_down(ref, n, at):
        return cp(at(ref, SUB, n), at(ref, end, n), lon, sth)

    def cube_rows(ref, first, n):
        return ref.at[:, 0:nt, pl.ds(first, n), :]

    def plane_rows(ref, first, n):
        return ref.at[0:nt, pl.ds(first, n), :]

    depth_up, depth_down = [rows_up(de, 2, plane_rows)], [rows_down(de, 2, plane_rows)]
    flow_up = [rows_up(r, 1, cube_rows) for r in (ur, vr)]
    flow_down = [rows_down(r, 1, cube_rows) for r in (ur, vr)]
    tracer_up = [rows_up(r, 2, cube_rows) for r in (tr, sr)]
    tracer_down = [rows_down(r, 2, cube_rows) for r in (tr, sr)]
    press_down = [cp(cube_rows(pm, SUB, 1), cube_rows(pn, 0, 1), lon, sth)]

    def strips(cp, strip, fe, fw, n):
        def at(ref, first, size):
            return ref.at[pl.ds(first, size), :]

        along = [cp(at(strip, 0, rows), at(fe, SUB, rows), wst, lat),
                 cp(at(strip, 0, rows), at(fw, SUB, rows), est, lat)]
        up = [cp(at(strip, rows - n, n), at(fe, SUB - n, n), wst, nth),
              cp(at(strip, rows - n, n), at(fw, SUB - n, n), est, nth)]
        down = [cp(at(strip, 0, n), at(fe, end, n), wst, sth),
                cp(at(strip, 0, n), at(fw, end, n), est, sth)]
        return along, up, down

    along0, corner_up0, corner_down0 = strips(
        cp, strip0, fe0, fw0, 2)
    along_b = [cp(strip_b, fe_b.at[own, :], wst, lat), cp(strip_b, fw_b.at[own, :], est, lat)]
    corner_up_b = [cp(strip_b.at[pl.ds(rows - 1, 1), :], fe_b.at[pl.ds(SUB - 1, 1), :], wst, nth)]
    corner_down_b = [cp(strip_b.at[pl.ds(0, 1), :], fw_b.at[pl.ds(end, 1), :], est, sth)]
    along_a = [cp(strip_a, fe_a, wst, lat), cp(strip_a, fw_a, est, lat)]
    along_c = [cp(strip_c, fe_c, wst, lat)]

    lane = lane_of((SUB, LANES))
    tall = lane_of((rows, LANES))

    for k in range(levels):
        for ref in (um, vm):
            ref[k, :, 0:SUB, :] = zero
            ref[k, :, end:, :] = zero
        pm[k, :, end:, :] = zero
        wu[k, :, end:, :] = zero
        ev[k, :, 0:SUB, :] = zero
    acc[...] = jnp.zeros_like(acc)

    sub = lax.broadcasted_iota(jnp.int32, (SUB, LANES), 0)
    j = (lat * rows + sub + SUB * lax.rem(lane, nr)).astype(F32)
    j = j + jnp.where(lane < LANES // 2, 0.5, 1.0)
    f = CORIOLIS_SCALE * jnp.sin(LATITUDE_SPAN * (j / lat_total - 0.5)) * (0.25 * TIME_STEP)
    for r in range(nr):
        fu_ref[r] = jnp.broadcast_to(f[:, r:r + 1], (SUB, LANES))
        at = LANES // 2 - (LANES // 2) % nr + nr + r
        fv_ref[r] = jnp.broadcast_to(f[:, at:at + 1], (SUB, LANES))
    fu_south = jnp.broadcast_to(f[0:1, 0:1], (SUB, LANES))
    fv_north = jnp.broadcast_to(f[SUB - 1:SUB, at:at + 1], (SUB, LANES))

    def edge(first, last, p):
        return pltpu.roll(jnp.where(tall < LANES // 2, first, last), 4 * p + 2, 1)

    arrived(ld_wi, ld_bi)
    depth = (wi[...] * bi[...]).astype(F32)
    de[0:nt, own, :] = depth
    strip0[...] = edge(depth[0], depth[nt - 1], 0)
    pl.semaphore_wait(barrier, 2 + 3 * has_n.astype(jnp.int32) + 3 * has_s.astype(jnp.int32))
    for c in along0:
        c.start()
    start_ns(depth_up + corner_up0, depth_down + corner_down0)
    for n, group in enumerate((ld_u, ld_v)):
        arrived(group)
        start_ns(flow_up[n:n + 1], flow_down[n:n + 1])

    place = lax.shift_right_logical(tall, 2)
    group = jnp.zeros((rows, LANES), F32)
    for k in range(levels):
        for n, ref in enumerate((ur, vr)):
            group = jnp.where(place == 2 * k + n, edge(ref[k, 0, own, :], ref[k, nt - 1, own, :], 2 * k + n), group)
    strip_b[...] = group
    for c in along_b:
        c.start()
    start_ns(corner_up_b, corner_down_b)

    HALF = 0.5 * GRAVITY_FACTOR * TIME_STEP
    arrived(ld_t, ld_s)
    group = jnp.zeros((rows, LANES), F32)
    total = jnp.zeros((nt, rows, LANES), F32)
    for k in range(levels):
        wet = de[0:nt, own, :] > k
        t = jnp.where(wet, tr[k, :, own, :], 0.0)
        s = jnp.where(wet, sr[k, :, own, :], 0.0)
        tm[k, :, own, :] = t
        sm[k, :, own, :] = s
        h = (HALF * HALINE_COEF) * s - (HALF * THERMAL_COEF) * t
        p = total + h
        total = p + h
        pm[k, :, own, :] = p
        group = jnp.where(tall == 8 * k + 1, pltpu.roll(p[0], 8 * k + 1, 1), group)
    strip_c[...] = group
    start_ns([], press_down)
    for c in along_c:
        c.start()
    start_ns(tracer_up, tracer_down)
    group = jnp.zeros((rows, LANES), F32)
    for k in range(levels):
        for n, ref in enumerate((tm, sm)):
            group = jnp.where(place == 2 * k + n, edge(ref[k, 0, own, :], ref[k, nt - 1, own, :], 2 * k + n), group)
    strip_a[...] = group
    for c in along_a:
        c.start()
    arrived(ld_e, ld_z, ld_m)
    flat[DEEP, :, own, :] = depth

    def faces(first, last):
        for r in range(first, last, SUB):
            d = de[:, r:r + SUB, :]
            hue[:, r:r + SUB, :] = jnp.minimum(d, east_all(d, lane))
            hve[:, r:r + SUB, :] = jnp.minimum(d, de[:, r + 1:r + SUB + 1, :])

    dz[:, 0:rows, :] = depth
    dz[:, rows:, :] = zero
    for r in range(SUB, end, SUB):
        d = dz[:, r - SUB:r, :]
        huc[:, r - SUB:r, :] = jnp.minimum(d, east_in(d, lane, 1))
        hvc[:, r - SUB:r, :] = jnp.minimum(d, dz[:, r - SUB + 1:r + 1, :])

    def east_fluxes(k, carry):
        kf = k.astype(F32)
        for r in range(SUB, end, SUB):
            here = slice(r, r + SUB)
            opening = huc[:, r - SUB:r, :] > kf
            w0, w1, w2, w3 = face_weights(jnp.where(opening, ur[k, :, here, :], 0.0), opening)
            for ref, to in ((tm, xt), (sm, xs)):
                c = ref[k, :, here, :]
                to[k, :, r - SUB:r, :] = (w0 * c + w1 * east_in(c, lane, 1)
                                          - w2 * east_in(c, lane, 2) + w3 * west_in(c, lane))
        return carry

    MIX = TIME_STEP * MOMENTUM_DIFF
    KEEP = 1.0 - TIME_STEP * BOTTOM_DRAG - 4.0 * MIX

    def sides(k, carry):
        kf = k.astype(F32)
        for r in range(0, rows, SUB):
            here, out = slice(SUB + r, 2 * SUB + r), slice(r, r + SUB)
            u = jnp.where(huc[:, out, :] > kf, ur[k, :, here, :], 0.0)
            v = jnp.where(hvc[:, out, :] > kf, vr[k, :, here, :], 0.0)
            w, e = west_in(u, lane), east_in(v, lane, 1)
            um[k, :, here, :] = u
            vm[k, :, here, :] = v
            wu[k, :, here, :] = w
            ev[k, :, here, :] = e
            xu[k, :, out, :] = east_in(u, lane, 1) + w
            xv[k, :, out, :] = west_in(v, lane) + e
            p = pm[k, :, here, :]
            px[k, :, out, :] = east_in(p, lane, 1) - p
        return carry

    def momentum(k, r, tiles):
        kf = k.astype(F32)
        at = SUB + SUB * r
        here, above, below = slice(at, at + SUB), slice(at + 1, at + SUB + 1), slice(at - 1, at + SUB - 1)
        out = slice(SUB * r, SUB * r + SUB)
        u, un, w = um[k, tiles, here, :], um[k, tiles, above, :], wu[k, tiles, here, :]
        v, vs, e = vm[k, tiles, here, :], vm[k, tiles, below, :], ev[k, tiles, here, :]
        around_u = xu[k, tiles, out, :] + (un + um[k, tiles, below, :])
        around_v = xv[k, tiles, out, :] + (vs + vm[k, tiles, above, :])
        vbar = (v + vs) + (e + ev[k, tiles, below, :])
        ubar = (u + un) + (w + wu[k, tiles, above, :])
        py = pm[k, tiles, above, :] - pm[k, tiles, here, :]
        ut = KEEP * u + MIX * around_u + fu_ref[r] * vbar - px[k, tiles, out, :]
        vt = KEEP * v + MIX * around_v - fv_ref[r] * ubar - py
        ut = jnp.where(hue[tiles, here, :] > kf, ut, 0.0)
        vt = jnp.where(hve[tiles, here, :] > kf, vt, 0.0)
        u_out[k, tiles, out, :] = ut
        v_out[k, tiles, out, :] = vt
        for n, x in enumerate((u, v, ut, vt)):
            acc[n, tiles, out, :] += x

    inner, rim = slice(0, nt - 1), slice(nt - 1, nt)
    hue[0:nt, own, :] = huc[...]
    hve[0:nt, own, :] = hvc[...]
    step_loop(0, levels, 6, sides, 0)

    def inside(k, carry):
        for r in range(nr - 1):
            momentum(k, r, inner)
        return carry

    step_loop(0, levels, 3, lambda k, c: inside(k, east_fluxes(k, c)), 0)

    for c in along0:
        c.wait_recv()
    recv_ns(depth_up, depth_down)
    de[nt, own, :] = pltpu.roll(jnp.where((tall & 3) >= 2, fe0[own, :], fw0[own, :]), LANES - 2, 1)
    faces(SUB, end)


    def last_sides(k, carry):
        kf = k.astype(F32)
        u = jnp.where(hue[rim, own, :] > kf, ur[k, rim, own, :], 0.0)
        um[k, rim, own, :] = u
        xu[k, rim, :, :] = east_in(u, tall, 1) + wu[k, rim, own, :]
        here, out = slice(end - SUB, end), slice(rows - SUB, rows)
        v = jnp.where(hve[0:nt, here, :] > kf, vr[k, :, here, :], 0.0)
        e = east_in(v, lane, 1)
        vm[k, :, here, :] = v
        ev[k, :, here, :] = e
        xv[k, :, out, :] = west_in(v, lane) + e
        return carry

    def outside(k, carry):
        for r in range(nr - 1):
            momentum(k, r, rim)
        momentum(k, nr - 1, slice(0, nt))
        return carry

    step_loop(0, levels, levels, last_sides, 0)
    step_loop(0, levels, levels, outside, 0)
    spot8 = lax.shift_right_logical(tall, 3)

    def pack(fields):
        group = jnp.zeros((rows, LANES), F32)
        for n, f in enumerate(fields):
            x = jnp.where(tall < LANES // 2, flat[f, 0, own, :], flat[f, nt - 1, own, :])
            group = jnp.where(spot8 == n, pltpu.roll(x, 8 * n + 4, 1), group)
        return group

    def far(fields, strip, fe, fw):
        def rows_of(first):
            return flat.at[fields, :, pl.ds(first, NSUB), :]

        up = [cp2(rows_of(end - NSUB), rows_of(SUB - NSUB), lon, nth)]
        down = [cp2(rows_of(SUB), rows_of(end), lon, sth)]
        along, corner_up, corner_down = strips(cp2, strip, fe, fw, NSUB)
        return along, up + corner_up, down + corner_down

    cp2 = copier(send2, recv2)
    flat[SUM_U, :, own, :] = acc[0]
    flat[SUM_V, :, own, :] = acc[1]
    strip3[...] = pack(range(SOON))
    along3, up3, down3 = far(pl.ds(0, SOON), strip3, fe3, fw3)
    for c in along3:
        c.start()
    start_ns(up3, down3)

    wind_u = jnp.where(hue[0:nt, own, :] > 0.0, (TIME_STEP * WIND_FACTOR) * zt[...], 0.0)
    wind_v = jnp.where(hve[0:nt, own, :] > 0.0, (TIME_STEP * WIND_FACTOR) * mt[...], 0.0)
    u_out[0, :, 0:rows, :] += wind_u
    v_out[0, :, 0:rows, :] += wind_v
    flat[PUSH_U, :, own, :] = acc[2] - acc[0] + wind_u
    flat[PUSH_V, :, own, :] = acc[3] - acc[1] + wind_v

    recv_ns(corner_up0, corner_down0)
    for out in (slice(0, SUB), slice(end, end + SUB)):
        de[nt, out, :] = pltpu.roll(jnp.where((lane & 3) >= 2, fe0[out, :], fw0[out, :]), LANES - 2, 1)
    faces(0, SUB)
    faces(end - SUB, end + SUB)
    level = lax.shift_right_logical(tall, 3).astype(F32)

    def by_lane(at, one, two, five, six):
        return jnp.where(at == 1, one, jnp.where(at == 2, two, jnp.where(at == 5, five, six)))

    def column(ref, c, at, which=own, n=rows):
        return jnp.broadcast_to(ref[c, which, at:at + 1], (n, LANES))

    LAST = LANES - 1
    spot = tall & 7
    for r in range(0, end + SUB, SUB):
        here = slice(r, r + SUB)
        edge_b[here, :] = by_lane(lane & 7, *(column(ref, nt, at, here, SUB) for ref in (hue, hve) for at in (LAST, 0)))
    mend[...] = by_lane(spot, column(hue, nt - 1, LAST), column(hue, 0, 0), column(hve, nt - 1, LAST), column(hve, 0, 0))

    recv_ns(flow_up, flow_down)
    recv_ns([], press_down)
    top = lax.broadcasted_iota(jnp.int32, (SUB, LANES), 0) == 0

    def far_rows(k, carry):
        nu, nv, su, sv = carry
        kf = k.astype(F32)
        out = slice(end, end + SUB)
        u = jnp.where(hue[0:nt, out, :] > kf, ur[k, :, out, :], 0.0)
        v = jnp.where(hve[0:nt, out, :] > kf, vr[k, :, out, :], 0.0)
        edge_row = slice(end - 1, end + SUB - 1)
        du = jnp.where(hue[0:nt, edge_row, :] > kf, MIX * u, 0.0)
        dv = jnp.where(hve[0:nt, edge_row, :] > kf,
                       MIX * v - fv_north * (u + west_in(u, lane)) - pn[k], 0.0)
        rim_rows[k, 0] = du
        rim_rows[k, 1] = dv
        nu, nv = nu + du, nv + dv

        out = slice(SUB - 1, 2 * SUB - 1)
        u = jnp.where(hue[0:nt, out, :] > kf, ur[k, :, out, :], 0.0)
        v = jnp.where(hve[0:nt, out, :] > kf, vr[k, :, out, :], 0.0)
        edge_row = slice(SUB, 2 * SUB)
        du = jnp.where(hue[0:nt, edge_row, :] > kf,
                       MIX * u + fu_south * (v + east_in(v, lane, 1)), 0.0)
        dv = jnp.where(hve[0:nt, edge_row, :] > kf, MIX * v, 0.0)
        rim_rows[k, 2] = du
        rim_rows[k, 3] = dv
        return nu, nv, su + du, sv + dv

    nu, nv, su, sv = step_loop(0, levels, levels, far_rows, (zero,) * 4)
    for f, north, south in ((PUSH_U, nu, su), (PUSH_V, nv, sv)):
        north, south = jnp.where(top, north, 0.0), jnp.where(top, south, 0.0)
        flat[f, :, SUB:2 * SUB, :] += south
        flat[f, :, end - SUB:end, :] += pltpu.roll(north, SUB - 1, 1)


    for c in along_b + along_c:
        c.wait_recv()
    recv_ns(corner_up_b, corner_down_b)
    for r in range(0, end + SUB, SUB):
        here = slice(r, r + SUB)
        x = jnp.where((lane & 3) >= 2, fe_b[here, :], fw_b[here, :])
        edge_b[here, :] = jnp.where(edge_b[here, :] > lax.shift_right_logical(lane, 3).astype(F32), x, 0.0)
    x = edge_b[own, :]
    near = jnp.where((spot & 1) == 1, pltpu.roll(x, LAST, 1), pltpu.roll(x, 1, 1))
    above, below = slice(SUB + 1, end + 1), slice(SUB - 1, end - 1)
    turn_u = fu_ref[...].reshape(rows, LANES) * pltpu.roll(x + edge_b[below, :], LANES - 5, 1) - fe_c[...]
    turn_v = fv_ref[...].reshape(rows, LANES) * pltpu.roll(x + edge_b[above, :], 5, 1)
    extra = MIX * near + jnp.where(spot == 1, turn_u, 0.0) - jnp.where(spot == 6, turn_v, 0.0)
    extra = jnp.where(mend[...] > level, extra, 0.0)
    total = jnp.zeros((rows, LANES), F32)
    for k in range(levels):
        total = total + (pltpu.roll(extra, LANES - 8 * k, 1) if k else extra)
    total_u, total_v = pltpu.roll(total, LANES - 2, 1), pltpu.roll(total, LANES - 6, 1)
    for f, d in ((PUSH_U, total_u), (PUSH_V, total_v)):
        flat[f, 0, own, :] += jnp.where(tall == 0, d, 0.0)
        flat[f, nt - 1, own, :] += jnp.where(tall == LAST, d, 0.0)

    strip2[...] = pack((PUSH_U, PUSH_V))
    along2, up2, down2 = far(pl.ds(SOON, FLAT - SOON), strip2, fe2, fw2)
    start_ns(up2, down2)
    for c in along2:
        c.start()

    for k in range(levels):
        du = pltpu.roll(extra, LANES - 2 - 8 * k, 1)
        dv = pltpu.roll(extra, LANES - 6 - 8 * k, 1)
        for ref, d in ((u_out, du), (v_out, dv)):
            ref[k, 0, 0:rows, :] += jnp.where(tall == 0, d, 0.0)
            ref[k, nt - 1, 0:rows, :] += jnp.where(tall == LAST, d, 0.0)

    def rim_updates(k, carry):
        row = slice(rows - 1, rows + SUB - 1)
        for n, ref in enumerate((u_out, v_out)):
            ref[k, :, row, :] += jnp.where(top, rim_rows[k, n], 0.0)
            ref[k, :, 0:SUB, :] += jnp.where(top, rim_rows[k, 2 + n], 0.0)
        return carry

    step_loop(0, levels, 3, rim_updates, 0)

    recv_ns(tracer_up, tracer_down)

    def tracer_rows(k, carry):
        kf = k.astype(F32)
        for a in (0, end):
            out = slice(a, a + SUB)
            wet = de[0:nt, out, :] > kf
            tm[k, :, out, :] = jnp.where(wet, tr[k, :, out, :], 0.0)
            sm[k, :, out, :] = jnp.where(wet, sr[k, :, out, :], 0.0)
        vm[k, :, 0:SUB, :] = jnp.where(hve[0:nt, 0:SUB, :] > kf, vr[k, :, 0:SUB, :], 0.0)
        return carry

    step_loop(0, levels, 2, tracer_rows, 0)

    starts = list(range(SUB - 1, end - SUB, SUB)) + [end - SUB]

    def north_fluxes(k, carry):
        kf = k.astype(F32)
        for a in starts:
            here = slice(a, a + SUB)
            w0, w1, w2, w3 = face_weights(vm[k, :, here, :], hve[0:nt, here, :] > kf)
            for ref, to in ((tm, yt), (sm, ys)):
                to[k, :, here, :] = (
                    w0 * ref[k, :, here, :] + w1 * ref[k, :, a + 1:a + SUB + 1, :]
                    - w2 * ref[k, :, a + 2:a + SUB + 2, :] + w3 * ref[k, :, a - 1:a + SUB - 1, :])
        return carry

    step_loop(0, levels, 1, north_fluxes, 0)
    for c in along_a:
        c.wait_recv()

    q = tall & 3

    def speeds(x, limit):
        x = jnp.where((tall & 7) < 4, x, pltpu.roll(x, 4, 1))
        opening = limit > level
        return face_weights(jnp.where(opening, x, 0.0), opening)

    mine = strip_a[...]
    a = jnp.where(q < 2, mine, fe_a[...])
    b = jnp.where(q < 2, fw_a[...], mine)
    w0, w1, w2, w3 = speeds(strip_b[...], jnp.where(
        q == 0, column(hue, nt - 1, LANES - 2), jnp.where(q == 1, column(hue, nt - 1, LAST), column(hue, 0, 0))))
    b_west = pltpu.roll(b, 1, 1)
    flux = (jnp.where(q == 1, w0 * a + w1 * pltpu.roll(a, LANES - 1, 1) + w3 * pltpu.roll(a, 1, 1), 0.0)
            - w2 * pltpu.roll(a, LANES - 2, 1))
    flux = jnp.where(q < 2, flux, jnp.where(q == 2, w3 * b_west, 0.0))
    w0, w1, w2, w3 = speeds(fw_b[own, :], column(hue, nt, LAST))
    first = w0 * b + w1 * pltpu.roll(b, LANES - 1, 1) - w2 * pltpu.roll(b, LANES - 2, 1) + w3 * b_west
    mend[...] = flux - pltpu.roll(jnp.where(q == 1, first, flux), 1, 1)

    def mended(x, m):
        edge_lane = lane_of(m.shape)
        first = x[:1] - jnp.where(edge_lane < 2, m, 0.0)[None]
        last = x[-1:] - jnp.where(edge_lane >= LANES - 2, m, 0.0)[None]
        return jnp.concatenate([first, x[1:-1], last], axis=0)

    span = 2 * SUB if rows % (2 * SUB) == 0 else SUB
    long = lane_of((span, LANES))
    DIFF = TIME_STEP * STABILITY_FACTOR * BACKGROUND_MIX
    BASE = TIME_STEP * (BACKGROUND_MIX + CONVECTIVE_MIX)
    for r in range(0, rows, span):
        out = slice(r, r + span)
        here, below = slice(SUB + r, SUB + r + span), slice(SUB + r - 1, SUB + r + span - 1)

        def star(k):
            fx = xt[k, :, out, :]
            t = tm[k, :, here, :] - (fx - west_in(fx, long)) - (yt[k, :, here, :] - yt[k, :, below, :])
            fx = xs[k, :, out, :]
            s = sm[k, :, here, :] - (fx - west_in(fx, long)) - (ys[k, :, here, :] - ys[k, :, below, :])
            t = mended(t, pltpu.roll(mend[out, :], LANES - 2 - 8 * k, 1))
            s = mended(s, pltpu.roll(mend[out, :], LANES - 6 - 8 * k, 1))
            return t, s, HALINE_COEF * s - THERMAL_COEF * t

        def forward(k, carry):
            t, s, dens, lower, qt, qs = carry
            tn, sn, densn = star(k)
            rise = jnp.maximum(densn - dens, 0.0)
            e = 1.0 + STABILITY_FACTOR * rise
            n = jnp.where(de[0:nt, here, :] > k.astype(F32), BASE + DIFF * rise, 0.0)
            w = 1.0 / (e * lower + n)
            rat = n * w
            ew = e * w
            gt, gs = t + qt, s + qs
            t_out[k - 1, :, out, :] = gt * ew
            s_out[k - 1, :, out, :] = gs * ew
            ratio[k - 1, :, out, :] = rat
            return tn, sn, densn, 1.0 + rat * lower, rat * gt, rat * gs

        zero = jnp.zeros((nt, span, LANES), F32)
        carry = star(0) + (zero + 1.0, zero, zero)
        t, s, _, lower, qt, qs = step_loop(1, levels, 2, forward, carry)
        w = 1.0 / lower
        t, s = (t + qt) * w, (s + qs) * w
        t_out[levels - 1, :, out, :] = t
        s_out[levels - 1, :, out, :] = s

        def backward(i, carry):
            t, s = carry
            k = levels - 2 - i
            rat = ratio[k, :, out, :]
            t = t_out[k, :, out, :] + rat * t
            s = s_out[k, :, out, :] + rat * s
            t_out[k, :, out, :] = t
            s_out[k, :, out, :] = s
            return t, s

        step_loop(0, levels - 1, 1, backward, (t, s))

    count = rows + 2 * NSUB
    wide = slice(SUB - NSUB, end + NSUB)
    half = (lane_of((count, LANES)) & 7) >= 4

    def finish(fields, fe, fw):
        halo = jnp.where(half, fe[wide, :], fw[wide, :])
        for n, f in enumerate(fields):
            flat_out[f, nt, 0:count] = pltpu.roll(halo, LANES - 8 * n - 4, 1)
            flat_out[f, 0:nt, 0:NSUB, :] = flat[f, :, SUB - NSUB:SUB, :]
            flat_out[f, 0:nt, rows + NSUB:count, :] = flat[f, :, end:end + NSUB, :]

    for f in range(FLAT):
        flat_out[f, 0:nt, pl.ds(NSUB, rows), :] = flat[f, :, own, :]
    flat_out[DEEP, :, count:, :] = jnp.zeros((nt + 1, SUB, LANES), F32)
    for c in along3:
        c.wait_recv()
    recv_ns(up3, down3)
    finish(range(SOON), fe3, fw3)
    for c in along0 + along_a + along_b + along_c + along2 + along3:
        c.wait_send()
    sent_ns(depth_up + corner_up0 + flow_up + tracer_up + corner_up_b + up2 + up3,
            depth_down + corner_down0 + flow_down + tracer_down + corner_down_b + press_down + down2 + down3)
    for c in along2:
        c.wait_recv()
    recv_ns(up2, down2)
    finish((PUSH_U, PUSH_V), fe2, fw2)


def tail(
    t, s, ut, vt, flat,
    t_out, s_out, u_out, v_out, eta_out, tx_out, ty_out,
    eta, bu, bv, hx, hy, un, vn, cor, sem,
):
    levels, nt, rows, _ = t.shape
    count = rows + 2 * NSUB
    lane = lane_of((SUB, LANES))
    copies = []

    def put(src, dst):
        for c in range(nt):
            copies.append(pltpu.make_async_copy(
                src(c), dst(pl.ds(c * LANES, LANES)), sem.at[len(copies)]))
            copies[-1].start()

    put(lambda c: t.at[:, c], lambda d: t_out.at[:, :, d])
    put(lambda c: s.at[:, c], lambda d: s_out.at[:, :, d])

    for ref in (eta, bu, bv):
        ref[:, 0:SUB, :] = jnp.zeros((nt + 1, SUB, LANES), F32)
        ref[:, count + SUB:, :] = jnp.zeros((nt + 1, SUB, LANES), F32)
    tiles = range(0, count, SUB)
    eta[:, SUB:count + SUB, :] = flat[ETA, :, 0:count, :]
    bu[:, SUB:count + SUB, :] = flat[SUM_U, :, 0:count, :]
    bv[:, SUB:count + SUB, :] = flat[SUM_V, :, 0:count, :]
    for r in tiles:
        d = flat[DEEP, :, r:r + SUB, :]
        hx[:, r:r + SUB, :] = jnp.minimum(d, east_all(d, lane))
        hy[:, r:r + SUB, :] = jnp.minimum(d, flat[DEEP, :, r + 1:r + SUB + 1, :])
    for sub in range(NSUB):
        for r in tiles:
            here, below = slice(SUB + r, 2 * SUB + r), slice(SUB + r - 1, 2 * SUB + r - 1)
            x = bu[:, here, :]
            eta[:, here, :] = eta[:, here, :] - HEIGHT_FACTOR * (
                x - west_all(x, lane) + (bv[:, here, :] - bv[:, below, :]))
        for r in tiles:
            here, above = slice(SUB + r, 2 * SUB + r), slice(SUB + r + 1, 2 * SUB + r + 1)
            raw = slice(r, r + SUB)
            x = eta[:, here, :]
            bu[:, here, :] = (bu[:, here, :] + (1.0 / NSUB) * flat[PUSH_U, :, raw, :]
                              - SLOPE_FACTOR * hx[:, raw, :] * (east_all(x, lane) - x))
            bv[:, here, :] = (bv[:, here, :] + (1.0 / NSUB) * flat[PUSH_V, :, raw, :]
                              - SLOPE_FACTOR * hy[:, raw, :] * (eta[:, above, :] - x))
    mid = pl.ds(SUB + NSUB, rows)
    put(lambda c: eta.at[c, mid, :], lambda d: eta_out.at[:, d])
    put(lambda c: bu.at[c, mid, :], lambda d: tx_out.at[:, d])
    put(lambda c: bv.at[c, mid, :], lambda d: ty_out.at[:, d])

    for r in range(0, rows, SUB):
        raw = slice(NSUB + r, NSUB + r + SUB)
        hu, hv = hx[0:nt, raw, :], hy[0:nt, raw, :]
        done = slice(SUB + NSUB + r, 2 * SUB + NSUB + r)
        out = slice(r, r + SUB)
        cor[0, :, out, :] = (bu[0:nt, done, :] - (flat[PUSH_U, 0:nt, raw, :] + flat[SUM_U, 0:nt, raw, :])) / jnp.maximum(hu, 1.0)
        cor[1, :, out, :] = (bv[0:nt, done, :] - (flat[PUSH_V, 0:nt, raw, :] + flat[SUM_V, 0:nt, raw, :])) / jnp.maximum(hv, 1.0)
        cor[2, :, out, :] = hu
        cor[3, :, out, :] = hv

    part = -(-levels // CHUNKS)
    for first in range(0, levels, part):
        last = min(first + part, levels)

        @pl.loop(first, last)
        def _(k):
            kf = k.astype(F32)
            un[k] = jnp.where(cor[2] > kf, ut[k, :, 0:rows, :] + cor[0], 0.0)
            vn[k] = jnp.where(cor[3] > kf, vt[k, :, 0:rows, :] + cor[1], 0.0)

        span = pl.ds(first, last - first)
        put(lambda c: un.at[span, c], lambda d: u_out.at[span, :, d])
        put(lambda c: vn.at[span, c], lambda d: v_out.at[span, :, d])
    for c in copies:
        c.wait()


def body(*args):
    levels, rows, cols = args[0].shape
    nt = cols // LANES
    erows = rows + 2 * SUB
    count = rows + 2 * NSUB

    def vmem(*shape):
        return pltpu.VMEM(shape, F32)

    def out(*shape):
        return jax.ShapeDtypeStruct(shape, F32)

    block = pl.BlockSpec(memory_space=pltpu.VMEM)
    far = pl.BlockSpec(memory_space=pltpu.HBM)
    raw = vmem(levels, nt, erows, LANES)
    own = vmem(levels, nt, rows, LANES)
    ints = pltpu.VMEM((nt, rows, LANES), jnp.int32)
    n1, n2 = 2 + 8 + 1 + 6 + 4 + 3, 2 * (2 + 6)
    cube = (levels, nt, rows, LANES)
    parts = pl.pallas_call(
        functools.partial(kernel, rows * lax.axis_size("lat")),
        out_shape=(out(*cube),) * 2 + (out(levels, nt, rows + SUB, LANES),) * 2 + (out(FLAT, nt + 1, count + SUB, LANES),),
        in_specs=[far] * 9,
        out_specs=(block,) * 5,
        scratch_shapes=(
            [raw] * 11 + [own] * 3 + [vmem(nt, rows, LANES)] * 2
            + [vmem(nt, rows + SUB, LANES), own, own, raw, raw, own]
            + [vmem(nt, rows, LANES)] * 2 + [ints] * 2
            + [vmem(nt + 1, erows + SUB, LANES)] + [vmem(nt + 1, erows, LANES)] * 2
            + [vmem(FLAT, nt, erows, LANES)]
            + [vmem(rows // SUB, SUB, LANES)] * 2
            + [vmem(rows, LANES), vmem(erows, LANES), vmem(erows, LANES)]
            + [vmem(rows, LANES)] * 3
            + [vmem(rows, LANES), vmem(erows, LANES), vmem(erows, LANES)]
            + [vmem(rows, LANES)] * 2
            + [vmem(rows, LANES), vmem(erows, LANES), vmem(erows, LANES)] * 2
            + [vmem(rows, LANES)]
            + [vmem(erows, LANES), vmem(4, nt, rows, LANES), vmem(levels, nt, SUB, LANES),
               vmem(levels, 4, nt, SUB, LANES)]
            + [pltpu.SemaphoreType.DMA((9 * nt,))]
            + [pltpu.SemaphoreType.DMA((n1,))] * 2
            + [pltpu.SemaphoreType.DMA((n2,))] * 2
        ),
        compiler_params=pltpu.CompilerParams(
            collective_id=0, has_side_effects=True, vmem_limit_bytes=32 * 1024 * 1024),
    )(*[pltpu.with_memory_space_constraint(a, pltpu.HBM) for a in args])
    cube, plane = (levels, rows, cols), (rows, cols)
    return pl.pallas_call(
        tail,
        out_shape=(pltpu.HBM(cube, F32),) * 4 + (pltpu.HBM(plane, F32),) * 3,
        in_specs=[block] * 5,
        out_specs=(far,) * 7,
        scratch_shapes=(
            [vmem(nt + 1, count + 2 * SUB, LANES)] * 3 + [vmem(nt + 1, count, LANES)] * 2
            + [own, own, vmem(4, nt, rows, LANES)]
            + [pltpu.SemaphoreType.DMA(((5 + 2 * CHUNKS) * nt,))]
        ),
        compiler_params=pltpu.CompilerParams(vmem_limit_bytes=32 * 1024 * 1024),
    )(*parts)


def solution(mesh):
    cube, plane = P(None, "lat", "lon"), P("lat", "lon")
    return jax.shard_map(
        body,
        mesh=mesh,
        in_specs=(cube,) * 4 + (plane,) * 5,
        out_specs=(cube,) * 4 + (plane,) * 3,
        check_vma=False,
    )
```
